128 devices in a mesh: gx: 32 (over y, z, core), gy: 4 (over x).
Axes of the slice: x: 4, y: 4, z: 4, core: 2. Of those that a mesh axis runs over, the one named last changes fastest.
Arguments:
- initial_heat_state: float32 [1, 2048, 8192], P(None, 'gx', 'gy'), may hold values from -6 to 6
- thermal_coefficient: float32 [1, 2048, 8192], P(None, 'gx', 'gy'), may hold values from 0.5 to 4
Outputs:
- updated: float32 [1, 2048, 8192], P(None, 'gx', 'gy')
The draws below stay inside these ranges and needn't reach their ends.
All inputs are finite; a program needn't handle non-finite values.
Results may differ from the reference program's by a relative error of at most 0.0025.
Values sent between devices are 32-bit elements; how exact they have to be, the bound alone decides.
No kernel may reach another device: no remote copies, remote signals or barrier semaphores. Data moves between devices by JAX's collectives and lax.ppermute only.
A program may use at most 128 MiB of HBM per device.

```python
import math
import jax
import jax.numpy as jnp
from jax import lax

SHEET_NUMBER = 1
GRID_WIDTH_EAST = 2048
GRID_HEIGHT_NORTH = 8192


def level_of(key, extent, pieces, least, largest):
    level = 1.0
    for axis_at, blocks in pieces:
        steps = jax.random.uniform(jax.random.fold_in(jax.random.fold_in(key, 6), axis_at), (blocks,), jnp.float32, least / len(pieces), largest / len(pieces))
        level = level * jnp.repeat(jnp.exp(steps), extent[axis_at] // blocks).reshape((-1,) + (1,) * (len(extent) - 1 - axis_at))
    return level


def centred(rng, shape, scale, reach, shards=(), kind=jnp.bfloat16):
    level = level_of(rng, shape, shards, -0.22, 0.18) if shards else 1.0
    drawn = jax.random.normal(rng, shape, jnp.float32) * scale * level
    return jnp.minimum(jnp.maximum(drawn, -reach), reach).astype(kind)


def setup_inputs(seed: int = 0) -> dict:
    streams_of = jax.random.split(jax.random.key(seed), 3)
    return {
        "initial_heat_state": centred(streams_of[0], (SHEET_NUMBER, GRID_WIDTH_EAST, GRID_HEIGHT_NORTH), 1.0, 6.0, ((1, 32), (2, 4)), jnp.float32),
        "thermal_coefficient": jnp.clip(jnp.exp(math.log(4.0) - 2.0794415 * jax.random.uniform(streams_of[1], (SHEET_NUMBER, GRID_WIDTH_EAST, GRID_HEIGHT_NORTH), jnp.float32) ** level_of(streams_of[1], (SHEET_NUMBER, GRID_WIDTH_EAST, GRID_HEIGHT_NORTH), ((1, 32), (2, 4)), -0.2, 0.2)), 0.5, 4.0),
    }


def neighbouring_sites(field, along):
    widths = [(0, 0), (0, 0), (0, 0)]
    widths[along] = (1, 1)
    padded = jnp.pad(field, widths)
    length = field.shape[along]
    before = lax.slice_in_dim(padded, 0, length, axis=along)
    after = lax.slice_in_dim(padded, 2, length + 2, axis=along)
    return before, after


def tridiagonal_sweep(lower, middle, upper, source, along):
    moved = tuple(jnp.moveaxis(item, along, 0) for item in (lower, middle, upper, source))
    start = jnp.zeros_like(moved[0][0])

    def forward(carry, rows):
        ratio_prev, value_prev = carry
        lower_row, middle_row, upper_row, source_row = rows
        pivot = middle_row - lower_row * ratio_prev
        ratio = upper_row / pivot
        value = (source_row - lower_row * value_prev) / pivot
        return (ratio, value), (ratio, value)

    _, (ratios, values) = lax.scan(forward, (start, start), moved)

    def backward(later, rows):
        ratio, value = rows
        current = value - ratio * later
        return current, current

    _, result = lax.scan(backward, start, (ratios, values), reverse=True)
    return jnp.moveaxis(result, 0, along)


def reference(initial_heat_state, thermal_coefficient):
    cond_west, cond_east = neighbouring_sites(thermal_coefficient, 1)
    cond_south, cond_north = neighbouring_sites(thermal_coefficient, 2)
    left_interface_mean = (cond_west + thermal_coefficient) * 0.5
    right_interface_mean = (cond_east + thermal_coefficient) * 0.5
    lower_interface_mean = (cond_south + thermal_coefficient) * 0.5
    upper_interface_mean = (cond_north + thermal_coefficient) * 0.5
    left_neighbour_heat, right_neighbour_heat = neighbouring_sites(initial_heat_state, 1)
    lower_neighbour_heat, upper_neighbour_heat = neighbouring_sites(initial_heat_state, 2)
    horizontal_current = right_interface_mean * (right_neighbour_heat - initial_heat_state) - left_interface_mean * (initial_heat_state - left_neighbour_heat)
    vertical_current = upper_interface_mean * (upper_neighbour_heat - initial_heat_state) - lower_interface_mean * (initial_heat_state - lower_neighbour_heat)
    explicit = 4000.0 * horizontal_current + 16000.0 * vertical_current
    initial_entry = tridiagonal_sweep(-2000.0 * left_interface_mean, 1.0 + 2000.0 * (left_interface_mean + right_interface_mean), -2000.0 * right_interface_mean, explicit, 1)
    heat_increment = tridiagonal_sweep(-8000.0 * lower_interface_mean, 1.0 + 8000.0 * (lower_interface_mean + upper_interface_mean), -8000.0 * upper_interface_mean, initial_entry, 2)
    return initial_heat_state + heat_increment
```

```python
import jax
import jax.numpy as jnp
from jax import lax
from jax.experimental import pallas as pl
from jax.experimental.pallas import tpu as pltpu
from jax.sharding import PartitionSpec as P

ROWS, COLS = 64, 2048
BANDS, TILES = ROWS // 8, COLS // 128
SEGMENTS = 4
Y_STEPS = 128
X_LEVELS, Y_LEVELS = 2, 6
F32 = jnp.float32
VMEM = pl.BlockSpec(memory_space=pltpu.VMEM)


def struct(*shape):
    return jax.ShapeDtypeStruct(shape, F32)


def whole(outs, args):
    return dict(in_specs=[VMEM] * len(args), out_specs=jax.tree.map(lambda _: VMEM, outs))


def call(kernel, outs, scratch=(), flops=2_000_000, name=None, **windows):
    def run(*args):
        return pl.pallas_call(
            kernel,
            out_shape=outs,
            **(windows or whole(outs, args)),
            scratch_shapes=list(scratch),
            compiler_params=pltpu.CompilerParams(vmem_limit_bytes=32 << 20),
            cost_estimate=pl.CostEstimate(flops=flops, bytes_accessed=1 << 20, transcendentals=0),
            name=name,
        )(*args)

    return run


def moved(chain, by, shift):
    out = []
    for s in range(SEGMENTS):
        runs, at = divmod(s + by, SEGMENTS)
        out.append(shift(chain[at], runs) if runs else chain[at])
    return out


def factor(link, n, levels, shift, along, back, gain, sep):
    m = n // SEGMENTS
    near = [link(s * m) for s in range(SEGMENTS)]
    ground = [jnp.ones_like(near[0])] * SEGMENTS
    held = [jnp.ones_like(near[0])] * SEGMENTS
    for step in range(1, m):
        for s in range(SEGMENTS):
            l = s * m + step
            v = link(l)
            r = 1.0 / (near[s] + ground[s] + v)
            t = v * r
            c = near[s] * r
            along[l], back[l], gain[l] = t, c, r
            held[s] = held[s] + ground[s] * c
            near[s] = near[s] * t
            ground[s] = ground[s] * t
            if step < m - 1:
                ground[s] = ground[s] + 1.0
    before = moved(ground, -1, shift)
    own = [held[s] + before[s] for s in range(SEGMENTS)]
    up = near
    down = moved(near, -1, shift)
    for level in range(levels):
        stride = 1 << level
        r = [1.0 / (own[s] + up[s] + down[s]) for s in range(SEGMENTS)]
        r_down, r_up = moved(r, -stride, shift), moved(r, stride, shift)
        own_down, own_up = moved(own, -stride, shift), moved(own, stride, shift)
        down_down, up_up = moved(down, -stride, shift), moved(up, stride, shift)
        for s in range(SEGMENTS):
            a, b = down[s] * r_down[s], up[s] * r_up[s]
            sep[(level * 2) * SEGMENTS + s] = a
            sep[(level * 2 + 1) * SEGMENTS + s] = b
            own[s] = own[s] + a * own_down[s] + b * own_up[s]
            down[s], up[s] = a * down_down[s], b * up_up[s]
    for s in range(SEGMENTS):
        sep[levels * 2 * SEGMENTS + s] = 1.0 / own[s]


def plus(a, b):
    return b if a is None else a if b is None else a + b


def times(a, b):
    return None if a is None else a * b


def solve(source, n, levels, shift, along, back, gain, sep, part, store):
    m = n // SEGMENTS
    total = [source(s * m) for s in range(SEGMENTS)]
    z = [source(s * m + 1) for s in range(SEGMENTS)]
    zero = [[False] * SEGMENTS for _ in range(m)]
    for step in range(1, m):
        for s in range(SEGMENTS):
            l = s * m + step
            zero[step][s] = z[s] is None
            if z[s] is not None:
                part[l] = z[s] * gain[l]
                total[s] = plus(total[s], z[s] * back[l])
                z[s] = z[s] * along[l]
            if step < m - 1:
                z[s] = plus(source(l + 1), z[s])
    shape = jnp.zeros(along.shape[1:], F32)
    z = [shape if v is None else v for v in z]
    before = moved(z, -1, shift)
    total = [plus(total[s], before[s]) for s in range(SEGMENTS)]
    for level in range(levels):
        stride = 1 << level
        lo, hi = moved(total, -stride, shift), moved(total, stride, shift)
        total = [
            total[s]
            + sep[(level * 2) * SEGMENTS + s] * lo[s]
            + sep[(level * 2 + 1) * SEGMENTS + s] * hi[s]
            for s in range(SEGMENTS)
        ]
    value = [total[s] * sep[levels * 2 * SEGMENTS + s] for s in range(SEGMENTS)]
    after = moved(value, 1, shift)
    for s in range(SEGMENTS):
        store(s * m, value[s])
    for step in reversed(range(1, m)):
        for s in range(SEGMENTS):
            l = s * m + step
            known = back[l] * value[s]
            if not zero[step][s]:
                known = known + part[l]
            after[s] = known + along[l] * after[s]
            store(l, after[s])


def x_shift(value, runs):
    return value


def y_shift(value, runs):
    if runs % 2 == 0:
        return pltpu.roll(value, (-(runs // 2)) % 8, 0)
    swapped = pltpu.roll(value, 64, 1)
    late = lax.broadcasted_iota(jnp.int32, value.shape, 1) >= 64
    if runs == 1:
        return jnp.where(late, pltpu.roll(swapped, 7, 0), swapped)
    return jnp.where(late, swapped, pltpu.roll(swapped, 1, 0))


def tile(ref, band, column):
    return ref[8 * band : 8 * band + 8, 128 * column : 128 * column + 128]


def row(ref, i):
    return ref[pl.ds((i // 8) * (8 * TILES) + i % 8, TILES, stride=8), :]


def edges_kernel(t_lo, k_lo, t_hi, k_hi, lo, hi):
    lo[...] = jnp.zeros_like(lo)
    hi[...] = jnp.zeros_like(hi)
    lo[0:1, 0:ROWS] = t_lo[...].T[0:1, :]
    lo[1:2, 0:ROWS] = k_lo[...].T[0:1, :]
    hi[0:1, 0:ROWS] = t_hi[...].T[127:128, :]
    hi[1:2, 0:ROWS] = k_hi[...].T[127:128, :]


def x_matrix_kernel(t, k, e, along, back, gain, sep, lo, hi, ends, flat):
    lane = lax.broadcasted_iota(jnp.int32, (8, 128), 1)
    for band in range(BANDS):
        ks = [tile(k, band, c) for c in range(TILES)]
        ts = [tile(t, band, c) for c in range(TILES)]
        k_left = [pltpu.roll(v, 127, 1) for v in ks]
        t_left = [pltpu.roll(v, 127, 1) for v in ts]
        flow = []
        for c in range(TILES):
            at = pl.ds((band * TILES + c) * 8, 8)
            flat[at, :] = ks[c]
            n = min(c + 1, TILES - 1)
            k_next = jnp.where(lane == 127, k_left[n], k_left[c])
            t_next = jnp.where(lane == 127, t_left[n], t_left[c])
            f = 8000.0 * (ks[c] + k_next) * (t_next - ts[c])
            if c == TILES - 1:
                f = jnp.where(lane == 127, 0.0, f)
            flow.append(f)
        turned = [pltpu.roll(v, 1, 1) for v in flow]
        for c in range(TILES):
            at = pl.ds((band * TILES + c) * 8, 8)
            first = turned[c - 1] if c else jnp.zeros_like(turned[0])
            f_before = jnp.where(lane == 0, first, turned[c])
            e[at, :] = 2.0 * ts[c] + (flow[c] - f_before)

    def link(l):
        if l == ROWS - 1:
            return jnp.zeros((TILES, 128), F32)
        return 1000.0 * (row(flat, l) + row(flat, l + 1))

    factor(link, ROWS, X_LEVELS, x_shift, along, back, gain, sep)
    one = jnp.ones((TILES, 128), F32)

    def at_start(l):
        return one if l == 0 else None

    def at_end(l):
        return one if l == ROWS - 1 else None

    def to(ref):
        def store(l, value):
            ref[l] = value

        return store

    args = (ROWS, X_LEVELS, x_shift, along, back, gain, sep)
    solve(at_start, *args, lo, to(lo))
    solve(at_end, *args, hi, to(hi))
    ends[0] = lo[0]
    ends[1] = lo[ROWS - 1]
    ends[2] = hi[ROWS - 1]
    ends[3] = row(flat, 0)
    ends[4] = row(flat, ROWS - 1)


def x_source_kernel(
    e, along, back, gain, sep, ends, own_lo, own_hi, below, above, u, port, flat, side
):
    side[...] = jnp.zeros_like(side)
    t_lo, k_lo = own_lo[0:1, :], own_lo[1:2, :]
    t_hi, k_hi = own_hi[0:1, :], own_hi[1:2, :]
    side[0:1, :] = -8000.0 * (k_lo + below[1:2, :]) * (t_lo - below[0:1, :])
    side[127:128, :] = 8000.0 * (k_hi + above[1:2, :]) * (above[0:1, :] - t_hi)
    edge = side[...].T
    lane = lax.broadcasted_iota(jnp.int32, (8, 128), 1)
    flat[...] = e[...]
    for band in range(BANDS):
        part = edge[8 * band : 8 * band + 8, :]
        at = pl.ds(band * TILES * 8, 8)
        flat[at, :] = flat[at, :] + jnp.where(lane == 0, part, 0.0)
        at = pl.ds((band * TILES + TILES - 1) * 8, 8)
        flat[at, :] = flat[at, :] + jnp.where(lane == 127, part, 0.0)

    def store(l, value):
        u[l] = value

    def source(l):
        return row(flat, l)

    solve(source, ROWS, X_LEVELS, x_shift, along, back, gain, sep, u, store)
    port[0] = u[0]
    port[1] = u[ROWS - 1]
    for n in range(5):
        port[2 + n] = ends[n]


def take(ref):
    return tuple(ref[n] for n in range(7))


def join(one, two, scale):
    a1, b1, al1, be1, ga1, kf1, kl1 = one
    a2, b2, al2, be2, ga2, kf2, kl2 = two
    rho = 1.0 / (1.0 / (scale * (kl1 + kf2)) + al2 + ga1)
    delta = (a2 - b1) * rho
    return (
        a1 + be1 * delta,
        b2 - be2 * delta,
        al1 - be1 * be1 * rho,
        be1 * be2 * rho,
        ga2 - be2 * be2 * rho,
        kf1,
        kl2,
    )


def past_up(state, port, scale):
    p, q, k = state
    a, b, al, be, ga, kf, kl = port
    w = be / (1.0 / (scale * (k + kf)) + al + q)
    return (b - w * (a - p), ga - w * be, kl)


def past_down(state, port, scale):
    p, q, k = state
    a, b, al, be, ga, kf, kl = port
    w = be / (1.0 / (scale * (k + kl)) + ga + q)
    return (a + w * (p - b), al - w * be, kf)


def choose(condition, new, old):
    return tuple(jnp.where(condition, x, y) for x, y in zip(new, old))


def reach(index, ports, lo, hi, scale):
    count = len(ports)
    for n in range(count - 1):
        lo = choose(n < index, past_up(lo, ports[n], scale), lo)
    for n in reversed(range(1, count)):
        hi = choose(n > index, past_down(hi, ports[n], scale), hi)
    return lo, hi


def flows(port, lo, hi, scale):
    a, b, al, be, ga, kf, kl = port
    d_lo = 1.0 / (scale * (lo[2] + kf)) + al + lo[1]
    d_hi = 1.0 / (scale * (hi[2] + kl)) + ga + hi[1]
    c_lo, c_hi = a - lo[0], hi[0] - b
    inverse = 1.0 / (d_lo * d_hi - be * be)
    return (d_hi * c_lo + be * c_hi) * inverse, (d_lo * c_hi + be * c_lo) * inverse


def place(index, own, received, table):
    table[index] = own[...]
    for s in (1, 2, 3):
        table[lax.rem(index + 4 - s, 4)] = received[s - 1][...]


def pair_kernel(own, other, out):
    core = lax.rem(lax.axis_index("gx"), 2)
    mine, theirs = take(own), take(other)
    first = choose(core == 0, mine, theirs)
    second = choose(core == 0, theirs, mine)
    for n, value in enumerate(join(first, second, 1000.0)):
        out[n] = value


def four_kernel(own, r1, r2, r3, out, table):
    z = lax.rem(lax.div(lax.axis_index("gx"), 2), 4)
    place(z, own, (r1, r2, r3), table)
    ports = [take(table.at[j]) for j in range(4)]
    joined = join(join(ports[0], ports[1], 1000.0), join(ports[2], ports[3], 1000.0), 1000.0)
    for n, value in enumerate(joined):
        out[n] = value


def to_runs(blocks, out):
    for p in range(TILES // 2):
        stack = [blocks(band, 2 * p + half) for half in range(2) for band in range(BANDS)]
        out[128 * p : 128 * p + 128, :] = jnp.concatenate(stack, axis=0).T


def cell(ref, l):
    return ref[pl.ds(l, 8, stride=128), :]


def y_matrix_kernel(k, along, back, gain, sep, lo, hi, ends, turned):
    to_runs(lambda band, column: tile(k, band, column), turned)
    lane = lax.broadcasted_iota(jnp.int32, (8, 128), 1)
    sublane = lax.broadcasted_iota(jnp.int32, (8, 128), 0)
    very_last = (lane >= 64) & (sublane == 7)
    very_first = (lane < 64) & (sublane == 0)

    def link(l):
        if l == Y_STEPS - 1:
            both = 4000.0 * (cell(turned, l) + y_shift(cell(turned, 0), 1))
            return jnp.where(very_last, 0.0, both)
        return 4000.0 * (cell(turned, l) + cell(turned, l + 1))

    factor(link, Y_STEPS, Y_LEVELS, y_shift, along, back, gain, sep)

    def at_start(l):
        return jnp.where(very_first, 1.0, 0.0) if l == 0 else None

    def at_end(l):
        return jnp.where(very_last, 1.0, 0.0) if l == Y_STEPS - 1 else None

    def to(ref):
        def store(l, value):
            ref[l] = value

        return store

    args = (Y_STEPS, Y_LEVELS, y_shift, along, back, gain, sep)
    solve(at_start, *args, lo, to(lo))
    solve(at_end, *args, hi, to(hi))
    last = Y_STEPS - 1
    ends[...] = jnp.zeros_like(ends)
    ends[0:1, :] = lo[0, 0:1, :]
    ends[1:2, :] = pltpu.roll(lo[last], 64, 1)[7:8, :]
    ends[2:3, :] = pltpu.roll(hi[last], 64, 1)[7:8, :]
    ends[3:4, :] = cell(turned, 0)[0:1, :]
    ends[4:5, :] = pltpu.roll(cell(turned, last), 64, 1)[7:8, :]


def y_source_kernel(
    own_y, y1, y2, y3, own_z, z1, z2, z3, own, other, u, x_lo, x_hi, t,
    along, back, gain, sep, ends, d, port, table_y, table_z, flat, turned,
):
    index = lax.axis_index("gx")
    core, z, y = lax.rem(index, 2), lax.rem(lax.div(index, 2), 4), lax.div(index, 8)
    place(y, own_y, (y1, y2, y3), table_y)
    place(z, own_z, (z1, z2, z3), table_z)
    nothing = (jnp.zeros((TILES, 128), F32),) * 3
    scale = 1000.0
    lo, hi = reach(y, [take(table_y.at[j]) for j in range(4)], nothing, nothing, scale)
    lo, hi = reach(z, [take(table_z.at[j]) for j in range(4)], lo, hi, scale)
    mine, theirs = take(own), take(other)
    lo = choose(core == 1, past_up(lo, theirs, scale), lo)
    hi = choose(core == 0, past_down(hi, theirs, scale), hi)
    f_lo, f_hi = flows(mine, lo, hi, scale)
    for i in range(ROWS):
        at = pl.ds((i // 8) * (8 * TILES) + i % 8, TILES, stride=8)
        flat[at, :] = u[i] - f_lo * x_lo[i] + f_hi * x_hi[i]

    def block(band, column):
        at = (band * TILES + column) * 8
        return flat[at : at + 8, :] - 2.0 * tile(t, band, column)

    to_runs(block, turned)

    def store(l, value):
        d[l] = value

    def source(l):
        return cell(turned, l)

    solve(source, Y_STEPS, Y_LEVELS, y_shift, along, back, gain, sep, d, store)
    port[...] = jnp.zeros_like(port)
    port[0:1, :] = d[0, 0:1, :]
    port[1:2, :] = pltpu.roll(d[Y_STEPS - 1], 64, 1)[7:8, :]
    port[2:7, :] = ends[0:5, :]


def finish_kernel(own, r1, r2, r3, d, y_lo, y_hi, t, out, table, turned):
    index = lax.axis_index("gy")
    place(index, own, (r1, r2, r3), table)
    lane = lax.broadcasted_iota(jnp.int32, (1, 128), 1)

    def port_of(ref):
        return tuple(jnp.where(lane < ROWS, ref[n : n + 1, :], 1.0) for n in range(7))

    nothing = (jnp.zeros((1, 128), F32),) * 3
    scale = 4000.0
    lo, hi = reach(index, [port_of(table.at[j]) for j in range(4)], nothing, nothing, scale)
    f_lo, f_hi = flows(port_of(own), lo, hi, scale)

    def doubled(f):
        f = jnp.broadcast_to(jnp.where(lane < ROWS, f, 0.0), (8, 128))
        return f + pltpu.roll(f, 64, 1)

    f_lo, f_hi = doubled(f_lo), doubled(f_hi)
    for l in range(Y_STEPS):
        turned[pl.ds(l, 8, stride=128), :] = d[l] - f_lo * y_lo[l] + f_hi * y_hi[l]
    for p in range(TILES // 2):
        block = turned[128 * p : 128 * p + 128, :].T
        for half in range(2):
            column = 2 * p + half
            for band in range(BANDS):
                at = 64 * half + 8 * band
                out[8 * band : 8 * band + 8, 128 * column : 128 * column + 128] = (
                    tile(t, band, column) + block[at : at + 8, :]
                )


def around(value, axis, size, stride, step):
    pairs = []
    for i in range(size):
        digit = (i // stride) % 4
        pairs.append((i, i + ((digit + step) % 4 - digit) * stride))
    return lax.ppermute(value, axis, pairs)


def per_device(initial_heat_state, thermal_coefficient):
    t, k = initial_heat_state[0], thermal_coefficient[0]
    first = pl.BlockSpec((ROWS, 128), lambda n: (0, 0))
    last = pl.BlockSpec((ROWS, 128), lambda n: (0, TILES - 1))
    own_lo, own_hi = call(
        edges_kernel,
        [struct(8, 128)] * 2,
        name="edges",
        grid=(1,),
        in_specs=[first, first, last, last],
        out_specs=[pl.BlockSpec((8, 128), lambda n: (0, 0))] * 2,
    )(t, k, t, k)
    below = lax.ppermute(own_hi, "gy", [(i, i + 1) for i in range(3)])
    above = lax.ppermute(own_lo, "gy", [(i + 1, i) for i in range(3)])
    flat = pltpu.VMEM((BANDS * TILES * 8, 128), F32)
    runs = pltpu.VMEM((TILES // 2 * 128, 128), F32)
    x_field, y_field = struct(ROWS, TILES, 128), struct(Y_STEPS, 8, 128)
    e, *x_coefficients, x_lo, x_hi, x_ends = call(
        x_matrix_kernel,
        [
            struct(BANDS * TILES * 8, 128),
            x_field,
            x_field,
            x_field,
            struct((2 * X_LEVELS + 1) * SEGMENTS, TILES, 128),
            x_field,
            x_field,
            struct(5, TILES, 128),
        ],
        [flat],
        name="x_matrix",
    )(t, k)
    x_port = struct(7, TILES, 128)
    u, own = call(
        x_source_kernel,
        [x_field, x_port],
        [flat, pltpu.VMEM((128, 128), F32)],
        name="x_source",
    )(e, *x_coefficients, x_ends, own_lo, own_hi, below, above)
    other = lax.ppermute(own, "gx", [(i, i ^ 1) for i in range(32)])
    own_z = call(pair_kernel, x_port, name="pair")(own, other)
    k_y, own_z = lax.optimization_barrier((k, own_z))
    from_z = [around(own_z, "gx", 32, 2, s) for s in (1, 2, 3)]
    *y_coefficients, y_lo, y_hi, y_ends = call(
        y_matrix_kernel,
        [
            y_field,
            y_field,
            y_field,
            struct((2 * Y_LEVELS + 1) * SEGMENTS, 8, 128),
            y_field,
            y_field,
            struct(8, 128),
        ],
        [runs],
        name="y_matrix",
    )(k_y)
    table = pltpu.VMEM((4, 7, TILES, 128), F32)
    own_y = call(four_kernel, x_port, [table], name="four")(own_z, *from_z)
    from_y = [around(own_y, "gx", 32, 8, s) for s in (1, 2, 3)]
    d, port = call(
        y_source_kernel,
        [y_field, struct(8, 128)],
        [table, table, flat, runs],
        name="y_source",
    )(own_y, *from_y, own_z, *from_z, own, other, u, x_lo, x_hi, t, *y_coefficients, y_ends)
    from_gy = [around(port, "gy", 4, 1, s) for s in (1, 2, 3)]
    updated = call(
        finish_kernel,
        struct(ROWS, COLS),
        [pltpu.VMEM((4, 8, 128), F32), runs],
        name="finish",
    )(port, *from_gy, d, y_lo, y_hi, t)
    return updated[None]


def solution(mesh):
    placed = (P(None, "gx", "gy"), P(None, "gx", "gy"))
    return jax.shard_map(
        per_device, mesh=mesh, in_specs=placed, out_specs=P(None, "gx", "gy"), check_vma=False
    )
```

```python
import jax
import jax.numpy as jnp
from jax import lax
from jax.experimental import pallas as pl
from jax.experimental.pallas import tpu as pltpu
from jax.sharding import PartitionSpec as P

ROWS, COLS = 64, 2048
BANDS, TILES = ROWS // 8, COLS // 128
SEGMENTS = 4
Y_STEPS = 128
X_LEVELS, Y_LEVELS = 2, 6
F32 = jnp.float32
VMEM = pl.BlockSpec(memory_space=pltpu.VMEM)
HBM = pl.BlockSpec(memory_space=pltpu.MemorySpace.HBM)


def struct(*shape):
    return jax.ShapeDtypeStruct(shape, F32)


def scratch(like):
    return pltpu.VMEM(like.shape, like.dtype)


def whole(outs, args):
    return dict(in_specs=[VMEM] * len(args), out_specs=jax.tree.map(lambda _: VMEM, outs))


def call(kernel, outs, buffers=(), flops=2_000_000, name=None, grant=32 << 20, **windows):
    def run(*args):
        return pl.pallas_call(
            kernel,
            out_shape=outs,
            **(windows or whole(outs, args)),
            scratch_shapes=list(buffers),
            compiler_params=pltpu.CompilerParams(vmem_limit_bytes=grant),
            cost_estimate=pl.CostEstimate(flops=flops, bytes_accessed=1 << 20, transcendentals=0),
            name=name,
        )(*args)

    return run


def moved(chain, by, shift):
    out = []
    for s in range(SEGMENTS):
        runs, at = divmod(s + by, SEGMENTS)
        out.append(shift(chain[at], runs) if runs else chain[at])
    return out


def factor(link, n, levels, shift, along, back, gain, sep):
    m = n // SEGMENTS
    near = [link(s * m) for s in range(SEGMENTS)]
    ground = [jnp.ones_like(near[0])] * SEGMENTS
    held = [jnp.ones_like(near[0])] * SEGMENTS
    for step in range(1, m):
        for s in range(SEGMENTS):
            l = s * m + step
            v = link(l)
            r = 1.0 / (near[s] + ground[s] + v)
            t = v * r
            c = near[s] * r
            along[l], back[l], gain[l] = t, c, r
            held[s] = held[s] + ground[s] * c
            near[s] = near[s] * t
            ground[s] = ground[s] * t
            if step < m - 1:
                ground[s] = ground[s] + 1.0
    before = moved(ground, -1, shift)
    own = [held[s] + before[s] for s in range(SEGMENTS)]
    up = near
    down = moved(near, -1, shift)
    for level in range(levels):
        stride = 1 << level
        r = [1.0 / (own[s] + up[s] + down[s]) for s in range(SEGMENTS)]
        r_down, r_up = moved(r, -stride, shift), moved(r, stride, shift)
        own_down, own_up = moved(own, -stride, shift), moved(own, stride, shift)
        down_down, up_up = moved(down, -stride, shift), moved(up, stride, shift)
        for s in range(SEGMENTS):
            a, b = down[s] * r_down[s], up[s] * r_up[s]
            sep[(level * 2) * SEGMENTS + s] = a
            sep[(level * 2 + 1) * SEGMENTS + s] = b
            own[s] = own[s] + a * own_down[s] + b * own_up[s]
            down[s], up[s] = a * down_down[s], b * up_up[s]
    for s in range(SEGMENTS):
        sep[levels * 2 * SEGMENTS + s] = 1.0 / own[s]


def plus(a, b):
    return b if a is None else a if b is None else a + b


def times(a, b):
    return None if a is None else a * b


def solve(source, n, levels, shift, along, back, gain, sep, part, store):
    m = n // SEGMENTS
    total = [source(s * m) for s in range(SEGMENTS)]
    z = [source(s * m + 1) for s in range(SEGMENTS)]
    zero = [[False] * SEGMENTS for _ in range(m)]
    for step in range(1, m):
        for s in range(SEGMENTS):
            l = s * m + step
            zero[step][s] = z[s] is None
            if z[s] is not None:
                part[l] = z[s] * gain[l]
                total[s] = plus(total[s], z[s] * back[l])
                z[s] = z[s] * along[l]
            if step < m - 1:
                z[s] = plus(source(l + 1), z[s])
    shape = jnp.zeros(along.shape[1:], F32)
    z = [shape if v is None else v for v in z]
    before = moved(z, -1, shift)
    total = [plus(total[s], before[s]) for s in range(SEGMENTS)]
    for level in range(levels):
        stride = 1 << level
        lo, hi = moved(total, -stride, shift), moved(total, stride, shift)
        total = [
            total[s]
            + sep[(level * 2) * SEGMENTS + s] * lo[s]
            + sep[(level * 2 + 1) * SEGMENTS + s] * hi[s]
            for s in range(SEGMENTS)
        ]
    value = [total[s] * sep[levels * 2 * SEGMENTS + s] for s in range(SEGMENTS)]
    after = moved(value, 1, shift)
    for s in range(SEGMENTS):
        store(s * m, value[s])
    for step in reversed(range(1, m)):
        for s in range(SEGMENTS):
            l = s * m + step
            known = back[l] * value[s]
            if not zero[step][s]:
                known = known + part[l]
            after[s] = known + along[l] * after[s]
            store(l, after[s])


def x_shift(value, runs):
    return value


def y_shift(value, runs):
    if runs % 2 == 0:
        return pltpu.roll(value, (-(runs // 2)) % 8, 0)
    swapped = pltpu.roll(value, 64, 1)
    late = lax.broadcasted_iota(jnp.int32, value.shape, 1) >= 64
    if runs == 1:
        return jnp.where(late, pltpu.roll(swapped, 7, 0), swapped)
    return jnp.where(late, swapped, pltpu.roll(swapped, 1, 0))


def tile(ref, band, column):
    return ref[8 * band : 8 * band + 8, 128 * column : 128 * column + 128]


def flat_tile(ref, band, column):
    at = (band * TILES + column) * 8
    return ref[at : at + 8, :]


def row(ref, i):
    return ref[pl.ds((i // 8) * (8 * TILES) + i % 8, TILES, stride=8), :]


def edges_kernel(t, k, lo, hi, strips, arrived):
    sides = (pl.ds(0, 128), pl.ds(128 * (TILES - 1), 128))
    copies = [
        pltpu.make_async_copy(ref.at[:, side], strips.at[n], arrived.at[n])
        for n, (side, ref) in enumerate((side, ref) for side in sides for ref in (t, k))
    ]
    for copy in copies:
        copy.start()
    lo[...] = jnp.zeros_like(lo)
    hi[...] = jnp.zeros_like(hi)
    for copy in copies:
        copy.wait()
    lo[0:1, 0:ROWS] = strips[0].T[0:1, :]
    lo[1:2, 0:ROWS] = strips[1].T[0:1, :]
    hi[0:1, 0:ROWS] = strips[2].T[127:128, :]
    hi[1:2, 0:ROWS] = strips[3].T[127:128, :]


def total(terms):
    sums = [None] * 4
    for n, term in enumerate(terms):
        sums[n % 4] = plus(sums[n % 4], term)
    return (sums[0] + sums[1]) + (sums[2] + sums[3])


def x_matrix_kernel(
    t_far, k_far, e, along, back, gain, sep, lo, hi, ends, t_flat, flat, t, k, arrived
):
    copies = []
    for band in range(BANDS):
        at = pl.ds(8 * band, 8)
        copies.append(
            [
                pltpu.make_async_copy(far.at[at, :], near.at[at, :], arrived.at[n, band])
                for n, (far, near) in enumerate(((t_far, t), (k_far, k)))
            ]
        )
        for copy in copies[-1]:
            copy.start()
    lane = lax.broadcasted_iota(jnp.int32, (8, 128), 1)
    for band in range(BANDS):
        for copy in copies[band]:
            copy.wait()
        ks = [tile(k, band, c) for c in range(TILES)]
        ts = [tile(t, band, c) for c in range(TILES)]
        k_left = [pltpu.roll(v, 127, 1) for v in ks]
        t_left = [pltpu.roll(v, 127, 1) for v in ts]
        flow = []
        for c in range(TILES):
            at = pl.ds((band * TILES + c) * 8, 8)
            flat[at, :] = ks[c]
            t_flat[at, :] = ts[c]
            n = min(c + 1, TILES - 1)
            k_next = jnp.where(lane == 127, k_left[n], k_left[c])
            t_next = jnp.where(lane == 127, t_left[n], t_left[c])
            f = 8000.0 * (ks[c] + k_next) * (t_next - ts[c])
            if c == TILES - 1:
                f = jnp.where(lane == 127, 0.0, f)
            flow.append(f)
        turned = [pltpu.roll(v, 1, 1) for v in flow]
        for c in range(TILES):
            at = pl.ds((band * TILES + c) * 8, 8)
            first = turned[c - 1] if c else jnp.zeros_like(turned[0])
            f_before = jnp.where(lane == 0, first, turned[c])
            e[at, :] = 2.0 * ts[c] + (flow[c] - f_before)

    def link(l):
        if l == ROWS - 1:
            return jnp.zeros((TILES, 128), F32)
        return 1000.0 * (row(flat, l) + row(flat, l + 1))

    factor(link, ROWS, X_LEVELS, x_shift, along, back, gain, sep)
    one = jnp.ones((TILES, 128), F32)

    def at_start(l):
        return one if l == 0 else None

    def at_end(l):
        return one if l == ROWS - 1 else None

    def to(ref):
        def store(l, value):
            ref[l] = value

        return store

    args = (ROWS, X_LEVELS, x_shift, along, back, gain, sep)
    solve(at_start, *args, lo, to(lo))
    solve(at_end, *args, hi, to(hi))
    ends[0] = total(lo[i] * row(e, i) for i in range(ROWS))
    ends[1] = total(hi[i] * row(e, i) for i in range(ROWS))
    ends[2] = lo[0]
    ends[3] = lo[ROWS - 1]
    ends[4] = hi[ROWS - 1]
    ends[5] = row(flat, 0)
    ends[6] = row(flat, ROWS - 1)


def x_port_kernel(ends, lo, hi, own_lo, own_hi, below, above, port, edge, side):
    at = lax.axis_index("gy")
    side[...] = jnp.zeros_like(side)
    t_lo, k_lo = own_lo[0:1, :], own_lo[1:2, :]
    t_hi, k_hi = own_hi[0:1, :], own_hi[1:2, :]
    before = jnp.where(at == 0, 0.0, below[...])
    after = jnp.where(at == lax.axis_size("gy") - 1, 0.0, above[...])
    side[0:1, :] = -8000.0 * (k_lo + before[1:2, :]) * (t_lo - before[0:1, :])
    side[127:128, :] = 8000.0 * (k_hi + after[1:2, :]) * (after[0:1, :] - t_hi)
    edge[...] = side[...].T[0:ROWS, :]
    lane = lax.broadcasted_iota(jnp.int32, (1, 128), 1)
    for n, response in enumerate((lo, hi)):
        port[n] = ends[n]
        for column, kept in ((0, 0), (TILES - 1, 127)):
            term = edge[...] * response[:, column, :]
            term = jnp.where(lane == kept, jnp.sum(term, axis=0, keepdims=True), 0.0)
            port[n, column : column + 1, :] = port[n, column : column + 1, :] + term
    for n in range(2, 7):
        port[n] = ends[n]


def x_solve_kernel(e, along, back, gain, sep, edge, u, flat):
    lane = lax.broadcasted_iota(jnp.int32, (8, 128), 1)
    flat[...] = e[...]
    for band in range(BANDS):
        part = edge[8 * band : 8 * band + 8, :]
        at = pl.ds(band * TILES * 8, 8)
        flat[at, :] = flat[at, :] + jnp.where(lane == 0, part, 0.0)
        at = pl.ds((band * TILES + TILES - 1) * 8, 8)
        flat[at, :] = flat[at, :] + jnp.where(lane == 127, part, 0.0)

    def store(l, value):
        u[l] = value

    def source(l):
        return row(flat, l)

    solve(source, ROWS, X_LEVELS, x_shift, along, back, gain, sep, u, store)


def take(ref):
    return tuple(ref[n] for n in range(7))


def join(one, two, scale):
    a1, b1, al1, be1, ga1, kf1, kl1 = one
    a2, b2, al2, be2, ga2, kf2, kl2 = two
    rho = 1.0 / (1.0 / (scale * (kl1 + kf2)) + al2 + ga1)
    delta = (a2 - b1) * rho
    return (
        a1 + be1 * delta,
        b2 - be2 * delta,
        al1 - be1 * be1 * rho,
        be1 * be2 * rho,
        ga2 - be2 * be2 * rho,
        kf1,
        kl2,
    )


def past_up(state, port, scale):
    p, q, k = state
    a, b, al, be, ga, kf, kl = port
    w = be / (1.0 / (scale * (k + kf)) + al + q)
    return (b - w * (a - p), ga - w * be, kl)


def past_down(state, port, scale):
    p, q, k = state
    a, b, al, be, ga, kf, kl = port
    w = be / (1.0 / (scale * (k + kl)) + ga + q)
    return (a + w * (p - b), al - w * be, kf)


def choose(condition, new, old):
    return tuple(jnp.where(condition, x, y) for x, y in zip(new, old))


def reach(index, ports, lo, hi, scale):
    count = len(ports)
    for n in range(count - 1):
        lo = choose(n < index, past_up(lo, ports[n], scale), lo)
    for n in reversed(range(1, count)):
        hi = choose(n > index, past_down(hi, ports[n], scale), hi)
    return lo, hi


def flows(port, lo, hi, scale):
    a, b, al, be, ga, kf, kl = port
    d_lo = 1.0 / (scale * (lo[2] + kf)) + al + lo[1]
    d_hi = 1.0 / (scale * (hi[2] + kl)) + ga + hi[1]
    c_lo, c_hi = a - lo[0], hi[0] - b
    inverse = 1.0 / (d_lo * d_hi - be * be)
    return (d_hi * c_lo + be * c_hi) * inverse, (d_lo * c_hi + be * c_lo) * inverse


def place(index, own, received, table):
    table[index] = own[...]
    for s in (1, 2, 3):
        table[lax.rem(index + 4 - s, 4)] = received[s - 1][...]


def pair_kernel(own, other, out):
    core = lax.rem(lax.axis_index("gx"), 2)
    mine, theirs = take(own), take(other)
    first = choose(core == 0, mine, theirs)
    second = choose(core == 0, theirs, mine)
    for n, value in enumerate(join(first, second, 1000.0)):
        out[n] = value


def four_kernel(own, r1, r2, r3, out, table):
    z = lax.rem(lax.div(lax.axis_index("gx"), 2), 4)
    place(z, own, (r1, r2, r3), table)
    ports = [take(table.at[j]) for j in range(4)]
    joined = join(join(ports[0], ports[1], 1000.0), join(ports[2], ports[3], 1000.0), 1000.0)
    for n, value in enumerate(joined):
        out[n] = value


def to_runs(blocks, out):
    for p in range(TILES // 2):
        stack = [blocks(band, 2 * p + half) for half in range(2) for band in range(BANDS)]
        out[128 * p : 128 * p + 128, :] = jnp.concatenate(stack, axis=0).T


def cell(ref, l):
    return ref[pl.ds(l, 8, stride=128), :]


def from_runs(turned, store):
    for p in range(TILES // 2):
        block = turned[128 * p : 128 * p + 128, :].T
        for half in range(2):
            for band in range(BANDS):
                at = ROWS * half + 8 * band
                store(band, 2 * p + half, block[at : at + 8, :])


def put(ref):
    def store(band, column, value):
        ref[8 * band : 8 * band + 8, 128 * column : 128 * column + 128] = value

    return store


def y_matrix_kernel(k, along, back, gain, sep, lo, hi, flat_lo, flat_hi, ends, turned):
    to_runs(lambda band, column: flat_tile(k, band, column), turned)
    lane = lax.broadcasted_iota(jnp.int32, (8, 128), 1)
    sublane = lax.broadcasted_iota(jnp.int32, (8, 128), 0)
    very_last = (lane >= 64) & (sublane == 7)
    very_first = (lane < 64) & (sublane == 0)

    def link(l):
        if l == Y_STEPS - 1:
            both = 4000.0 * (cell(turned, l) + y_shift(cell(turned, 0), 1))
            return jnp.where(very_last, 0.0, both)
        return 4000.0 * (cell(turned, l) + cell(turned, l + 1))

    factor(link, Y_STEPS, Y_LEVELS, y_shift, along, back, gain, sep)

    def at_start(l):
        return jnp.where(very_first, 1.0, 0.0) if l == 0 else None

    def at_end(l):
        return jnp.where(very_last, 1.0, 0.0) if l == Y_STEPS - 1 else None

    def to(ref):
        def store(l, value):
            ref[l] = value

        return store

    args = (Y_STEPS, Y_LEVELS, y_shift, along, back, gain, sep)
    solve(at_start, *args, lo, to(lo))
    solve(at_end, *args, hi, to(hi))
    last = Y_STEPS - 1
    ends[...] = jnp.zeros_like(ends)
    ends[0:1, :] = lo[0, 0:1, :]
    ends[1:2, :] = pltpu.roll(lo[last], 64, 1)[7:8, :]
    ends[2:3, :] = pltpu.roll(hi[last], 64, 1)[7:8, :]
    ends[3:4, :] = cell(turned, 0)[0:1, :]
    ends[4:5, :] = pltpu.roll(cell(turned, last), 64, 1)[7:8, :]
    for response, flat in ((lo, flat_lo), (hi, flat_hi)):
        for l in range(Y_STEPS):
            turned[pl.ds(l, 8, stride=128), :] = response[l]
        from_runs(turned, put(flat))


def y_port_kernel(
    own_y, y1, y2, y3, own_z, z1, z2, z3, own, other, u, x_lo, x_hi, t,
    lo_y, hi_y, ends, turned, port, table_y, table_z, flat,
):
    index = lax.axis_index("gx")
    core, z, y = lax.rem(index, 2), lax.rem(lax.div(index, 2), 4), lax.div(index, 8)
    place(y, own_y, (y1, y2, y3), table_y)
    place(z, own_z, (z1, z2, z3), table_z)
    nothing = (jnp.zeros((TILES, 128), F32),) * 3
    scale = 1000.0
    lo, hi = reach(y, [take(table_y.at[j]) for j in range(4)], nothing, nothing, scale)
    lo, hi = reach(z, [take(table_z.at[j]) for j in range(4)], lo, hi, scale)
    mine, theirs = take(own), take(other)
    lo = choose(core == 1, past_up(lo, theirs, scale), lo)
    hi = choose(core == 0, past_down(hi, theirs, scale), hi)
    f_lo, f_hi = flows(mine, lo, hi, scale)
    for i in range(ROWS):
        at = pl.ds((i // 8) * (8 * TILES) + i % 8, TILES, stride=8)
        flat[at, :] = u[i] - f_lo * x_lo[i] + f_hi * x_hi[i]

    def block(band, column):
        return flat_tile(flat, band, column) - 2.0 * flat_tile(t, band, column)

    to_runs(block, turned)
    port[...] = jnp.zeros_like(port)
    for n, response in enumerate((lo_y, hi_y)):
        both = total(response[l] * cell(turned, l) for l in range(Y_STEPS))
        both = jnp.sum(both + pltpu.roll(both, 64, 1), axis=0, keepdims=True)
        port[n : n + 1, :] = both
    port[2:7, :] = ends[0:5, :]


def y_solve_kernel(turned, along, back, gain, sep, t, out, d, again):
    def store(l, value):
        d[l] = value
        again[pl.ds(l, 8, stride=128), :] = value

    def source(l):
        return cell(turned, l)

    solve(source, Y_STEPS, Y_LEVELS, y_shift, along, back, gain, sep, d, store)
    keep = put(out)

    def plus_start(band, column, value):
        keep(band, column, value + flat_tile(t, band, column))

    from_runs(again, plus_start)


def finish_kernel(own, r1, r2, r3, base, y_lo, y_hi, out, table, side, done, sent):
    index = lax.axis_index("gy")
    place(index, own, (r1, r2, r3), table)
    lane = lax.broadcasted_iota(jnp.int32, (1, 128), 1)

    def port_of(ref):
        return tuple(jnp.where(lane < ROWS, ref[n : n + 1, :], 1.0) for n in range(7))

    nothing = (jnp.zeros((1, 128), F32),) * 3
    scale = 4000.0
    lo, hi = reach(index, [port_of(table.at[j]) for j in range(4)], nothing, nothing, scale)
    f_lo, f_hi = flows(port_of(own), lo, hi, scale)
    side[...] = jnp.zeros_like(side)
    side[0:1, :] = f_lo
    side[1:2, :] = f_hi
    upright = side[...].T
    copies = []
    for band in range(BANDS):
        at = slice(8 * band, 8 * band + 8)
        down = jnp.broadcast_to(upright[at, 0:1], (8, 128))
        up = jnp.broadcast_to(upright[at, 1:2], (8, 128))
        keep = put(done)
        for column in range(TILES):
            part = tile(base, band, column)
            part = part - down * tile(y_lo, band, column) + up * tile(y_hi, band, column)
            keep(band, column, part)
        copy = pltpu.make_async_copy(done.at[at, :], out.at[at, :], sent.at[band])
        copy.start()
        copies.append(copy)
    for copy in copies:
        copy.wait()


def around(value, axis, size, stride, step):
    pairs = []
    for i in range(size):
        digit = (i // stride) % 4
        pairs.append((i, i + ((digit + step) % 4 - digit) * stride))
    return lax.ppermute(value, axis, pairs)


def per_device(initial_heat_state, thermal_coefficient):
    t, k = initial_heat_state[0], thermal_coefficient[0]
    own_lo, own_hi = call(
        edges_kernel,
        [struct(8, 128)] * 2,
        [pltpu.VMEM((4, ROWS, 128), F32), pltpu.SemaphoreType.DMA((4,))],
        name="edges",
        grant=56 << 20,
        in_specs=[HBM, HBM],
        out_specs=[VMEM, VMEM],
    )(t, k)
    below = around(own_hi, "gy", 4, 1, 1)
    above = around(own_lo, "gy", 4, 1, 3)
    flat = struct(BANDS * TILES * 8, 128)
    runs = struct(TILES // 2 * 128, 128)
    x_field, y_field, natural = struct(ROWS, TILES, 128), struct(Y_STEPS, 8, 128), struct(ROWS, COLS)
    x_port = struct(7, TILES, 128)
    e, *x_coefficients, x_lo, x_hi, x_ends, t_flat, k_flat = call(
        x_matrix_kernel,
        [
            flat,
            x_field,
            x_field,
            x_field,
            struct((2 * X_LEVELS + 1) * SEGMENTS, TILES, 128),
            x_field,
            x_field,
            x_port,
            flat,
            flat,
        ],
        [scratch(natural), scratch(natural), pltpu.SemaphoreType.DMA((2, BANDS))],
        name="x_matrix",
        in_specs=[HBM, HBM],
        out_specs=[VMEM] * 10,
    )(t, k)
    own, edge = call(
        x_port_kernel,
        [x_port, struct(ROWS, 128)],
        [pltpu.VMEM((128, 128), F32)],
        flops=200_000,
        name="x_port",
    )(x_ends, x_lo, x_hi, own_lo, own_hi, below, above)
    u = call(x_solve_kernel, x_field, [scratch(flat)], flops=700_000, name="x_solve")(
        e, *x_coefficients, edge
    )
    other = lax.ppermute(own, "gx", [(i, i ^ 1) for i in range(32)])
    own_z = call(pair_kernel, x_port, name="pair")(own, other)
    k_y, own_z = lax.optimization_barrier((k_flat, own_z))
    from_z = [around(own_z, "gx", 32, 2, s) for s in (1, 2, 3)]
    *y_coefficients, y_lo, y_hi, flat_lo, flat_hi, y_ends = call(
        y_matrix_kernel,
        [
            y_field,
            y_field,
            y_field,
            struct((2 * Y_LEVELS + 1) * SEGMENTS, 8, 128),
            y_field,
            y_field,
            natural,
            natural,
            struct(8, 128),
        ],
        [scratch(runs)],
        name="y_matrix",
    )(k_y)
    table = pltpu.VMEM((4, 7, TILES, 128), F32)
    own_y = call(four_kernel, x_port, [table], name="four")(own_z, *from_z)
    from_y = [around(own_y, "gx", 32, 8, s) for s in (1, 2, 3)]
    turned, port = call(
        y_port_kernel, [runs, struct(8, 128)], [table, table, scratch(flat)], name="y_port"
    )(own_y, *from_y, own_z, *from_z, own, other, u, x_lo, x_hi, t_flat, y_lo, y_hi, y_ends)
    from_gy = [around(port, "gy", 4, 1, s) for s in (1, 2, 3)]
    base = call(
        y_solve_kernel, natural, [scratch(y_field), scratch(runs)], name="y_solve"
    )(turned, *y_coefficients, t_flat)
    updated = call(
        finish_kernel,
        natural,
        [
            pltpu.VMEM((4, 8, 128), F32),
            pltpu.VMEM((128, 128), F32),
            scratch(natural),
            pltpu.SemaphoreType.DMA((BANDS,)),
        ],
        name="finish",
        in_specs=[VMEM] * 7,
        out_specs=HBM,
    )(port, *from_gy, base, flat_lo, flat_hi)
    return updated[None]


def solution(mesh):
    placed = (P(None, "gx", "gy"), P(None, "gx", "gy"))
    return jax.shard_map(
        per_device, mesh=mesh, in_specs=placed, out_specs=P(None, "gx", "gy"), check_vma=False
    )
```

```python
import jax
import jax.numpy as jnp
from jax import lax
from jax.experimental import pallas as pl
from jax.experimental.pallas import tpu as pltpu
from jax.sharding import PartitionSpec as P

ROWS, COLS = 64, 2048
BANDS, TILES = ROWS // 8, COLS // 128
SEGMENTS = 4
Y_STEPS = 128
X_LEVELS, Y_LEVELS = 2, 6
F32 = jnp.float32
VMEM = pl.BlockSpec(memory_space=pltpu.VMEM)
HBM = pl.BlockSpec(memory_space=pltpu.MemorySpace.HBM)


def struct(*shape):
    return jax.ShapeDtypeStruct(shape, F32)


def scratch(like):
    return pltpu.VMEM(like.shape, like.dtype)


def whole(outs, args):
    return dict(in_specs=[VMEM] * len(args), out_specs=jax.tree.map(lambda _: VMEM, outs))


def call(kernel, outs, buffers=(), flops=2_000_000, name=None, grant=32 << 20, **windows):
    def run(*args):
        return pl.pallas_call(
            kernel,
            out_shape=outs,
            **(windows or whole(outs, args)),
            scratch_shapes=list(buffers),
            compiler_params=pltpu.CompilerParams(vmem_limit_bytes=grant),
            cost_estimate=pl.CostEstimate(flops=flops, bytes_accessed=1 << 20, transcendentals=0),
            name=name,
        )(*args)

    return run


def moved(chain, by, shift):
    out = []
    for s in range(SEGMENTS):
        runs, at = divmod(s + by, SEGMENTS)
        out.append(shift(chain[at], runs) if runs else chain[at])
    return out


def factor(link, n, levels, shift, along, back, gain, sep):
    m = n // SEGMENTS
    near = [link(s * m) for s in range(SEGMENTS)]
    ground = [jnp.ones_like(near[0])] * SEGMENTS
    held = [jnp.ones_like(near[0])] * SEGMENTS
    for step in range(1, m):
        for s in range(SEGMENTS):
            l = s * m + step
            v = link(l)
            r = 1.0 / (near[s] + ground[s] + v)
            t = v * r
            c = near[s] * r
            along[l], back[l], gain[l] = t, c, r
            held[s] = held[s] + ground[s] * c
            near[s] = near[s] * t
            ground[s] = ground[s] * t
            if step < m - 1:
                ground[s] = ground[s] + 1.0
    before = moved(ground, -1, shift)
    own = [held[s] + before[s] for s in range(SEGMENTS)]
    up = near
    down = moved(near, -1, shift)
    for level in range(levels):
        stride = 1 << level
        r = [1.0 / (own[s] + up[s] + down[s]) for s in range(SEGMENTS)]
        r_down, r_up = moved(r, -stride, shift), moved(r, stride, shift)
        own_down, own_up = moved(own, -stride, shift), moved(own, stride, shift)
        down_down, up_up = moved(down, -stride, shift), moved(up, stride, shift)
        for s in range(SEGMENTS):
            a, b = down[s] * r_down[s], up[s] * r_up[s]
            sep[(level * 2) * SEGMENTS + s] = a
            sep[(level * 2 + 1) * SEGMENTS + s] = b
            own[s] = own[s] + a * own_down[s] + b * own_up[s]
            down[s], up[s] = a * down_down[s], b * up_up[s]
    for s in range(SEGMENTS):
        sep[levels * 2 * SEGMENTS + s] = 1.0 / own[s]


def plus(a, b):
    return b if a is None else a if b is None else a + b


def times(a, b):
    return None if a is None else a * b


def solve(source, n, levels, shift, along, back, gain, sep, part, store):
    m = n // SEGMENTS
    total = [source(s * m) for s in range(SEGMENTS)]
    z = [source(s * m + 1) for s in range(SEGMENTS)]
    zero = [[False] * SEGMENTS for _ in range(m)]
    for step in range(1, m):
        for s in range(SEGMENTS):
            l = s * m + step
            zero[step][s] = z[s] is None
            if z[s] is not None:
                part[l] = z[s] * gain[l]
                total[s] = plus(total[s], z[s] * back[l])
                z[s] = z[s] * along[l]
            if step < m - 1:
                z[s] = plus(source(l + 1), z[s])
    shape = jnp.zeros(along.shape[1:], F32)
    z = [shape if v is None else v for v in z]
    before = moved(z, -1, shift)
    total = [plus(total[s], before[s]) for s in range(SEGMENTS)]
    for level in range(levels):
        stride = 1 << level
        lo, hi = moved(total, -stride, shift), moved(total, stride, shift)
        total = [
            total[s]
            + sep[(level * 2) * SEGMENTS + s] * lo[s]
            + sep[(level * 2 + 1) * SEGMENTS + s] * hi[s]
            for s in range(SEGMENTS)
        ]
    value = [total[s] * sep[levels * 2 * SEGMENTS + s] for s in range(SEGMENTS)]
    after = moved(value, 1, shift)
    for s in range(SEGMENTS):
        store(s * m, value[s])
    for step in reversed(range(1, m)):
        for s in range(SEGMENTS):
            l = s * m + step
            known = back[l] * value[s]
            if not zero[step][s]:
                known = known + part[l]
            after[s] = known + along[l] * after[s]
            store(l, after[s])


def x_shift(value, runs):
    return value


def y_shift(value, runs):
    if runs % 2 == 0:
        return pltpu.roll(value, (-(runs // 2)) % 8, 0)
    swapped = pltpu.roll(value, 64, 1)
    late = lax.broadcasted_iota(jnp.int32, value.shape, 1) >= 64
    if runs == 1:
        return jnp.where(late, pltpu.roll(swapped, 7, 0), swapped)
    return jnp.where(late, swapped, pltpu.roll(swapped, 1, 0))


def tile(ref, band, column):
    return ref[8 * band : 8 * band + 8, 128 * column : 128 * column + 128]


def flat_tile(ref, band, column):
    at = (band * TILES + column) * 8
    return ref[at : at + 8, :]


def row(ref, i):
    return ref[pl.ds((i // 8) * (8 * TILES) + i % 8, TILES, stride=8), :]


def edges_kernel(t, k, lo, hi, strips, arrived):
    sides = (pl.ds(0, 128), pl.ds(128 * (TILES - 1), 128))
    copies = [
        pltpu.make_async_copy(ref.at[:, side], strips.at[n], arrived.at[n])
        for n, (side, ref) in enumerate((side, ref) for side in sides for ref in (t, k))
    ]
    for copy in copies:
        copy.start()
    lo[...] = jnp.zeros_like(lo)
    hi[...] = jnp.zeros_like(hi)
    for copy in copies:
        copy.wait()
    lo[0:1, 0:ROWS] = strips[0].T[0:1, :]
    lo[1:2, 0:ROWS] = strips[1].T[0:1, :]
    hi[0:1, 0:ROWS] = strips[2].T[127:128, :]
    hi[1:2, 0:ROWS] = strips[3].T[127:128, :]


def total(terms):
    sums = [None] * 4
    for n, term in enumerate(terms):
        sums[n % 4] = plus(sums[n % 4], term)
    return (sums[0] + sums[1]) + (sums[2] + sums[3])


def x_matrix_kernel(t, k, e, along, back, gain, sep, lo, hi, ends, t_flat, flat, own):
    own[...] = jnp.zeros_like(own)
    for n, (ref, column) in enumerate(((t, 0), (k, 0), (t, TILES - 1), (k, TILES - 1))):
        strip = ref[:, 128 * column : 128 * column + 128].T
        at = 127 if column else 0
        own[n : n + 1, 0:ROWS] = strip[at : at + 1, :]
    lane = lax.broadcasted_iota(jnp.int32, (8, 128), 1)
    for band in range(BANDS):
        ks = [tile(k, band, c) for c in range(TILES)]
        ts = [tile(t, band, c) for c in range(TILES)]
        k_left = [pltpu.roll(v, 127, 1) for v in ks]
        t_left = [pltpu.roll(v, 127, 1) for v in ts]
        flow = []
        for c in range(TILES):
            at = pl.ds((band * TILES + c) * 8, 8)
            flat[at, :] = ks[c]
            t_flat[at, :] = ts[c]
            n = min(c + 1, TILES - 1)
            k_next = jnp.where(lane == 127, k_left[n], k_left[c])
            t_next = jnp.where(lane == 127, t_left[n], t_left[c])
            f = 8000.0 * (ks[c] + k_next) * (t_next - ts[c])
            if c == TILES - 1:
                f = jnp.where(lane == 127, 0.0, f)
            flow.append(f)
        turned = [pltpu.roll(v, 1, 1) for v in flow]
        for c in range(TILES):
            at = pl.ds((band * TILES + c) * 8, 8)
            first = turned[c - 1] if c else jnp.zeros_like(turned[0])
            f_before = jnp.where(lane == 0, first, turned[c])
            e[at, :] = 2.0 * ts[c] + (flow[c] - f_before)

    def link(l):
        if l == ROWS - 1:
            return jnp.zeros((TILES, 128), F32)
        return 1000.0 * (row(flat, l) + row(flat, l + 1))

    factor(link, ROWS, X_LEVELS, x_shift, along, back, gain, sep)
    one = jnp.ones((TILES, 128), F32)

    def at_start(l):
        return one if l == 0 else None

    def at_end(l):
        return one if l == ROWS - 1 else None

    def to(ref):
        def store(l, value):
            ref[l] = value

        return store

    args = (ROWS, X_LEVELS, x_shift, along, back, gain, sep)
    solve(at_start, *args, lo, to(lo))
    solve(at_end, *args, hi, to(hi))
    ends[0] = total(lo[i] * row(e, i) for i in range(ROWS))
    ends[1] = total(hi[i] * row(e, i) for i in range(ROWS))
    ends[2] = lo[0]
    ends[3] = lo[ROWS - 1]
    ends[4] = hi[ROWS - 1]
    ends[5] = row(flat, 0)
    ends[6] = row(flat, ROWS - 1)


def x_port_kernel(ends, lo, hi, own, below, above, port, edge, side):
    at = lax.axis_index("gy")
    side[...] = jnp.zeros_like(side)
    t_lo, k_lo, t_hi, k_hi = (own[n : n + 1, :] for n in range(4))
    before = jnp.where(at == 0, 0.0, below[...])
    after = jnp.where(at == lax.axis_size("gy") - 1, 0.0, above[...])
    side[0:1, :] = -8000.0 * (k_lo + before[1:2, :]) * (t_lo - before[0:1, :])
    side[127:128, :] = 8000.0 * (k_hi + after[1:2, :]) * (after[0:1, :] - t_hi)
    edge[...] = side[...].T[0:ROWS, :]
    lane = lax.broadcasted_iota(jnp.int32, (1, 128), 1)
    for n, response in enumerate((lo, hi)):
        port[n] = ends[n]
        for column, kept in ((0, 0), (TILES - 1, 127)):
            term = edge[...] * response[:, column, :]
            term = jnp.where(lane == kept, jnp.sum(term, axis=0, keepdims=True), 0.0)
            port[n, column : column + 1, :] = port[n, column : column + 1, :] + term
    for n in range(2, 7):
        port[n] = ends[n]


def x_solve_kernel(e, along, back, gain, sep, edge, u, flat):
    lane = lax.broadcasted_iota(jnp.int32, (8, 128), 1)
    flat[...] = e[...]
    for band in range(BANDS):
        part = edge[8 * band : 8 * band + 8, :]
        at = pl.ds(band * TILES * 8, 8)
        flat[at, :] = flat[at, :] + jnp.where(lane == 0, part, 0.0)
        at = pl.ds((band * TILES + TILES - 1) * 8, 8)
        flat[at, :] = flat[at, :] + jnp.where(lane == 127, part, 0.0)

    def store(l, value):
        u[l] = value

    def source(l):
        return row(flat, l)

    solve(source, ROWS, X_LEVELS, x_shift, along, back, gain, sep, u, store)


def take(ref):
    return tuple(ref[n] for n in range(7))


def join(one, two, scale):
    a1, b1, al1, be1, ga1, kf1, kl1 = one
    a2, b2, al2, be2, ga2, kf2, kl2 = two
    rho = 1.0 / (1.0 / (scale * (kl1 + kf2)) + al2 + ga1)
    delta = (a2 - b1) * rho
    return (
        a1 + be1 * delta,
        b2 - be2 * delta,
        al1 - be1 * be1 * rho,
        be1 * be2 * rho,
        ga2 - be2 * be2 * rho,
        kf1,
        kl2,
    )


def past_up(state, port, scale):
    p, q, k = state
    a, b, al, be, ga, kf, kl = port
    w = be / (1.0 / (scale * (k + kf)) + al + q)
    return (b - w * (a - p), ga - w * be, kl)


def past_down(state, port, scale):
    p, q, k = state
    a, b, al, be, ga, kf, kl = port
    w = be / (1.0 / (scale * (k + kl)) + ga + q)
    return (a + w * (p - b), al - w * be, kf)


def choose(condition, new, old):
    return tuple(jnp.where(condition, x, y) for x, y in zip(new, old))


def reach(index, ports, lo, hi, scale):
    count = len(ports)
    for n in range(count - 1):
        lo = choose(n < index, past_up(lo, ports[n], scale), lo)
    for n in reversed(range(1, count)):
        hi = choose(n > index, past_down(hi, ports[n], scale), hi)
    return lo, hi


def flows(port, lo, hi, scale):
    a, b, al, be, ga, kf, kl = port
    d_lo = 1.0 / (scale * (lo[2] + kf)) + al + lo[1]
    d_hi = 1.0 / (scale * (hi[2] + kl)) + ga + hi[1]
    c_lo, c_hi = a - lo[0], hi[0] - b
    inverse = 1.0 / (d_lo * d_hi - be * be)
    return (d_hi * c_lo + be * c_hi) * inverse, (d_lo * c_hi + be * c_lo) * inverse


def place(index, own, received, table):
    table[index] = own[...]
    for s in (1, 2, 3):
        table[lax.rem(index + 4 - s, 4)] = received[s - 1][...]


def pair_kernel(own, other, out):
    core = lax.rem(lax.axis_index("gx"), 2)
    mine, theirs = take(own), take(other)
    first = choose(core == 0, mine, theirs)
    second = choose(core == 0, theirs, mine)
    for n, value in enumerate(join(first, second, 1000.0)):
        out[n] = value


def four_kernel(own, r1, r2, r3, out, table):
    z = lax.rem(lax.div(lax.axis_index("gx"), 2), 4)
    place(z, own, (r1, r2, r3), table)
    ports = [take(table.at[j]) for j in range(4)]
    joined = join(join(ports[0], ports[1], 1000.0), join(ports[2], ports[3], 1000.0), 1000.0)
    for n, value in enumerate(joined):
        out[n] = value


def to_runs(blocks, out):
    for p in range(TILES // 2):
        stack = [blocks(band, 2 * p + half) for half in range(2) for band in range(BANDS)]
        out[128 * p : 128 * p + 128, :] = jnp.concatenate(stack, axis=0).T


def cell(ref, l):
    return ref[pl.ds(l, 8, stride=128), :]


def from_runs(turned, store):
    for p in range(TILES // 2):
        block = turned[128 * p : 128 * p + 128, :].T
        for half in range(2):
            for band in range(BANDS):
                at = ROWS * half + 8 * band
                store(band, 2 * p + half, block[at : at + 8, :])


def put(ref):
    def store(band, column, value):
        ref[8 * band : 8 * band + 8, 128 * column : 128 * column + 128] = value

    return store


def y_matrix_kernel(k, along, back, gain, sep, lo, hi, flat_lo, flat_hi, ends, turned):
    to_runs(lambda band, column: flat_tile(k, band, column), turned)
    lane = lax.broadcasted_iota(jnp.int32, (8, 128), 1)
    sublane = lax.broadcasted_iota(jnp.int32, (8, 128), 0)
    very_last = (lane >= 64) & (sublane == 7)
    very_first = (lane < 64) & (sublane == 0)

    def link(l):
        if l == Y_STEPS - 1:
            both = 4000.0 * (cell(turned, l) + y_shift(cell(turned, 0), 1))
            return jnp.where(very_last, 0.0, both)
        return 4000.0 * (cell(turned, l) + cell(turned, l + 1))

    factor(link, Y_STEPS, Y_LEVELS, y_shift, along, back, gain, sep)

    def at_start(l):
        return jnp.where(very_first, 1.0, 0.0) if l == 0 else None

    def at_end(l):
        return jnp.where(very_last, 1.0, 0.0) if l == Y_STEPS - 1 else None

    def to(ref):
        def store(l, value):
            ref[l] = value

        return store

    args = (Y_STEPS, Y_LEVELS, y_shift, along, back, gain, sep)
    solve(at_start, *args, lo, to(lo))
    solve(at_end, *args, hi, to(hi))
    last = Y_STEPS - 1
    ends[...] = jnp.zeros_like(ends)
    ends[0:1, :] = lo[0, 0:1, :]
    ends[1:2, :] = pltpu.roll(lo[last], 64, 1)[7:8, :]
    ends[2:3, :] = pltpu.roll(hi[last], 64, 1)[7:8, :]
    ends[3:4, :] = cell(turned, 0)[0:1, :]
    ends[4:5, :] = pltpu.roll(cell(turned, last), 64, 1)[7:8, :]
    for response, flat in ((lo, flat_lo), (hi, flat_hi)):
        for l in range(Y_STEPS):
            turned[pl.ds(l, 8, stride=128), :] = response[l]
        from_runs(turned, put(flat))


def y_port_kernel(
    own_y, y1, y2, y3, own_z, z1, z2, z3, own, other, u, x_lo, x_hi, t,
    lo_y, hi_y, ends, turned, port, table_y, table_z, flat,
):
    index = lax.axis_index("gx")
    core, z, y = lax.rem(index, 2), lax.rem(lax.div(index, 2), 4), lax.div(index, 8)
    place(y, own_y, (y1, y2, y3), table_y)
    place(z, own_z, (z1, z2, z3), table_z)
    nothing = (jnp.zeros((TILES, 128), F32),) * 3
    scale = 1000.0
    lo, hi = reach(y, [take(table_y.at[j]) for j in range(4)], nothing, nothing, scale)
    lo, hi = reach(z, [take(table_z.at[j]) for j in range(4)], lo, hi, scale)
    mine, theirs = take(own), take(other)
    lo = choose(core == 1, past_up(lo, theirs, scale), lo)
    hi = choose(core == 0, past_down(hi, theirs, scale), hi)
    f_lo, f_hi = flows(mine, lo, hi, scale)
    for i in range(ROWS):
        at = pl.ds((i // 8) * (8 * TILES) + i % 8, TILES, stride=8)
        flat[at, :] = u[i] - f_lo * x_lo[i] + f_hi * x_hi[i]

    def block(band, column):
        return flat_tile(flat, band, column) - 2.0 * flat_tile(t, band, column)

    to_runs(block, turned)
    port[...] = jnp.zeros_like(port)
    for n, response in enumerate((lo_y, hi_y)):
        both = total(response[l] * cell(turned, l) for l in range(Y_STEPS))
        both = jnp.sum(both + pltpu.roll(both, 64, 1), axis=0, keepdims=True)
        port[n : n + 1, :] = both
    port[2:7, :] = ends[0:5, :]


def y_solve_kernel(turned, along, back, gain, sep, t, out, d, again):
    def store(l, value):
        d[l] = value
        again[pl.ds(l, 8, stride=128), :] = value

    def source(l):
        return cell(turned, l)

    solve(source, Y_STEPS, Y_LEVELS, y_shift, along, back, gain, sep, d, store)
    keep = put(out)

    def plus_start(band, column, value):
        keep(band, column, value + flat_tile(t, band, column))

    from_runs(again, plus_start)


def finish_kernel(own, r1, r2, r3, base, y_lo, y_hi, out, table, side, done, sent):
    index = lax.axis_index("gy")
    place(index, own, (r1, r2, r3), table)
    lane = lax.broadcasted_iota(jnp.int32, (1, 128), 1)

    def port_of(ref):
        return tuple(jnp.where(lane < ROWS, ref[n : n + 1, :], 1.0) for n in range(7))

    nothing = (jnp.zeros((1, 128), F32),) * 3
    scale = 4000.0
    lo, hi = reach(index, [port_of(table.at[j]) for j in range(4)], nothing, nothing, scale)
    f_lo, f_hi = flows(port_of(own), lo, hi, scale)
    side[...] = jnp.zeros_like(side)
    side[0:1, :] = f_lo
    side[1:2, :] = f_hi
    upright = side[...].T
    copies = []
    for band in range(BANDS):
        at = slice(8 * band, 8 * band + 8)
        down = jnp.broadcast_to(upright[at, 0:1], (8, 128))
        up = jnp.broadcast_to(upright[at, 1:2], (8, 128))
        keep = put(done)
        for column in range(TILES):
            part = tile(base, band, column)
            part = part - down * tile(y_lo, band, column) + up * tile(y_hi, band, column)
            keep(band, column, part)
        copy = pltpu.make_async_copy(done.at[at, :], out.at[at, :], sent.at[band])
        copy.start()
        copies.append(copy)
    for copy in copies:
        copy.wait()


def around(value, axis, size, stride, step):
    pairs = []
    for i in range(size):
        digit = (i // stride) % 4
        pairs.append((i, i + ((digit + step) % 4 - digit) * stride))
    return lax.ppermute(value, axis, pairs)


def per_device(initial_heat_state, thermal_coefficient):
    t, k = initial_heat_state[0], thermal_coefficient[0]
    own_lo, own_hi = call(
        edges_kernel,
        [struct(8, 128)] * 2,
        [pltpu.VMEM((4, ROWS, 128), F32), pltpu.SemaphoreType.DMA((4,))],
        name="edges",
        grant=56 << 20,
        in_specs=[HBM, HBM],
        out_specs=[VMEM, VMEM],
    )(t, k)
    below = around(own_hi, "gy", 4, 1, 1)
    above = around(own_lo, "gy", 4, 1, 3)
    flat = struct(BANDS * TILES * 8, 128)
    runs = struct(TILES // 2 * 128, 128)
    x_field, y_field, natural = struct(ROWS, TILES, 128), struct(Y_STEPS, 8, 128), struct(ROWS, COLS)
    x_port = struct(7, TILES, 128)
    e, *x_coefficients, x_lo, x_hi, x_ends, t_flat, k_flat, own = call(
        x_matrix_kernel,
        [
            flat,
            x_field,
            x_field,
            x_field,
            struct((2 * X_LEVELS + 1) * SEGMENTS, TILES, 128),
            x_field,
            x_field,
            x_port,
            flat,
            flat,
            struct(8, 128),
        ],
        name="x_matrix",
    )(t, k)
    own, edge = call(
        x_port_kernel,
        [x_port, struct(ROWS, 128)],
        [pltpu.VMEM((128, 128), F32)],
        flops=200_000,
        name="x_port",
    )(x_ends, x_lo, x_hi, own, below, above)
    u = call(x_solve_kernel, x_field, [scratch(flat)], flops=700_000, name="x_solve")(
        e, *x_coefficients, edge
    )
    other = lax.ppermute(own, "gx", [(i, i ^ 1) for i in range(32)])
    own_z = call(pair_kernel, x_port, name="pair")(own, other)
    k_y, own_z = lax.optimization_barrier((k_flat, own_z))
    from_z = [around(own_z, "gx", 32, 2, s) for s in (1, 2, 3)]
    *y_coefficients, y_lo, y_hi, flat_lo, flat_hi, y_ends = call(
        y_matrix_kernel,
        [
            y_field,
            y_field,
            y_field,
            struct((2 * Y_LEVELS + 1) * SEGMENTS, 8, 128),
            y_field,
            y_field,
            natural,
            natural,
            struct(8, 128),
        ],
        [scratch(runs)],
        name="y_matrix",
    )(k_y)
    table = pltpu.VMEM((4, 7, TILES, 128), F32)
    own_y = call(four_kernel, x_port, [table], name="four")(own_z, *from_z)
    from_y = [around(own_y, "gx", 32, 8, s) for s in (1, 2, 3)]
    turned, port = call(
        y_port_kernel, [runs, struct(8, 128)], [table, table, scratch(flat)], name="y_port"
    )(own_y, *from_y, own_z, *from_z, own, other, u, x_lo, x_hi, t_flat, y_lo, y_hi, y_ends)
    from_gy = [around(port, "gy", 4, 1, s) for s in (1, 2, 3)]
    base = call(
        y_solve_kernel, natural, [scratch(y_field), scratch(runs)], name="y_solve"
    )(turned, *y_coefficients, t_flat)
    updated = call(
        finish_kernel,
        natural,
        [
            pltpu.VMEM((4, 8, 128), F32),
            pltpu.VMEM((128, 128), F32),
            scratch(natural),
            pltpu.SemaphoreType.DMA((BANDS,)),
        ],
        name="finish",
        in_specs=[VMEM] * 7,
        out_specs=HBM,
    )(port, *from_gy, base, flat_lo, flat_hi)
    return updated[None]


def solution(mesh):
    placed = (P(None, "gx", "gy"), P(None, "gx", "gy"))
    return jax.shard_map(
        per_device, mesh=mesh, in_specs=placed, out_specs=P(None, "gx", "gy"), check_vma=False
    )
```

```python
import jax
import jax.numpy as jnp
from jax import lax
from jax.experimental import pallas as pl
from jax.experimental.pallas import tpu as pltpu
from jax.sharding import PartitionSpec as P

ROWS, COLS = 64, 2048
BANDS, TILES = ROWS // 8, COLS // 128
SEGMENTS = 4
Y_STEPS = 128
X_LEVELS, Y_LEVELS = 2, 6
F32 = jnp.float32
VMEM = pl.BlockSpec(memory_space=pltpu.VMEM)
HBM = pl.BlockSpec(memory_space=pltpu.MemorySpace.HBM)


def struct(*shape):
    return jax.ShapeDtypeStruct(shape, F32)


def scratch(like):
    return pltpu.VMEM(like.shape, like.dtype)


def whole(outs, args):
    return dict(in_specs=[VMEM] * len(args), out_specs=jax.tree.map(lambda _: VMEM, outs))


def call(kernel, outs, buffers=(), flops=2_000_000, name=None, grant=32 << 20, **windows):
    def run(*args):
        return pl.pallas_call(
            kernel,
            out_shape=outs,
            **(windows or whole(outs, args)),
            scratch_shapes=list(buffers),
            compiler_params=pltpu.CompilerParams(vmem_limit_bytes=grant),
            cost_estimate=pl.CostEstimate(flops=flops, bytes_accessed=1 << 20, transcendentals=0),
            name=name,
        )(*args)

    return run


def moved(chain, by, shift):
    out = []
    for s in range(SEGMENTS):
        runs, at = divmod(s + by, SEGMENTS)
        out.append(shift(chain[at], runs) if runs else chain[at])
    return out


def factor(link, n, levels, shift, along, back, gain, sep):
    m = n // SEGMENTS
    near = [link(s * m) for s in range(SEGMENTS)]
    ground = [jnp.ones_like(near[0])] * SEGMENTS
    held = [jnp.ones_like(near[0])] * SEGMENTS
    for step in range(1, m):
        for s in range(SEGMENTS):
            l = s * m + step
            v = link(l)
            r = 1.0 / (near[s] + ground[s] + v)
            t = v * r
            c = near[s] * r
            along[l], back[l], gain[l] = t, c, r
            held[s] = held[s] + ground[s] * c
            near[s] = near[s] * t
            ground[s] = ground[s] * t
            if step < m - 1:
                ground[s] = ground[s] + 1.0
    before = moved(ground, -1, shift)
    own = [held[s] + before[s] for s in range(SEGMENTS)]
    up = near
    down = moved(near, -1, shift)
    for level in range(levels):
        stride = 1 << level
        r = [1.0 / (own[s] + up[s] + down[s]) for s in range(SEGMENTS)]
        r_down, r_up = moved(r, -stride, shift), moved(r, stride, shift)
        own_down, own_up = moved(own, -stride, shift), moved(own, stride, shift)
        down_down, up_up = moved(down, -stride, shift), moved(up, stride, shift)
        for s in range(SEGMENTS):
            a, b = down[s] * r_down[s], up[s] * r_up[s]
            sep[(level * 2) * SEGMENTS + s] = a
            sep[(level * 2 + 1) * SEGMENTS + s] = b
            own[s] = own[s] + a * own_down[s] + b * own_up[s]
            down[s], up[s] = a * down_down[s], b * up_up[s]
    for s in range(SEGMENTS):
        sep[levels * 2 * SEGMENTS + s] = 1.0 / own[s]


def plus(a, b):
    return b if a is None else a if b is None else a + b


def times(a, b):
    return None if a is None else a * b


def solve(source, n, levels, shift, along, back, gain, sep, part, store):
    m = n // SEGMENTS
    total = [source(s * m) for s in range(SEGMENTS)]
    z = [source(s * m + 1) for s in range(SEGMENTS)]
    zero = [[False] * SEGMENTS for _ in range(m)]
    for step in range(1, m):
        for s in range(SEGMENTS):
            l = s * m + step
            zero[step][s] = z[s] is None
            if z[s] is not None:
                part[l] = z[s] * gain[l]
                total[s] = plus(total[s], z[s] * back[l])
                z[s] = z[s] * along[l]
            if step < m - 1:
                z[s] = plus(source(l + 1), z[s])
    shape = jnp.zeros(along.shape[1:], F32)
    z = [shape if v is None else v for v in z]
    before = moved(z, -1, shift)
    total = [plus(total[s], before[s]) for s in range(SEGMENTS)]
    for level in range(levels):
        stride = 1 << level
        lo, hi = moved(total, -stride, shift), moved(total, stride, shift)
        total = [
            total[s]
            + sep[(level * 2) * SEGMENTS + s] * lo[s]
            + sep[(level * 2 + 1) * SEGMENTS + s] * hi[s]
            for s in range(SEGMENTS)
        ]
    value = [total[s] * sep[levels * 2 * SEGMENTS + s] for s in range(SEGMENTS)]
    after = moved(value, 1, shift)
    for s in range(SEGMENTS):
        store(s * m, value[s])
    for step in reversed(range(1, m)):
        for s in range(SEGMENTS):
            l = s * m + step
            known = back[l] * value[s]
            if not zero[step][s]:
                known = known + part[l]
            after[s] = known + along[l] * after[s]
            store(l, after[s])


def x_shift(value, runs):
    return value


def y_shift(value, runs):
    if runs % 2 == 0:
        return pltpu.roll(value, (-(runs // 2)) % 8, 0)
    swapped = pltpu.roll(value, 64, 1)
    late = lax.broadcasted_iota(jnp.int32, value.shape, 1) >= 64
    if runs == 1:
        return jnp.where(late, pltpu.roll(swapped, 7, 0), swapped)
    return jnp.where(late, swapped, pltpu.roll(swapped, 1, 0))


def tile(ref, band, column):
    return ref[8 * band : 8 * band + 8, 128 * column : 128 * column + 128]


def flat_tile(ref, band, column):
    at = (band * TILES + column) * 8
    return ref[at : at + 8, :]


def row(ref, i):
    return ref[pl.ds((i // 8) * (8 * TILES) + i % 8, TILES, stride=8), :]


def edges_kernel(t, k, lo, hi, strips, arrived):
    sides = (pl.ds(0, 128), pl.ds(128 * (TILES - 1), 128))
    copies = [
        pltpu.make_async_copy(ref.at[:, side], strips.at[n], arrived.at[n])
        for n, (side, ref) in enumerate((side, ref) for side in sides for ref in (t, k))
    ]
    for copy in copies:
        copy.start()
    lo[...] = jnp.zeros_like(lo)
    hi[...] = jnp.zeros_like(hi)
    for copy in copies:
        copy.wait()
    lo[0:1, 0:ROWS] = strips[0].T[0:1, :]
    lo[1:2, 0:ROWS] = strips[1].T[0:1, :]
    hi[0:1, 0:ROWS] = strips[2].T[127:128, :]
    hi[1:2, 0:ROWS] = strips[3].T[127:128, :]


def total(terms):
    sums = [None] * 4
    for n, term in enumerate(terms):
        sums[n % 4] = plus(sums[n % 4], term)
    return (sums[0] + sums[1]) + (sums[2] + sums[3])


def x_matrix_kernel(t, k, e, along, back, gain, sep, lo, hi, ends, t_flat, flat, own):
    own[...] = jnp.zeros_like(own)
    for n, (ref, column) in enumerate(((t, 0), (k, 0), (t, TILES - 1), (k, TILES - 1))):
        strip = ref[:, 128 * column : 128 * column + 128].T
        at = 127 if column else 0
        own[n : n + 1, 0:ROWS] = strip[at : at + 1, :]
    lane = lax.broadcasted_iota(jnp.int32, (8, 128), 1)
    for band in range(BANDS):
        ks = [tile(k, band, c) for c in range(TILES)]
        ts = [tile(t, band, c) for c in range(TILES)]
        k_left = [pltpu.roll(v, 127, 1) for v in ks]
        t_left = [pltpu.roll(v, 127, 1) for v in ts]
        flow = []
        for c in range(TILES):
            at = pl.ds((band * TILES + c) * 8, 8)
            flat[at, :] = ks[c]
            t_flat[at, :] = ts[c]
            n = min(c + 1, TILES - 1)
            k_next = jnp.where(lane == 127, k_left[n], k_left[c])
            t_next = jnp.where(lane == 127, t_left[n], t_left[c])
            f = 8000.0 * (ks[c] + k_next) * (t_next - ts[c])
            if c == TILES - 1:
                f = jnp.where(lane == 127, 0.0, f)
            flow.append(f)
        turned = [pltpu.roll(v, 1, 1) for v in flow]
        for c in range(TILES):
            at = pl.ds((band * TILES + c) * 8, 8)
            first = turned[c - 1] if c else jnp.zeros_like(turned[0])
            f_before = jnp.where(lane == 0, first, turned[c])
            e[at, :] = 2.0 * ts[c] + (flow[c] - f_before)

    def link(l):
        if l == ROWS - 1:
            return jnp.zeros((TILES, 128), F32)
        return 1000.0 * (row(flat, l) + row(flat, l + 1))

    factor(link, ROWS, X_LEVELS, x_shift, along, back, gain, sep)
    one = jnp.ones((TILES, 128), F32)

    def at_start(l):
        return one if l == 0 else None

    def at_end(l):
        return one if l == ROWS - 1 else None

    def to(ref):
        def store(l, value):
            ref[l] = value

        return store

    args = (ROWS, X_LEVELS, x_shift, along, back, gain, sep)
    solve(at_start, *args, lo, to(lo))
    solve(at_end, *args, hi, to(hi))
    ends[0] = total(lo[i] * row(e, i) for i in range(ROWS))
    ends[1] = total(hi[i] * row(e, i) for i in range(ROWS))
    ends[2] = lo[0]
    ends[3] = lo[ROWS - 1]
    ends[4] = hi[ROWS - 1]
    ends[5] = row(flat, 0)
    ends[6] = row(flat, ROWS - 1)


def x_port_kernel(ends, lo, hi, own, below, above, port, edge, side):
    at = lax.axis_index("gy")
    side[...] = jnp.zeros_like(side)
    t_lo, k_lo, t_hi, k_hi = (own[n : n + 1, :] for n in range(4))
    before = jnp.where(at == 0, 0.0, below[...])
    after = jnp.where(at == lax.axis_size("gy") - 1, 0.0, above[...])
    side[0:1, :] = -8000.0 * (k_lo + before[1:2, :]) * (t_lo - before[0:1, :])
    side[127:128, :] = 8000.0 * (k_hi + after[1:2, :]) * (after[0:1, :] - t_hi)
    edge[...] = side[...].T[0:ROWS, :]
    lane = lax.broadcasted_iota(jnp.int32, (1, 128), 1)
    for n, response in enumerate((lo, hi)):
        port[n] = ends[n]
        for column, kept in ((0, 0), (TILES - 1, 127)):
            term = edge[...] * response[:, column, :]
            term = jnp.where(lane == kept, jnp.sum(term, axis=0, keepdims=True), 0.0)
            port[n, column : column + 1, :] = port[n, column : column + 1, :] + term
    for n in range(2, 7):
        port[n] = ends[n]


def x_solve_kernel(e, along, back, gain, sep, edge, u, flat):
    lane = lax.broadcasted_iota(jnp.int32, (8, 128), 1)
    flat[...] = e[...]
    for band in range(BANDS):
        part = edge[8 * band : 8 * band + 8, :]
        at = pl.ds(band * TILES * 8, 8)
        flat[at, :] = flat[at, :] + jnp.where(lane == 0, part, 0.0)
        at = pl.ds((band * TILES + TILES - 1) * 8, 8)
        flat[at, :] = flat[at, :] + jnp.where(lane == 127, part, 0.0)

    def store(l, value):
        u[l] = value

    def source(l):
        return row(flat, l)

    solve(source, ROWS, X_LEVELS, x_shift, along, back, gain, sep, u, store)


def take(ref):
    return tuple(ref[n] for n in range(7))


def join(one, two, scale):
    a1, b1, al1, be1, ga1, kf1, kl1 = one
    a2, b2, al2, be2, ga2, kf2, kl2 = two
    rho = 1.0 / (1.0 / (scale * (kl1 + kf2)) + al2 + ga1)
    delta = (a2 - b1) * rho
    return (
        a1 + be1 * delta,
        b2 - be2 * delta,
        al1 - be1 * be1 * rho,
        be1 * be2 * rho,
        ga2 - be2 * be2 * rho,
        kf1,
        kl2,
    )


def past_up(state, port, scale):
    p, q, k = state
    a, b, al, be, ga, kf, kl = port
    w = be / (1.0 / (scale * (k + kf)) + al + q)
    return (b - w * (a - p), ga - w * be, kl)


def past_down(state, port, scale):
    p, q, k = state
    a, b, al, be, ga, kf, kl = port
    w = be / (1.0 / (scale * (k + kl)) + ga + q)
    return (a + w * (p - b), al - w * be, kf)


def choose(condition, new, old):
    return tuple(jnp.where(condition, x, y) for x, y in zip(new, old))


def reach(index, ports, lo, hi, scale):
    count = len(ports)
    for n in range(count - 1):
        lo = choose(n < index, past_up(lo, ports[n], scale), lo)
    for n in reversed(range(1, count)):
        hi = choose(n > index, past_down(hi, ports[n], scale), hi)
    return lo, hi


def flows(port, lo, hi, scale):
    a, b, al, be, ga, kf, kl = port
    d_lo = 1.0 / (scale * (lo[2] + kf)) + al + lo[1]
    d_hi = 1.0 / (scale * (hi[2] + kl)) + ga + hi[1]
    c_lo, c_hi = a - lo[0], hi[0] - b
    inverse = 1.0 / (d_lo * d_hi - be * be)
    return (d_hi * c_lo + be * c_hi) * inverse, (d_lo * c_hi + be * c_lo) * inverse


def place(index, own, received, table):
    table[index] = own[...]
    for s in (1, 2, 3):
        table[lax.rem(index + 4 - s, 4)] = received[s - 1][...]


def pair_kernel(own, other, out):
    core = lax.rem(lax.axis_index("gx"), 2)
    mine, theirs = take(own), take(other)
    first = choose(core == 0, mine, theirs)
    second = choose(core == 0, theirs, mine)
    for n, value in enumerate(join(first, second, 1000.0)):
        out[n] = value


def four_kernel(own, r1, r2, r3, out, table):
    z = lax.rem(lax.div(lax.axis_index("gx"), 2), 4)
    place(z, own, (r1, r2, r3), table)
    ports = [take(table.at[j]) for j in range(4)]
    joined = join(join(ports[0], ports[1], 1000.0), join(ports[2], ports[3], 1000.0), 1000.0)
    for n, value in enumerate(joined):
        out[n] = value


def to_runs(blocks, out):
    for p in range(TILES // 2):
        stack = [blocks(band, 2 * p + half) for half in range(2) for band in range(BANDS)]
        out[128 * p : 128 * p + 128, :] = jnp.concatenate(stack, axis=0).T


def cell(ref, l):
    return ref[pl.ds(l, 8, stride=128), :]


def from_runs(turned, store):
    for p in range(TILES // 2):
        block = turned[128 * p : 128 * p + 128, :].T
        for half in range(2):
            for band in range(BANDS):
                at = ROWS * half + 8 * band
                store(band, 2 * p + half, block[at : at + 8, :])


def put(ref):
    def store(band, column, value):
        ref[8 * band : 8 * band + 8, 128 * column : 128 * column + 128] = value

    return store


def y_matrix_kernel(k, along, back, gain, sep, lo, hi, flat_lo, flat_hi, ends, turned):
    to_runs(lambda band, column: flat_tile(k, band, column), turned)
    lane = lax.broadcasted_iota(jnp.int32, (8, 128), 1)
    sublane = lax.broadcasted_iota(jnp.int32, (8, 128), 0)
    very_last = (lane >= 64) & (sublane == 7)
    very_first = (lane < 64) & (sublane == 0)

    def link(l):
        if l == Y_STEPS - 1:
            both = 4000.0 * (cell(turned, l) + y_shift(cell(turned, 0), 1))
            return jnp.where(very_last, 0.0, both)
        return 4000.0 * (cell(turned, l) + cell(turned, l + 1))

    factor(link, Y_STEPS, Y_LEVELS, y_shift, along, back, gain, sep)

    def at_start(l):
        return jnp.where(very_first, 1.0, 0.0) if l == 0 else None

    def at_end(l):
        return jnp.where(very_last, 1.0, 0.0) if l == Y_STEPS - 1 else None

    def to(ref):
        def store(l, value):
            ref[l] = value

        return store

    args = (Y_STEPS, Y_LEVELS, y_shift, along, back, gain, sep)
    solve(at_start, *args, lo, to(lo))
    solve(at_end, *args, hi, to(hi))
    last = Y_STEPS - 1
    ends[...] = jnp.zeros_like(ends)
    ends[0:1, :] = lo[0, 0:1, :]
    ends[1:2, :] = pltpu.roll(lo[last], 64, 1)[7:8, :]
    ends[2:3, :] = pltpu.roll(hi[last], 64, 1)[7:8, :]
    ends[3:4, :] = cell(turned, 0)[0:1, :]
    ends[4:5, :] = pltpu.roll(cell(turned, last), 64, 1)[7:8, :]
    for response, flat in ((lo, flat_lo), (hi, flat_hi)):
        for l in range(Y_STEPS):
            turned[pl.ds(l, 8, stride=128), :] = response[l]
        from_runs(turned, put(flat))


def y_port_kernel(
    own_y, y1, y2, y3, own_z, z1, z2, z3, own, other, u, x_lo, x_hi, t,
    lo_y, hi_y, ends, turned, port, table_y, table_z, flat,
):
    index = lax.axis_index("gx")
    core, z, y = lax.rem(index, 2), lax.rem(lax.div(index, 2), 4), lax.div(index, 8)
    place(y, own_y, (y1, y2, y3), table_y)
    place(z, own_z, (z1, z2, z3), table_z)
    nothing = (jnp.zeros((TILES, 128), F32),) * 3
    scale = 1000.0
    lo, hi = reach(y, [take(table_y.at[j]) for j in range(4)], nothing, nothing, scale)
    lo, hi = reach(z, [take(table_z.at[j]) for j in range(4)], lo, hi, scale)
    mine, theirs = take(own), take(other)
    lo = choose(core == 1, past_up(lo, theirs, scale), lo)
    hi = choose(core == 0, past_down(hi, theirs, scale), hi)
    f_lo, f_hi = flows(mine, lo, hi, scale)
    for i in range(ROWS):
        at = pl.ds((i // 8) * (8 * TILES) + i % 8, TILES, stride=8)
        flat[at, :] = u[i] - f_lo * x_lo[i] + f_hi * x_hi[i]

    def block(band, column):
        return flat_tile(flat, band, column) - 2.0 * flat_tile(t, band, column)

    to_runs(block, turned)
    port[...] = jnp.zeros_like(port)
    for n, response in enumerate((lo_y, hi_y)):
        both = total(response[l] * cell(turned, l) for l in range(Y_STEPS))
        both = jnp.sum(both + pltpu.roll(both, 64, 1), axis=0, keepdims=True)
        port[n : n + 1, :] = both
    port[2:7, :] = ends[0:5, :]


def y_solve_kernel(turned, along, back, gain, sep, t, out, d, again):
    def store(l, value):
        d[l] = value
        again[pl.ds(l, 8, stride=128), :] = value

    def source(l):
        return cell(turned, l)

    solve(source, Y_STEPS, Y_LEVELS, y_shift, along, back, gain, sep, d, store)
    keep = put(out)

    def plus_start(band, column, value):
        keep(band, column, value + flat_tile(t, band, column))

    from_runs(again, plus_start)


def finish_kernel(own, r1, r2, r3, base, y_lo, y_hi, out, table, side, done, sent):
    index = lax.axis_index("gy")
    place(index, own, (r1, r2, r3), table)
    lane = lax.broadcasted_iota(jnp.int32, (1, 128), 1)

    def port_of(ref):
        return tuple(jnp.where(lane < ROWS, ref[n : n + 1, :], 1.0) for n in range(7))

    nothing = (jnp.zeros((1, 128), F32),) * 3
    scale = 4000.0
    lo, hi = reach(index, [port_of(table.at[j]) for j in range(4)], nothing, nothing, scale)
    f_lo, f_hi = flows(port_of(own), lo, hi, scale)
    side[...] = jnp.zeros_like(side)
    side[0:1, :] = f_lo
    side[1:2, :] = f_hi
    upright = side[...].T
    copies = []
    for band in range(BANDS):
        at = slice(8 * band, 8 * band + 8)
        down = jnp.broadcast_to(upright[at, 0:1], (8, 128))
        up = jnp.broadcast_to(upright[at, 1:2], (8, 128))
        keep = put(done)
        for column in range(TILES):
            part = tile(base, band, column)
            part = part - down * tile(y_lo, band, column) + up * tile(y_hi, band, column)
            keep(band, column, part)
        copy = pltpu.make_async_copy(done.at[at, :], out.at[at, :], sent.at[band])
        copy.start()
        copies.append(copy)
    for copy in copies:
        copy.wait()


def around(value, axis, size, stride, step, cross=0):
    pairs = []
    for i in range(size):
        digit = (i // stride) % 4
        pairs.append((i, (i + ((digit + step) % 4 - digit) * stride) ^ cross))
    return lax.ppermute(value, axis, pairs)


def per_device(initial_heat_state, thermal_coefficient):
    t, k = initial_heat_state[0], thermal_coefficient[0]
    own_lo, own_hi = call(
        edges_kernel,
        [struct(8, 128)] * 2,
        [pltpu.VMEM((4, ROWS, 128), F32), pltpu.SemaphoreType.DMA((4,))],
        name="edges",
        grant=56 << 20,
        in_specs=[HBM, HBM],
        out_specs=[VMEM, VMEM],
    )(t, k)
    below = around(own_hi, "gy", 4, 1, 1)
    above = around(own_lo, "gy", 4, 1, 3)
    flat = struct(BANDS * TILES * 8, 128)
    runs = struct(TILES // 2 * 128, 128)
    x_field, y_field, natural = struct(ROWS, TILES, 128), struct(Y_STEPS, 8, 128), struct(ROWS, COLS)
    x_port = struct(7, TILES, 128)
    e, *x_coefficients, x_lo, x_hi, x_ends, t_flat, k_flat, own = call(
        x_matrix_kernel,
        [
            flat,
            x_field,
            x_field,
            x_field,
            struct((2 * X_LEVELS + 1) * SEGMENTS, TILES, 128),
            x_field,
            x_field,
            x_port,
            flat,
            flat,
            struct(8, 128),
        ],
        name="x_matrix",
    )(t, k)
    own, edge = call(
        x_port_kernel,
        [x_port, struct(ROWS, 128)],
        [pltpu.VMEM((128, 128), F32)],
        flops=200_000,
        name="x_port",
    )(x_ends, x_lo, x_hi, own, below, above)
    u = call(x_solve_kernel, x_field, [scratch(flat)], flops=700_000, name="x_solve")(
        e, *x_coefficients, edge
    )
    other = lax.ppermute(own, "gx", [(i, i ^ 1) for i in range(32)])
    own_z = call(pair_kernel, x_port, name="pair")(own, other)
    k_y, own_z = lax.optimization_barrier((k_flat, own_z))
    from_z = [around(own_z, "gx", 32, 2, s, 1) for s in (1, 2, 3)]
    *y_coefficients, y_lo, y_hi, flat_lo, flat_hi, y_ends = call(
        y_matrix_kernel,
        [
            y_field,
            y_field,
            y_field,
            struct((2 * Y_LEVELS + 1) * SEGMENTS, 8, 128),
            y_field,
            y_field,
            natural,
            natural,
            struct(8, 128),
        ],
        [scratch(runs)],
        name="y_matrix",
    )(k_y)
    table = pltpu.VMEM((4, 7, TILES, 128), F32)
    own_y = call(four_kernel, x_port, [table], name="four")(own_z, *from_z)
    from_y = [around(own_y, "gx", 32, 8, s, 1) for s in (1, 2, 3)]
    turned, port = call(
        y_port_kernel, [runs, struct(8, 128)], [table, table, scratch(flat)], name="y_port"
    )(own_y, *from_y, own_z, *from_z, own, other, u, x_lo, x_hi, t_flat, y_lo, y_hi, y_ends)
    from_gy = [around(port, "gy", 4, 1, s) for s in (1, 2, 3)]
    base = call(
        y_solve_kernel, natural, [scratch(y_field), scratch(runs)], name="y_solve"
    )(turned, *y_coefficients, t_flat)
    updated = call(
        finish_kernel,
        natural,
        [
            pltpu.VMEM((4, 8, 128), F32),
            pltpu.VMEM((128, 128), F32),
            scratch(natural),
            pltpu.SemaphoreType.DMA((BANDS,)),
        ],
        name="finish",
        in_specs=[VMEM] * 7,
        out_specs=HBM,
    )(port, *from_gy, base, flat_lo, flat_hi)
    return updated[None]


def solution(mesh):
    placed = (P(None, "gx", "gy"), P(None, "gx", "gy"))
    return jax.shard_map(
        per_device, mesh=mesh, in_specs=placed, out_specs=P(None, "gx", "gy"), check_vma=False
    )
```

```python
import jax
import jax.numpy as jnp
from jax import lax
from jax.experimental import pallas as pl
from jax.experimental.pallas import tpu as pltpu
from jax.sharding import PartitionSpec as P

ROWS, COLS = 64, 2048
BANDS, TILES = ROWS // 8, COLS // 128
SEGMENTS = 4
Y_STEPS = 128
X_LEVELS, Y_LEVELS = 2, 6
RING = (2, 1, 3)
F32 = jnp.float32
VMEM = pl.BlockSpec(memory_space=pltpu.VMEM)
HBM = pl.BlockSpec(memory_space=pltpu.MemorySpace.HBM)


def struct(*shape):
    return jax.ShapeDtypeStruct(shape, F32)


def scratch(like):
    return pltpu.VMEM(like.shape, like.dtype)


def whole(outs, args):
    return dict(in_specs=[VMEM] * len(args), out_specs=jax.tree.map(lambda _: VMEM, outs))


def call(kernel, outs, buffers=(), flops=2_000_000, name=None, grant=32 << 20, **windows):
    def run(*args):
        return pl.pallas_call(
            kernel,
            out_shape=outs,
            **(windows or whole(outs, args)),
            scratch_shapes=list(buffers),
            compiler_params=pltpu.CompilerParams(vmem_limit_bytes=grant),
            cost_estimate=pl.CostEstimate(flops=flops, bytes_accessed=1 << 20, transcendentals=0),
            name=name,
        )(*args)

    return run


def moved(chain, by, shift):
    out = []
    for s in range(SEGMENTS):
        runs, at = divmod(s + by, SEGMENTS)
        out.append(shift(chain[at], runs) if runs else chain[at])
    return out


def factor(link, n, levels, shift, along, back, gain, sep):
    m = n // SEGMENTS
    near = [link(s * m) for s in range(SEGMENTS)]
    ground = [jnp.ones_like(near[0])] * SEGMENTS
    held = [jnp.ones_like(near[0])] * SEGMENTS
    for step in range(1, m):
        for s in range(SEGMENTS):
            l = s * m + step
            v = link(l)
            r = 1.0 / (near[s] + ground[s] + v)
            t = v * r
            c = near[s] * r
            along[l], back[l], gain[l] = t, c, r
            held[s] = held[s] + ground[s] * c
            near[s] = near[s] * t
            ground[s] = ground[s] * t
            if step < m - 1:
                ground[s] = ground[s] + 1.0
    before = moved(ground, -1, shift)
    own = [held[s] + before[s] for s in range(SEGMENTS)]
    up = near
    down = moved(near, -1, shift)
    for level in range(levels):
        stride = 1 << level
        r = [1.0 / (own[s] + up[s] + down[s]) for s in range(SEGMENTS)]
        r_down, r_up = moved(r, -stride, shift), moved(r, stride, shift)
        own_down, own_up = moved(own, -stride, shift), moved(own, stride, shift)
        down_down, up_up = moved(down, -stride, shift), moved(up, stride, shift)
        for s in range(SEGMENTS):
            a, b = down[s] * r_down[s], up[s] * r_up[s]
            sep[(level * 2) * SEGMENTS + s] = a
            sep[(level * 2 + 1) * SEGMENTS + s] = b
            own[s] = own[s] + a * own_down[s] + b * own_up[s]
            down[s], up[s] = a * down_down[s], b * up_up[s]
    for s in range(SEGMENTS):
        sep[levels * 2 * SEGMENTS + s] = 1.0 / own[s]


def plus(a, b):
    return b if a is None else a if b is None else a + b


def times(a, b):
    return None if a is None else a * b


def solve(source, n, levels, shift, along, back, gain, sep, part, store):
    m = n // SEGMENTS
    total = [source(s * m) for s in range(SEGMENTS)]
    z = [source(s * m + 1) for s in range(SEGMENTS)]
    zero = [[False] * SEGMENTS for _ in range(m)]
    for step in range(1, m):
        for s in range(SEGMENTS):
            l = s * m + step
            zero[step][s] = z[s] is None
            if z[s] is not None:
                part[l] = z[s] * gain[l]
                total[s] = plus(total[s], z[s] * back[l])
                z[s] = z[s] * along[l]
            if step < m - 1:
                z[s] = plus(source(l + 1), z[s])
    shape = jnp.zeros(along.shape[1:], F32)
    z = [shape if v is None else v for v in z]
    before = moved(z, -1, shift)
    total = [plus(total[s], before[s]) for s in range(SEGMENTS)]
    for level in range(levels):
        stride = 1 << level
        lo, hi = moved(total, -stride, shift), moved(total, stride, shift)
        total = [
            total[s]
            + sep[(level * 2) * SEGMENTS + s] * lo[s]
            + sep[(level * 2 + 1) * SEGMENTS + s] * hi[s]
            for s in range(SEGMENTS)
        ]
    value = [total[s] * sep[levels * 2 * SEGMENTS + s] for s in range(SEGMENTS)]
    after = moved(value, 1, shift)
    for s in range(SEGMENTS):
        store(s * m, value[s])
    for step in reversed(range(1, m)):
        for s in range(SEGMENTS):
            l = s * m + step
            known = back[l] * value[s]
            if not zero[step][s]:
                known = known + part[l]
            after[s] = known + along[l] * after[s]
            store(l, after[s])


def x_shift(value, runs):
    return value


def y_shift(value, runs):
    if runs % 2 == 0:
        return pltpu.roll(value, (-(runs // 2)) % 8, 0)
    swapped = pltpu.roll(value, 64, 1)
    late = lax.broadcasted_iota(jnp.int32, value.shape, 1) >= 64
    if runs == 1:
        return jnp.where(late, pltpu.roll(swapped, 7, 0), swapped)
    return jnp.where(late, swapped, pltpu.roll(swapped, 1, 0))


def tile(ref, band, column):
    return ref[8 * band : 8 * band + 8, 128 * column : 128 * column + 128]


def flat_tile(ref, band, column):
    at = (band * TILES + column) * 8
    return ref[at : at + 8, :]


def row(ref, i):
    return ref[pl.ds((i // 8) * (8 * TILES) + i % 8, TILES, stride=8), :]


def edges_kernel(t, k, lo, hi, strips, arrived):
    sides = (pl.ds(0, 128), pl.ds(128 * (TILES - 1), 128))
    copies = [
        pltpu.make_async_copy(ref.at[:, side], strips.at[n], arrived.at[n])
        for n, (side, ref) in enumerate((side, ref) for side in sides for ref in (t, k))
    ]
    for copy in copies:
        copy.start()
    lo[...] = jnp.zeros_like(lo)
    hi[...] = jnp.zeros_like(hi)
    for copy in copies:
        copy.wait()
    lo[0:1, 0:ROWS] = strips[0].T[0:1, :]
    lo[1:2, 0:ROWS] = strips[1].T[0:1, :]
    hi[0:1, 0:ROWS] = strips[2].T[127:128, :]
    hi[1:2, 0:ROWS] = strips[3].T[127:128, :]


def total(terms):
    sums = [None] * 4
    for n, term in enumerate(terms):
        sums[n % 4] = plus(sums[n % 4], term)
    return (sums[0] + sums[1]) + (sums[2] + sums[3])


def x_matrix_kernel(t, k, e, along, back, gain, sep, lo, hi, ends, t_flat, flat, own):
    own[...] = jnp.zeros_like(own)
    for n, (ref, column) in enumerate(((t, 0), (k, 0), (t, TILES - 1), (k, TILES - 1))):
        strip = ref[:, 128 * column : 128 * column + 128].T
        at = 127 if column else 0
        own[n : n + 1, 0:ROWS] = strip[at : at + 1, :]
    lane = lax.broadcasted_iota(jnp.int32, (8, 128), 1)
    for band in range(BANDS):
        ks = [tile(k, band, c) for c in range(TILES)]
        ts = [tile(t, band, c) for c in range(TILES)]
        k_left = [pltpu.roll(v, 127, 1) for v in ks]
        t_left = [pltpu.roll(v, 127, 1) for v in ts]
        flow = []
        for c in range(TILES):
            at = pl.ds((band * TILES + c) * 8, 8)
            flat[at, :] = ks[c]
            t_flat[at, :] = ts[c]
            n = min(c + 1, TILES - 1)
            k_next = jnp.where(lane == 127, k_left[n], k_left[c])
            t_next = jnp.where(lane == 127, t_left[n], t_left[c])
            f = 8000.0 * (ks[c] + k_next) * (t_next - ts[c])
            if c == TILES - 1:
                f = jnp.where(lane == 127, 0.0, f)
            flow.append(f)
        turned = [pltpu.roll(v, 1, 1) for v in flow]
        for c in range(TILES):
            at = pl.ds((band * TILES + c) * 8, 8)
            first = turned[c - 1] if c else jnp.zeros_like(turned[0])
            f_before = jnp.where(lane == 0, first, turned[c])
            e[at, :] = 2.0 * ts[c] + (flow[c] - f_before)

    def link(l):
        if l == ROWS - 1:
            return jnp.zeros((TILES, 128), F32)
        return 1000.0 * (row(flat, l) + row(flat, l + 1))

    factor(link, ROWS, X_LEVELS, x_shift, along, back, gain, sep)
    one = jnp.ones((TILES, 128), F32)

    def at_start(l):
        return one if l == 0 else None

    def at_end(l):
        return one if l == ROWS - 1 else None

    def to(ref):
        def store(l, value):
            ref[l] = value

        return store

    args = (ROWS, X_LEVELS, x_shift, along, back, gain, sep)
    solve(at_start, *args, lo, to(lo))
    solve(at_end, *args, hi, to(hi))
    ends[0] = total(lo[i] * row(e, i) for i in range(ROWS))
    ends[1] = total(hi[i] * row(e, i) for i in range(ROWS))
    ends[2] = lo[0]
    ends[3] = lo[ROWS - 1]
    ends[4] = hi[ROWS - 1]
    ends[5] = row(flat, 0)
    ends[6] = row(flat, ROWS - 1)


def x_port_kernel(ends, lo, hi, own, below, above, port, edge, side):
    at = lax.axis_index("gy")
    side[...] = jnp.zeros_like(side)
    t_lo, k_lo, t_hi, k_hi = (own[n : n + 1, :] for n in range(4))
    before = jnp.where(at == 0, 0.0, below[...])
    after = jnp.where(at == lax.axis_size("gy") - 1, 0.0, above[...])
    side[0:1, :] = -8000.0 * (k_lo + before[1:2, :]) * (t_lo - before[0:1, :])
    side[127:128, :] = 8000.0 * (k_hi + after[1:2, :]) * (after[0:1, :] - t_hi)
    edge[...] = side[...].T[0:ROWS, :]
    lane = lax.broadcasted_iota(jnp.int32, (1, 128), 1)
    for n, response in enumerate((lo, hi)):
        port[n] = ends[n]
        for column, kept in ((0, 0), (TILES - 1, 127)):
            term = edge[...] * response[:, column, :]
            term = jnp.where(lane == kept, jnp.sum(term, axis=0, keepdims=True), 0.0)
            port[n, column : column + 1, :] = port[n, column : column + 1, :] + term
    for n in range(2, 7):
        port[n] = ends[n]


def x_solve_kernel(e, along, back, gain, sep, edge, u, flat):
    lane = lax.broadcasted_iota(jnp.int32, (8, 128), 1)
    flat[...] = e[...]
    for band in range(BANDS):
        part = edge[8 * band : 8 * band + 8, :]
        at = pl.ds(band * TILES * 8, 8)
        flat[at, :] = flat[at, :] + jnp.where(lane == 0, part, 0.0)
        at = pl.ds((band * TILES + TILES - 1) * 8, 8)
        flat[at, :] = flat[at, :] + jnp.where(lane == 127, part, 0.0)

    def store(l, value):
        u[l] = value

    def source(l):
        return row(flat, l)

    solve(source, ROWS, X_LEVELS, x_shift, along, back, gain, sep, u, store)


def take(ref):
    return tuple(ref[n] for n in range(7))


def join(one, two, scale):
    a1, b1, al1, be1, ga1, kf1, kl1 = one
    a2, b2, al2, be2, ga2, kf2, kl2 = two
    rho = 1.0 / (1.0 / (scale * (kl1 + kf2)) + al2 + ga1)
    delta = (a2 - b1) * rho
    return (
        a1 + be1 * delta,
        b2 - be2 * delta,
        al1 - be1 * be1 * rho,
        be1 * be2 * rho,
        ga2 - be2 * be2 * rho,
        kf1,
        kl2,
    )


def past_up(state, port, scale):
    p, q, k = state
    a, b, al, be, ga, kf, kl = port
    w = be / (1.0 / (scale * (k + kf)) + al + q)
    return (b - w * (a - p), ga - w * be, kl)


def past_down(state, port, scale):
    p, q, k = state
    a, b, al, be, ga, kf, kl = port
    w = be / (1.0 / (scale * (k + kl)) + ga + q)
    return (a + w * (p - b), al - w * be, kf)


def choose(condition, new, old):
    return tuple(jnp.where(condition, x, y) for x, y in zip(new, old))


def reach(index, ports, lo, hi, scale):
    count = len(ports)
    for n in range(count - 1):
        lo = choose(n < index, past_up(lo, ports[n], scale), lo)
    for n in reversed(range(1, count)):
        hi = choose(n > index, past_down(hi, ports[n], scale), hi)
    return lo, hi


def flows(port, lo, hi, scale):
    a, b, al, be, ga, kf, kl = port
    d_lo = 1.0 / (scale * (lo[2] + kf)) + al + lo[1]
    d_hi = 1.0 / (scale * (hi[2] + kl)) + ga + hi[1]
    c_lo, c_hi = a - lo[0], hi[0] - b
    inverse = 1.0 / (d_lo * d_hi - be * be)
    return (d_hi * c_lo + be * c_hi) * inverse, (d_lo * c_hi + be * c_lo) * inverse


def place(index, own, received, table):
    table[index] = own[...]
    for s, value in zip(RING, received):
        table[lax.rem(index + 4 - s, 4)] = value[...]


def pair_kernel(own, other, out):
    core = lax.rem(lax.axis_index("gx"), 2)
    mine, theirs = take(own), take(other)
    first = choose(core == 0, mine, theirs)
    second = choose(core == 0, theirs, mine)
    for n, value in enumerate(join(first, second, 1000.0)):
        out[n] = value


def four_kernel(own, r1, r2, r3, out, table):
    z = lax.rem(lax.div(lax.axis_index("gx"), 2), 4)
    place(z, own, (r1, r2, r3), table)
    ports = [take(table.at[j]) for j in range(4)]
    joined = join(join(ports[0], ports[1], 1000.0), join(ports[2], ports[3], 1000.0), 1000.0)
    for n, value in enumerate(joined):
        out[n] = value


def to_runs(blocks, out):
    for p in range(TILES // 2):
        stack = [blocks(band, 2 * p + half) for half in range(2) for band in range(BANDS)]
        out[128 * p : 128 * p + 128, :] = jnp.concatenate(stack, axis=0).T


def cell(ref, l):
    return ref[pl.ds(l, 8, stride=128), :]


def from_runs(turned, store):
    for p in range(TILES // 2):
        block = turned[128 * p : 128 * p + 128, :].T
        for half in range(2):
            for band in range(BANDS):
                at = ROWS * half + 8 * band
                store(band, 2 * p + half, block[at : at + 8, :])


def put(ref):
    def store(band, column, value):
        ref[8 * band : 8 * band + 8, 128 * column : 128 * column + 128] = value

    return store


def y_matrix_kernel(k, along, back, gain, sep, lo, hi, flat_lo, flat_hi, ends, turned):
    to_runs(lambda band, column: flat_tile(k, band, column), turned)
    lane = lax.broadcasted_iota(jnp.int32, (8, 128), 1)
    sublane = lax.broadcasted_iota(jnp.int32, (8, 128), 0)
    very_last = (lane >= 64) & (sublane == 7)
    very_first = (lane < 64) & (sublane == 0)

    def link(l):
        if l == Y_STEPS - 1:
            both = 4000.0 * (cell(turned, l) + y_shift(cell(turned, 0), 1))
            return jnp.where(very_last, 0.0, both)
        return 4000.0 * (cell(turned, l) + cell(turned, l + 1))

    factor(link, Y_STEPS, Y_LEVELS, y_shift, along, back, gain, sep)

    def at_start(l):
        return jnp.where(very_first, 1.0, 0.0) if l == 0 else None

    def at_end(l):
        return jnp.where(very_last, 1.0, 0.0) if l == Y_STEPS - 1 else None

    def to(ref):
        def store(l, value):
            ref[l] = value

        return store

    args = (Y_STEPS, Y_LEVELS, y_shift, along, back, gain, sep)
    solve(at_start, *args, lo, to(lo))
    solve(at_end, *args, hi, to(hi))
    last = Y_STEPS - 1
    ends[...] = jnp.zeros_like(ends)
    ends[0:1, :] = lo[0, 0:1, :]
    ends[1:2, :] = pltpu.roll(lo[last], 64, 1)[7:8, :]
    ends[2:3, :] = pltpu.roll(hi[last], 64, 1)[7:8, :]
    ends[3:4, :] = cell(turned, 0)[0:1, :]
    ends[4:5, :] = pltpu.roll(cell(turned, last), 64, 1)[7:8, :]
    for response, flat in ((lo, flat_lo), (hi, flat_hi)):
        for l in range(Y_STEPS):
            turned[pl.ds(l, 8, stride=128), :] = response[l]
        from_runs(turned, put(flat))


def blend_kernel(u, x_lo, x_hi, y_lo, y_hi, t, source, lo, hi, mixed, known, flat, side):
    for ref, out in ((u, flat), (x_lo, lo), (x_hi, hi)):
        for i in range(ROWS):
            at = pl.ds((i // 8) * (8 * TILES) + i % 8, TILES, stride=8)
            out[at, :] = ref[i]
    for band in range(BANDS):
        sums = [None, None]
        for column in range(TILES):
            at = pl.ds((band * TILES + column) * 8, 8)
            value = flat[at, :] - 2.0 * t[at, :]
            source[at, :] = value
            for n, response in enumerate((y_lo, y_hi)):
                r = tile(response, band, column)
                sums[n] = plus(sums[n], r * value)
                mixed[2 * n, at, :] = r * lo[at, :]
                mixed[2 * n + 1, at, :] = r * hi[at, :]
        for n in range(2):
            side[64 * n + 8 * band : 64 * n + 8 * band + 8, :] = sums[n]
    known[...] = jnp.broadcast_to(jnp.sum(side[...].T, axis=0, keepdims=True), (8, 128))


def y_port_kernel(
    own_y, y1, y2, y3, own_z, z1, z2, z3, own, other, mixed, known, ends,
    port, flow, table_y, table_z, side,
):
    index = lax.axis_index("gx")
    core, z, y = lax.rem(index, 2), lax.rem(lax.div(index, 2), 4), lax.div(index, 8)
    place(y, own_y, (y1, y2, y3), table_y)
    place(z, own_z, (z1, z2, z3), table_z)
    nothing = (jnp.zeros((TILES, 128), F32),) * 3
    scale = 1000.0
    lo, hi = reach(y, [take(table_y.at[j]) for j in range(4)], nothing, nothing, scale)
    lo, hi = reach(z, [take(table_z.at[j]) for j in range(4)], lo, hi, scale)
    mine, theirs = take(own), take(other)
    lo = choose(core == 1, past_up(lo, theirs, scale), lo)
    hi = choose(core == 0, past_down(hi, theirs, scale), hi)
    flow[0], flow[1] = flows(mine, lo, hi, scale)
    sums = [None] * (2 * BANDS)
    for column in range(TILES):
        down, up = across(flow, column)
        for band in range(BANDS):
            at = pl.ds((band * TILES + column) * 8, 8)
            for n in range(2):
                part = up * mixed[2 * n + 1, at, :] - down * mixed[2 * n, at, :]
                sums[BANDS * n + band] = plus(sums[BANDS * n + band], part)
    for n, value in enumerate(sums):
        side[8 * n : 8 * n + 8, :] = value
    both = jnp.sum(side[...].T, axis=0, keepdims=True) + known[0:1, :]
    port[...] = jnp.zeros_like(port)
    port[0:1, :] = both
    port[1:2, :] = pltpu.roll(both, 64, 1)
    port[2:7, :] = ends[0:5, :]


def across(flow, column):
    return tuple(
        jnp.broadcast_to(flow[n, column : column + 1, :], (8, 128)) for n in range(2)
    )


def y_solve_kernel(source, lo, hi, flow, along, back, gain, sep, t, out, d, turned):
    def block(band, column):
        down, up = across(flow, column)
        x = flat_tile(source, band, column)
        return x - down * flat_tile(lo, band, column) + up * flat_tile(hi, band, column)

    to_runs(block, turned)

    def store(l, value):
        d[l] = value

    def cells(l):
        return cell(turned, l)

    solve(cells, Y_STEPS, Y_LEVELS, y_shift, along, back, gain, sep, d, store)
    for l in range(Y_STEPS):
        turned[pl.ds(l, 8, stride=128), :] = d[l]
    keep = put(out)

    def plus_start(band, column, value):
        keep(band, column, value + flat_tile(t, band, column))

    from_runs(turned, plus_start)


def finish_kernel(own, r1, r2, r3, base, y_lo, y_hi, out, table, side, done, sent):
    index = lax.axis_index("gy")
    place(index, own, (r1, r2, r3), table)
    lane = lax.broadcasted_iota(jnp.int32, (1, 128), 1)

    def port_of(ref):
        return tuple(jnp.where(lane < ROWS, ref[n : n + 1, :], 1.0) for n in range(7))

    nothing = (jnp.zeros((1, 128), F32),) * 3
    scale = 4000.0
    lo, hi = reach(index, [port_of(table.at[j]) for j in range(4)], nothing, nothing, scale)
    f_lo, f_hi = flows(port_of(own), lo, hi, scale)
    side[...] = jnp.zeros_like(side)
    side[0:1, :] = f_lo
    side[1:2, :] = f_hi
    upright = side[...].T
    copies = []
    for band in range(BANDS):
        at = slice(8 * band, 8 * band + 8)
        down = jnp.broadcast_to(upright[at, 0:1], (8, 128))
        up = jnp.broadcast_to(upright[at, 1:2], (8, 128))
        keep = put(done)
        for column in range(TILES):
            part = tile(base, band, column)
            part = part - down * tile(y_lo, band, column) + up * tile(y_hi, band, column)
            keep(band, column, part)
        copy = pltpu.make_async_copy(done.at[at, :], out.at[at, :], sent.at[band])
        copy.start()
        copies.append(copy)
    for copy in copies:
        copy.wait()


def around(value, axis, size, stride, step):
    pairs = []
    for i in range(size):
        digit = (i // stride) % 4
        pairs.append((i, i + ((digit + step) % 4 - digit) * stride))
    return lax.ppermute(value, axis, pairs)


def per_device(initial_heat_state, thermal_coefficient):
    t, k = initial_heat_state[0], thermal_coefficient[0]
    own_lo, own_hi = call(
        edges_kernel,
        [struct(8, 128)] * 2,
        [pltpu.VMEM((4, ROWS, 128), F32), pltpu.SemaphoreType.DMA((4,))],
        name="edges",
        grant=56 << 20,
        in_specs=[HBM, HBM],
        out_specs=[VMEM, VMEM],
    )(t, k)
    below = around(own_hi, "gy", 4, 1, 1)
    above = around(own_lo, "gy", 4, 1, 3)
    flat = struct(BANDS * TILES * 8, 128)
    runs = struct(TILES // 2 * 128, 128)
    x_field, y_field, natural = struct(ROWS, TILES, 128), struct(Y_STEPS, 8, 128), struct(ROWS, COLS)
    x_port = struct(7, TILES, 128)
    e, *x_coefficients, x_lo, x_hi, x_ends, t_flat, k_flat, own = call(
        x_matrix_kernel,
        [
            flat,
            x_field,
            x_field,
            x_field,
            struct((2 * X_LEVELS + 1) * SEGMENTS, TILES, 128),
            x_field,
            x_field,
            x_port,
            flat,
            flat,
            struct(8, 128),
        ],
        name="x_matrix",
    )(t, k)
    own, edge = call(
        x_port_kernel,
        [x_port, struct(ROWS, 128)],
        [pltpu.VMEM((128, 128), F32)],
        flops=200_000,
        name="x_port",
    )(x_ends, x_lo, x_hi, own, below, above)
    u = call(x_solve_kernel, x_field, [scratch(flat)], flops=700_000, name="x_solve")(
        e, *x_coefficients, edge
    )
    other = lax.ppermute(own, "gx", [(i, i ^ 1) for i in range(32)])
    own_z = call(pair_kernel, x_port, name="pair")(own, other)
    k_y, own_z = lax.optimization_barrier((k_flat, own_z))
    from_z = [around(own_z, "gx", 32, 2, s) for s in RING]
    *y_coefficients, y_lo, y_hi, flat_lo, flat_hi, y_ends = call(
        y_matrix_kernel,
        [
            y_field,
            y_field,
            y_field,
            struct((2 * Y_LEVELS + 1) * SEGMENTS, 8, 128),
            y_field,
            y_field,
            natural,
            natural,
            struct(8, 128),
        ],
        [scratch(runs)],
        name="y_matrix",
    )(k_y)
    *from_z, y_ends, u = lax.optimization_barrier((*from_z, y_ends, u))
    table = pltpu.VMEM((4, 7, TILES, 128), F32)
    own_y = call(four_kernel, x_port, [table], name="four")(own_z, *from_z)
    from_y = [around(own_y, "gx", 32, 8, s) for s in RING]
    square = pltpu.VMEM((128, 128), F32)
    source, lo_flat, hi_flat, mixed, known = call(
        blend_kernel,
        [flat, flat, flat, struct(4, BANDS * TILES * 8, 128), struct(8, 128)],
        [scratch(flat), square],
        name="blend",
    )(u, x_lo, x_hi, flat_lo, flat_hi, t_flat)
    port, flow = call(
        y_port_kernel,
        [struct(8, 128), struct(2, TILES, 128)],
        [table, table, square],
        name="y_port",
    )(own_y, *from_y, own_z, *from_z, own, other, mixed, known, y_ends)
    from_gy = [around(port, "gy", 4, 1, s) for s in RING]
    base = call(
        y_solve_kernel, natural, [scratch(y_field), scratch(runs)], name="y_solve"
    )(source, lo_flat, hi_flat, flow, *y_coefficients, t_flat)
    updated = call(
        finish_kernel,
        natural,
        [
            pltpu.VMEM((4, 8, 128), F32),
            pltpu.VMEM((128, 128), F32),
            scratch(natural),
            pltpu.SemaphoreType.DMA((BANDS,)),
        ],
        name="finish",
        in_specs=[VMEM] * 7,
        out_specs=HBM,
    )(port, *from_gy, base, flat_lo, flat_hi)
    return updated[None]


def solution(mesh):
    placed = (P(None, "gx", "gy"), P(None, "gx", "gy"))
    return jax.shard_map(
        per_device, mesh=mesh, in_specs=placed, out_specs=P(None, "gx", "gy"), check_vma=False
    )
```

```python
import jax
import jax.numpy as jnp
from jax import lax
from jax.experimental import pallas as pl
from jax.experimental.pallas import tpu as pltpu
from jax.sharding import PartitionSpec as P

ROWS, COLS = 64, 2048
BANDS, TILES = ROWS // 8, COLS // 128
SEGMENTS = 4
Y_STEPS = 128
X_LEVELS, Y_LEVELS = 2, 6
GRANT = (527 << 20) // 10
RING = (2, 1, 3)
F32 = jnp.float32
VMEM = pl.BlockSpec(memory_space=pltpu.VMEM)
HBM = pl.BlockSpec(memory_space=pltpu.MemorySpace.HBM)


def struct(*shape):
    return jax.ShapeDtypeStruct(shape, F32)


def scratch(like):
    return pltpu.VMEM(like.shape, like.dtype)


def whole(outs, args):
    return dict(in_specs=[VMEM] * len(args), out_specs=jax.tree.map(lambda _: VMEM, outs))


def call(kernel, outs, buffers=(), flops=2_000_000, name=None, grant=32 << 20, **windows):
    def run(*args):
        return pl.pallas_call(
            kernel,
            out_shape=outs,
            **(windows or whole(outs, args)),
            scratch_shapes=list(buffers),
            compiler_params=pltpu.CompilerParams(vmem_limit_bytes=grant),
            cost_estimate=pl.CostEstimate(flops=flops, bytes_accessed=1 << 20, transcendentals=0),
            name=name,
        )(*args)

    return run


def moved(chain, by, shift):
    out = []
    for s in range(SEGMENTS):
        runs, at = divmod(s + by, SEGMENTS)
        out.append(shift(chain[at], runs) if runs else chain[at])
    return out


def factor(link, n, levels, shift, along, back, gain, sep):
    m = n // SEGMENTS
    near = [link(s * m) for s in range(SEGMENTS)]
    ground = [jnp.ones_like(near[0])] * SEGMENTS
    held = [jnp.ones_like(near[0])] * SEGMENTS
    for step in range(1, m):
        for s in range(SEGMENTS):
            l = s * m + step
            v = link(l)
            r = 1.0 / (near[s] + ground[s] + v)
            t = v * r
            c = near[s] * r
            along[l], back[l], gain[l] = t, c, r
            held[s] = held[s] + ground[s] * c
            near[s] = near[s] * t
            ground[s] = ground[s] * t
            if step < m - 1:
                ground[s] = ground[s] + 1.0
    before = moved(ground, -1, shift)
    own = [held[s] + before[s] for s in range(SEGMENTS)]
    up = near
    down = moved(near, -1, shift)
    for level in range(levels):
        stride = 1 << level
        r = [1.0 / (own[s] + up[s] + down[s]) for s in range(SEGMENTS)]
        r_down, r_up = moved(r, -stride, shift), moved(r, stride, shift)
        own_down, own_up = moved(own, -stride, shift), moved(own, stride, shift)
        down_down, up_up = moved(down, -stride, shift), moved(up, stride, shift)
        for s in range(SEGMENTS):
            a, b = down[s] * r_down[s], up[s] * r_up[s]
            sep[(level * 2) * SEGMENTS + s] = a
            sep[(level * 2 + 1) * SEGMENTS + s] = b
            own[s] = own[s] + a * own_down[s] + b * own_up[s]
            down[s], up[s] = a * down_down[s], b * up_up[s]
    for s in range(SEGMENTS):
        sep[levels * 2 * SEGMENTS + s] = 1.0 / own[s]


def plus(a, b):
    return b if a is None else a if b is None else a + b


def times(a, b):
    return None if a is None else a * b


def solve(source, n, levels, shift, along, back, gain, sep, part, store):
    m = n // SEGMENTS
    total = [source(s * m) for s in range(SEGMENTS)]
    z = [source(s * m + 1) for s in range(SEGMENTS)]
    zero = [[False] * SEGMENTS for _ in range(m)]
    for step in range(1, m):
        for s in range(SEGMENTS):
            l = s * m + step
            zero[step][s] = z[s] is None
            if z[s] is not None:
                part[l] = z[s] * gain[l]
                total[s] = plus(total[s], z[s] * back[l])
                z[s] = z[s] * along[l]
            if step < m - 1:
                z[s] = plus(source(l + 1), z[s])
    shape = jnp.zeros(along.shape[1:], F32)
    z = [shape if v is None else v for v in z]
    before = moved(z, -1, shift)
    total = [plus(total[s], before[s]) for s in range(SEGMENTS)]
    for level in range(levels):
        stride = 1 << level
        lo, hi = moved(total, -stride, shift), moved(total, stride, shift)
        total = [
            total[s]
            + sep[(level * 2) * SEGMENTS + s] * lo[s]
            + sep[(level * 2 + 1) * SEGMENTS + s] * hi[s]
            for s in range(SEGMENTS)
        ]
    value = [total[s] * sep[levels * 2 * SEGMENTS + s] for s in range(SEGMENTS)]
    after = moved(value, 1, shift)
    for s in range(SEGMENTS):
        store(s * m, value[s])
    for step in reversed(range(1, m)):
        for s in range(SEGMENTS):
            l = s * m + step
            known = back[l] * value[s]
            if not zero[step][s]:
                known = known + part[l]
            after[s] = known + along[l] * after[s]
            store(l, after[s])


def x_shift(value, runs):
    return value


def y_shift(value, runs):
    if runs % 2 == 0:
        return pltpu.roll(value, (-(runs // 2)) % 8, 0)
    swapped = pltpu.roll(value, 64, 1)
    late = lax.broadcasted_iota(jnp.int32, value.shape, 1) >= 64
    if runs == 1:
        return jnp.where(late, pltpu.roll(swapped, 7, 0), swapped)
    return jnp.where(late, swapped, pltpu.roll(swapped, 1, 0))


def tile(ref, band, column):
    return ref[8 * band : 8 * band + 8, 128 * column : 128 * column + 128]


def flat_tile(ref, band, column):
    at = (band * TILES + column) * 8
    return ref[at : at + 8, :]


def row(ref, i):
    return ref[pl.ds((i // 8) * (8 * TILES) + i % 8, TILES, stride=8), :]


def load_kernel(t_far, k_far, t, k, lo, hi, own, arrived):
    copies = []
    for band in range(BANDS):
        at = pl.ds(8 * band, 8)
        for n, (far, near) in enumerate(((t_far, t), (k_far, k))):
            copy = pltpu.make_async_copy(far.at[at, :], near.at[at, :], arrived.at[n, band])
            copy.start()
            copies.append(copy)
    for ref in (lo, hi, own):
        ref[...] = jnp.zeros_like(ref)
    for copy in copies:
        copy.wait()
    for n, (ref, column) in enumerate(((t, 0), (k, 0), (t, TILES - 1), (k, TILES - 1))):
        strip = ref[:, 128 * column : 128 * column + 128].T
        at = 127 if column else 0
        edge = strip[at : at + 1, :]
        own[n : n + 1, 0:ROWS] = edge
        (hi if column else lo)[n % 2 : n % 2 + 1, 0:ROWS] = edge


def total(terms):
    sums = [None] * 4
    for n, term in enumerate(terms):
        sums[n % 4] = plus(sums[n % 4], term)
    return (sums[0] + sums[1]) + (sums[2] + sums[3])


def x_matrix_kernel(t, k, e, along, back, gain, sep, lo, hi, ends, t_flat, flat):
    lane = lax.broadcasted_iota(jnp.int32, (8, 128), 1)
    for band in range(BANDS):
        ks = [tile(k, band, c) for c in range(TILES)]
        ts = [tile(t, band, c) for c in range(TILES)]
        k_left = [pltpu.roll(v, 127, 1) for v in ks]
        t_left = [pltpu.roll(v, 127, 1) for v in ts]
        flow = []
        for c in range(TILES):
            at = pl.ds((band * TILES + c) * 8, 8)
            flat[at, :] = ks[c]
            t_flat[at, :] = ts[c]
            n = min(c + 1, TILES - 1)
            k_next = jnp.where(lane == 127, k_left[n], k_left[c])
            t_next = jnp.where(lane == 127, t_left[n], t_left[c])
            f = 8000.0 * (ks[c] + k_next) * (t_next - ts[c])
            if c == TILES - 1:
                f = jnp.where(lane == 127, 0.0, f)
            flow.append(f)
        turned = [pltpu.roll(v, 1, 1) for v in flow]
        for c in range(TILES):
            at = pl.ds((band * TILES + c) * 8, 8)
            first = turned[c - 1] if c else jnp.zeros_like(turned[0])
            f_before = jnp.where(lane == 0, first, turned[c])
            e[at, :] = 2.0 * ts[c] + (flow[c] - f_before)

    def link(l):
        if l == ROWS - 1:
            return jnp.zeros((TILES, 128), F32)
        return 1000.0 * (row(flat, l) + row(flat, l + 1))

    factor(link, ROWS, X_LEVELS, x_shift, along, back, gain, sep)
    one = jnp.ones((TILES, 128), F32)

    def at_start(l):
        return one if l == 0 else None

    def at_end(l):
        return one if l == ROWS - 1 else None

    def to(ref):
        def store(l, value):
            ref[l] = value

        return store

    args = (ROWS, X_LEVELS, x_shift, along, back, gain, sep)
    solve(at_start, *args, lo, to(lo))
    solve(at_end, *args, hi, to(hi))
    ends[0] = total(lo[i] * row(e, i) for i in range(ROWS))
    ends[1] = total(hi[i] * row(e, i) for i in range(ROWS))
    ends[2] = lo[0]
    ends[3] = lo[ROWS - 1]
    ends[4] = hi[ROWS - 1]
    ends[5] = row(flat, 0)
    ends[6] = row(flat, ROWS - 1)


def x_port_kernel(ends, lo, hi, own, below, above, port, edge, side):
    at = lax.axis_index("gy")
    side[...] = jnp.zeros_like(side)
    t_lo, k_lo, t_hi, k_hi = (own[n : n + 1, :] for n in range(4))
    before = jnp.where(at == 0, 0.0, below[...])
    after = jnp.where(at == lax.axis_size("gy") - 1, 0.0, above[...])
    side[0:1, :] = -8000.0 * (k_lo + before[1:2, :]) * (t_lo - before[0:1, :])
    side[127:128, :] = 8000.0 * (k_hi + after[1:2, :]) * (after[0:1, :] - t_hi)
    edge[...] = side[...].T[0:ROWS, :]
    lane = lax.broadcasted_iota(jnp.int32, (1, 128), 1)
    for n, response in enumerate((lo, hi)):
        port[n] = ends[n]
        for column, kept in ((0, 0), (TILES - 1, 127)):
            term = edge[...] * response[:, column, :]
            term = jnp.where(lane == kept, jnp.sum(term, axis=0, keepdims=True), 0.0)
            port[n, column : column + 1, :] = port[n, column : column + 1, :] + term
    for n in range(2, 7):
        port[n] = ends[n]


def x_solve_kernel(e, along, back, gain, sep, edge, u, flat):
    lane = lax.broadcasted_iota(jnp.int32, (8, 128), 1)
    flat[...] = e[...]
    for band in range(BANDS):
        part = edge[8 * band : 8 * band + 8, :]
        at = pl.ds(band * TILES * 8, 8)
        flat[at, :] = flat[at, :] + jnp.where(lane == 0, part, 0.0)
        at = pl.ds((band * TILES + TILES - 1) * 8, 8)
        flat[at, :] = flat[at, :] + jnp.where(lane == 127, part, 0.0)

    def store(l, value):
        u[l] = value

    def source(l):
        return row(flat, l)

    solve(source, ROWS, X_LEVELS, x_shift, along, back, gain, sep, u, store)


def take(ref):
    return tuple(ref[n] for n in range(7))


def join(one, two, scale):
    a1, b1, al1, be1, ga1, kf1, kl1 = one
    a2, b2, al2, be2, ga2, kf2, kl2 = two
    rho = 1.0 / (1.0 / (scale * (kl1 + kf2)) + al2 + ga1)
    delta = (a2 - b1) * rho
    return (
        a1 + be1 * delta,
        b2 - be2 * delta,
        al1 - be1 * be1 * rho,
        be1 * be2 * rho,
        ga2 - be2 * be2 * rho,
        kf1,
        kl2,
    )


def past_up(state, port, scale):
    p, q, k = state
    a, b, al, be, ga, kf, kl = port
    w = be / (1.0 / (scale * (k + kf)) + al + q)
    return (b - w * (a - p), ga - w * be, kl)


def past_down(state, port, scale):
    p, q, k = state
    a, b, al, be, ga, kf, kl = port
    w = be / (1.0 / (scale * (k + kl)) + ga + q)
    return (a + w * (p - b), al - w * be, kf)


def choose(condition, new, old):
    return tuple(jnp.where(condition, x, y) for x, y in zip(new, old))


def reach(index, ports, lo, hi, scale):
    count = len(ports)
    for n in range(count - 1):
        lo = choose(n < index, past_up(lo, ports[n], scale), lo)
    for n in reversed(range(1, count)):
        hi = choose(n > index, past_down(hi, ports[n], scale), hi)
    return lo, hi


def flows(port, lo, hi, scale):
    a, b, al, be, ga, kf, kl = port
    d_lo = 1.0 / (scale * (lo[2] + kf)) + al + lo[1]
    d_hi = 1.0 / (scale * (hi[2] + kl)) + ga + hi[1]
    c_lo, c_hi = a - lo[0], hi[0] - b
    inverse = 1.0 / (d_lo * d_hi - be * be)
    return (d_hi * c_lo + be * c_hi) * inverse, (d_lo * c_hi + be * c_lo) * inverse


def place(index, own, received, table):
    table[index] = own[...]
    for s, value in zip(RING, received):
        table[lax.rem(index + 4 - s, 4)] = value[...]


def pair_kernel(own, other, out):
    core = lax.rem(lax.axis_index("gx"), 2)
    mine, theirs = take(own), take(other)
    first = choose(core == 0, mine, theirs)
    second = choose(core == 0, theirs, mine)
    for n, value in enumerate(join(first, second, 1000.0)):
        out[n] = value


def four_kernel(own, r1, r2, r3, out, table):
    z = lax.rem(lax.div(lax.axis_index("gx"), 2), 4)
    place(z, own, (r1, r2, r3), table)
    ports = [take(table.at[j]) for j in range(4)]
    joined = join(join(ports[0], ports[1], 1000.0), join(ports[2], ports[3], 1000.0), 1000.0)
    for n, value in enumerate(joined):
        out[n] = value


def to_runs(blocks, out):
    for p in range(TILES // 2):
        stack = [blocks(band, 2 * p + half) for half in range(2) for band in range(BANDS)]
        out[128 * p : 128 * p + 128, :] = jnp.concatenate(stack, axis=0).T


def cell(ref, l):
    return ref[pl.ds(l, 8, stride=128), :]


def from_runs(turned, store):
    for p in range(TILES // 2):
        block = turned[128 * p : 128 * p + 128, :].T
        for half in range(2):
            for band in range(BANDS):
                at = ROWS * half + 8 * band
                store(band, 2 * p + half, block[at : at + 8, :])


def put(ref):
    def store(band, column, value):
        ref[8 * band : 8 * band + 8, 128 * column : 128 * column + 128] = value

    return store


def y_matrix_kernel(k, along, back, gain, sep, lo, hi, ends, turned):
    to_runs(lambda band, column: tile(k, band, column), turned)
    lane = lax.broadcasted_iota(jnp.int32, (8, 128), 1)
    sublane = lax.broadcasted_iota(jnp.int32, (8, 128), 0)
    very_last = (lane >= 64) & (sublane == 7)
    very_first = (lane < 64) & (sublane == 0)

    def link(l):
        if l == Y_STEPS - 1:
            both = 4000.0 * (cell(turned, l) + y_shift(cell(turned, 0), 1))
            return jnp.where(very_last, 0.0, both)
        return 4000.0 * (cell(turned, l) + cell(turned, l + 1))

    factor(link, Y_STEPS, Y_LEVELS, y_shift, along, back, gain, sep)

    def at_start(l):
        return jnp.where(very_first, 1.0, 0.0) if l == 0 else None

    def at_end(l):
        return jnp.where(very_last, 1.0, 0.0) if l == Y_STEPS - 1 else None

    def to(ref):
        def store(l, value):
            ref[l] = value

        return store

    args = (Y_STEPS, Y_LEVELS, y_shift, along, back, gain, sep)
    solve(at_start, *args, lo, to(lo))
    solve(at_end, *args, hi, to(hi))
    last = Y_STEPS - 1
    ends[...] = jnp.zeros_like(ends)
    ends[0:1, :] = lo[0, 0:1, :]
    ends[1:2, :] = pltpu.roll(lo[last], 64, 1)[7:8, :]
    ends[2:3, :] = pltpu.roll(hi[last], 64, 1)[7:8, :]
    ends[3:4, :] = cell(turned, 0)[0:1, :]
    ends[4:5, :] = pltpu.roll(cell(turned, last), 64, 1)[7:8, :]


def upright_kernel(lo, hi, flat_lo, flat_hi, turned):
    for n, (response, flat) in enumerate(((lo, flat_lo), (hi, flat_hi))):
        for l in range(Y_STEPS):
            turned[n, pl.ds(l, 8, stride=128), :] = response[l]
        from_runs(turned.at[n], put(flat))


def blend_kernel(u, x_lo, x_hi, y_lo, y_hi, t, source, lo, hi, mixed, known, flat, side):
    for ref, out in ((u, flat), (x_lo, lo), (x_hi, hi)):
        for i in range(ROWS):
            at = pl.ds((i // 8) * (8 * TILES) + i % 8, TILES, stride=8)
            out[at, :] = ref[i]
    for band in range(BANDS):
        sums = [None, None]
        for column in range(TILES):
            at = pl.ds((band * TILES + column) * 8, 8)
            value = flat[at, :] - 2.0 * t[at, :]
            source[at, :] = value
            for n, response in enumerate((y_lo, y_hi)):
                r = tile(response, band, column)
                sums[n] = plus(sums[n], r * value)
                mixed[2 * n, at, :] = r * lo[at, :]
                mixed[2 * n + 1, at, :] = r * hi[at, :]
        for n in range(2):
            side[64 * n + 8 * band : 64 * n + 8 * band + 8, :] = sums[n]
    known[...] = jnp.broadcast_to(jnp.sum(side[...].T, axis=0, keepdims=True), (8, 128))


def y_port_kernel(
    own_y, y1, y2, y3, own_z, z1, z2, z3, own, other, mixed, known, ends,
    port, flow, table_y, table_z, side,
):
    index = lax.axis_index("gx")
    core, z, y = lax.rem(index, 2), lax.rem(lax.div(index, 2), 4), lax.div(index, 8)
    place(y, own_y, (y1, y2, y3), table_y)
    place(z, own_z, (z1, z2, z3), table_z)
    nothing = (jnp.zeros((TILES, 128), F32),) * 3
    scale = 1000.0
    lo, hi = reach(y, [take(table_y.at[j]) for j in range(4)], nothing, nothing, scale)
    lo, hi = reach(z, [take(table_z.at[j]) for j in range(4)], lo, hi, scale)
    mine, theirs = take(own), take(other)
    lo = choose(core == 1, past_up(lo, theirs, scale), lo)
    hi = choose(core == 0, past_down(hi, theirs, scale), hi)
    flow[0], flow[1] = flows(mine, lo, hi, scale)
    sums = [None] * (2 * BANDS)
    for column in range(TILES):
        down, up = across(flow, column)
        for band in range(BANDS):
            at = pl.ds((band * TILES + column) * 8, 8)
            for n in range(2):
                part = up * mixed[2 * n + 1, at, :] - down * mixed[2 * n, at, :]
                sums[BANDS * n + band] = plus(sums[BANDS * n + band], part)
    for n, value in enumerate(sums):
        side[8 * n : 8 * n + 8, :] = value
    both = jnp.sum(side[...].T, axis=0, keepdims=True) + known[0:1, :]
    port[...] = jnp.zeros_like(port)
    port[0:1, :] = both
    port[1:2, :] = pltpu.roll(both, 64, 1)
    port[2:7, :] = ends[0:5, :]


def across(flow, column):
    return tuple(
        jnp.broadcast_to(flow[n, column : column + 1, :], (8, 128)) for n in range(2)
    )


def y_solve_kernel(source, lo, hi, flow, along, back, gain, sep, t, out, d, turned):
    def block(band, column):
        down, up = across(flow, column)
        x = flat_tile(source, band, column)
        return x - down * flat_tile(lo, band, column) + up * flat_tile(hi, band, column)

    to_runs(block, turned)

    def store(l, value):
        d[l] = value

    def cells(l):
        return cell(turned, l)

    solve(cells, Y_STEPS, Y_LEVELS, y_shift, along, back, gain, sep, d, store)
    for l in range(Y_STEPS):
        turned[pl.ds(l, 8, stride=128), :] = d[l]
    keep = put(out)

    def plus_start(band, column, value):
        keep(band, column, value + flat_tile(t, band, column))

    from_runs(turned, plus_start)


def finish_kernel(own, r1, r2, r3, base, y_lo, y_hi, out, table, side, done, sent):
    index = lax.axis_index("gy")
    place(index, own, (r1, r2, r3), table)
    lane = lax.broadcasted_iota(jnp.int32, (1, 128), 1)

    def port_of(ref):
        return tuple(jnp.where(lane < ROWS, ref[n : n + 1, :], 1.0) for n in range(7))

    nothing = (jnp.zeros((1, 128), F32),) * 3
    scale = 4000.0
    lo, hi = reach(index, [port_of(table.at[j]) for j in range(4)], nothing, nothing, scale)
    f_lo, f_hi = flows(port_of(own), lo, hi, scale)
    side[...] = jnp.zeros_like(side)
    side[0:1, :] = f_lo
    side[1:2, :] = f_hi
    upright = side[...].T
    copies = []
    for band in range(BANDS):
        at = slice(8 * band, 8 * band + 8)
        down = jnp.broadcast_to(upright[at, 0:1], (8, 128))
        up = jnp.broadcast_to(upright[at, 1:2], (8, 128))
        keep = put(done)
        for column in range(TILES):
            part = tile(base, band, column)
            part = part - down * tile(y_lo, band, column) + up * tile(y_hi, band, column)
            keep(band, column, part)
        copy = pltpu.make_async_copy(done.at[at, :], out.at[at, :], sent.at[band])
        copy.start()
        copies.append(copy)
    for copy in copies:
        copy.wait()


def around(value, axis, size, stride, step):
    pairs = []
    for i in range(size):
        digit = (i // stride) % 4
        pairs.append((i, i + ((digit + step) % 4 - digit) * stride))
    return lax.ppermute(value, axis, pairs)


def per_device(initial_heat_state, thermal_coefficient):
    t, k = initial_heat_state[0], thermal_coefficient[0]
    natural = struct(ROWS, COLS)
    t, k, own_lo, own_hi, own_edges = call(
        load_kernel,
        [natural, natural] + [struct(8, 128)] * 3,
        [pltpu.SemaphoreType.DMA((2, BANDS))],
        name="load",
        grant=GRANT,
        in_specs=[HBM, HBM],
        out_specs=[VMEM] * 5,
    )(t, k)
    below = around(own_hi, "gy", 4, 1, 1)
    above = around(own_lo, "gy", 4, 1, 3)
    flat = struct(BANDS * TILES * 8, 128)
    runs = struct(TILES // 2 * 128, 128)
    x_field, y_field = struct(ROWS, TILES, 128), struct(Y_STEPS, 8, 128)
    x_port = struct(7, TILES, 128)
    e, *x_coefficients, x_lo, x_hi, x_ends, t_flat, k_flat = call(
        x_matrix_kernel,
        [
            flat,
            x_field,
            x_field,
            x_field,
            struct((2 * X_LEVELS + 1) * SEGMENTS, TILES, 128),
            x_field,
            x_field,
            x_port,
            flat,
            flat,
        ],
        name="x_matrix",
    )(t, k)
    *y_coefficients, y_lo, y_hi, y_ends = call(
        y_matrix_kernel,
        [
            y_field,
            y_field,
            y_field,
            struct((2 * Y_LEVELS + 1) * SEGMENTS, 8, 128),
            y_field,
            y_field,
            struct(8, 128),
        ],
        [scratch(runs)],
        name="y_matrix",
    )(k)
    below, above, y_lo = lax.optimization_barrier((below, above, y_lo))
    own, edge = call(
        x_port_kernel,
        [x_port, struct(ROWS, 128)],
        [pltpu.VMEM((128, 128), F32)],
        flops=200_000,
        name="x_port",
    )(x_ends, x_lo, x_hi, own_edges, below, above)
    u = call(x_solve_kernel, x_field, [scratch(flat)], flops=700_000, name="x_solve")(
        e, *x_coefficients, edge
    )
    other = lax.ppermute(own, "gx", [(i, i ^ 1) for i in range(32)])
    other, u = lax.optimization_barrier((other, u))
    own_z = call(pair_kernel, x_port, name="pair")(own, other)
    from_z = [around(own_z, "gx", 32, 2, s) for s in RING]
    flat_lo, flat_hi = call(
        upright_kernel,
        [natural, natural],
        [pltpu.VMEM((2, TILES // 2 * 128, 128), F32)],
        name="upright",
    )(y_lo, y_hi)
    *from_z, flat_lo = lax.optimization_barrier((*from_z, flat_lo))
    table = pltpu.VMEM((4, 7, TILES, 128), F32)
    own_y = call(four_kernel, x_port, [table], name="four")(own_z, *from_z)
    from_y = [around(own_y, "gx", 32, 8, s) for s in RING]
    square = pltpu.VMEM((128, 128), F32)
    source, lo_flat, hi_flat, mixed, known = call(
        blend_kernel,
        [flat, flat, flat, struct(4, BANDS * TILES * 8, 128), struct(8, 128)],
        [scratch(flat), square],
        name="blend",
    )(u, x_lo, x_hi, flat_lo, flat_hi, t_flat)
    port, flow = call(
        y_port_kernel,
        [struct(8, 128), struct(2, TILES, 128)],
        [table, table, square],
        name="y_port",
    )(own_y, *from_y, own_z, *from_z, own, other, mixed, known, y_ends)
    from_gy = [around(port, "gy", 4, 1, s) for s in RING]
    base = call(
        y_solve_kernel, natural, [scratch(y_field), scratch(runs)], name="y_solve"
    )(source, lo_flat, hi_flat, flow, *y_coefficients, t_flat)
    updated = call(
        finish_kernel,
        natural,
        [
            pltpu.VMEM((4, 8, 128), F32),
            pltpu.VMEM((128, 128), F32),
            scratch(natural),
            pltpu.SemaphoreType.DMA((BANDS,)),
        ],
        name="finish",
        in_specs=[VMEM] * 7,
        out_specs=HBM,
    )(port, *from_gy, base, flat_lo, flat_hi)
    return updated[None]


def solution(mesh):
    placed = (P(None, "gx", "gy"), P(None, "gx", "gy"))
    return jax.shard_map(
        per_device, mesh=mesh, in_specs=placed, out_specs=P(None, "gx", "gy"), check_vma=False
    )
```

```python
import jax
import jax.numpy as jnp
from jax import lax
from jax.experimental import pallas as pl
from jax.experimental.pallas import tpu as pltpu
from jax.sharding import PartitionSpec as P

ROWS, COLS = 64, 2048
BANDS, TILES = ROWS // 8, COLS // 128
SEGMENTS = 4
Y_STEPS = 128
X_LEVELS, Y_LEVELS = 2, 6
GRANT = (527 << 20) // 10
RING = (2, 1, 3)
F32 = jnp.float32
VMEM = pl.BlockSpec(memory_space=pltpu.VMEM)
HBM = pl.BlockSpec(memory_space=pltpu.MemorySpace.HBM)


def struct(*shape):
    return jax.ShapeDtypeStruct(shape, F32)


def scratch(like):
    return pltpu.VMEM(like.shape, like.dtype)


def whole(outs, args):
    return dict(in_specs=[VMEM] * len(args), out_specs=jax.tree.map(lambda _: VMEM, outs))


def call(kernel, outs, buffers=(), flops=2_000_000, name=None, grant=32 << 20, **windows):
    def run(*args):
        return pl.pallas_call(
            kernel,
            out_shape=outs,
            **(windows or whole(outs, args)),
            scratch_shapes=list(buffers),
            compiler_params=pltpu.CompilerParams(vmem_limit_bytes=grant),
            cost_estimate=pl.CostEstimate(flops=flops, bytes_accessed=1 << 20, transcendentals=0),
            name=name,
        )(*args)

    return run


def moved(chain, by, shift):
    out = []
    for s in range(SEGMENTS):
        runs, at = divmod(s + by, SEGMENTS)
        out.append(shift(chain[at], runs) if runs else chain[at])
    return out


def factor(link, n, levels, shift, along, back, gain, sep):
    m = n // SEGMENTS
    near = [link(s * m) for s in range(SEGMENTS)]
    ground = [jnp.ones_like(near[0])] * SEGMENTS
    held = [jnp.ones_like(near[0])] * SEGMENTS
    for step in range(1, m):
        for s in range(SEGMENTS):
            l = s * m + step
            v = link(l)
            r = 1.0 / (near[s] + ground[s] + v)
            t = v * r
            c = near[s] * r
            along[l], back[l], gain[l] = t, c, r
            held[s] = held[s] + ground[s] * c
            near[s] = near[s] * t
            ground[s] = ground[s] * t
            if step < m - 1:
                ground[s] = ground[s] + 1.0
    before = moved(ground, -1, shift)
    own = [held[s] + before[s] for s in range(SEGMENTS)]
    up = near
    down = moved(near, -1, shift)
    for level in range(levels):
        stride = 1 << level
        r = [1.0 / (own[s] + up[s] + down[s]) for s in range(SEGMENTS)]
        r_down, r_up = moved(r, -stride, shift), moved(r, stride, shift)
        own_down, own_up = moved(own, -stride, shift), moved(own, stride, shift)
        down_down, up_up = moved(down, -stride, shift), moved(up, stride, shift)
        for s in range(SEGMENTS):
            a, b = down[s] * r_down[s], up[s] * r_up[s]
            sep[(level * 2) * SEGMENTS + s] = a
            sep[(level * 2 + 1) * SEGMENTS + s] = b
            own[s] = own[s] + a * own_down[s] + b * own_up[s]
            down[s], up[s] = a * down_down[s], b * up_up[s]
    for s in range(SEGMENTS):
        sep[levels * 2 * SEGMENTS + s] = 1.0 / own[s]


def plus(a, b):
    return b if a is None else a if b is None else a + b


def times(a, b):
    return None if a is None else a * b


def solve(source, n, levels, shift, along, back, gain, sep, part, store):
    m = n // SEGMENTS
    total = [source(s * m) for s in range(SEGMENTS)]
    z = [source(s * m + 1) for s in range(SEGMENTS)]
    zero = [[False] * SEGMENTS for _ in range(m)]
    for step in range(1, m):
        for s in range(SEGMENTS):
            l = s * m + step
            zero[step][s] = z[s] is None
            if z[s] is not None:
                part[l] = z[s] * gain[l]
                total[s] = plus(total[s], z[s] * back[l])
                z[s] = z[s] * along[l]
            if step < m - 1:
                z[s] = plus(source(l + 1), z[s])
    shape = jnp.zeros(along.shape[1:], F32)
    z = [shape if v is None else v for v in z]
    before = moved(z, -1, shift)
    total = [plus(total[s], before[s]) for s in range(SEGMENTS)]
    for level in range(levels):
        stride = 1 << level
        lo, hi = moved(total, -stride, shift), moved(total, stride, shift)
        total = [
            total[s]
            + sep[(level * 2) * SEGMENTS + s] * lo[s]
            + sep[(level * 2 + 1) * SEGMENTS + s] * hi[s]
            for s in range(SEGMENTS)
        ]
    value = [total[s] * sep[levels * 2 * SEGMENTS + s] for s in range(SEGMENTS)]
    after = moved(value, 1, shift)
    for s in range(SEGMENTS):
        store(s * m, value[s])
    for step in reversed(range(1, m)):
        for s in range(SEGMENTS):
            l = s * m + step
            known = back[l] * value[s]
            if not zero[step][s]:
                known = known + part[l]
            after[s] = known + along[l] * after[s]
            store(l, after[s])


def x_shift(value, runs):
    return value


def y_shift(value, runs):
    if runs % 2 == 0:
        return pltpu.roll(value, (-(runs // 2)) % 8, 0)
    swapped = pltpu.roll(value, 64, 1)
    late = lax.broadcasted_iota(jnp.int32, value.shape, 1) >= 64
    if runs == 1:
        return jnp.where(late, pltpu.roll(swapped, 7, 0), swapped)
    return jnp.where(late, swapped, pltpu.roll(swapped, 1, 0))


def tile(ref, band, column):
    return ref[8 * band : 8 * band + 8, 128 * column : 128 * column + 128]


def flat_tile(ref, band, column):
    at = (band * TILES + column) * 8
    return ref[at : at + 8, :]


def row(ref, i):
    return ref[pl.ds((i // 8) * (8 * TILES) + i % 8, TILES, stride=8), :]


def load_kernel(t_far, k_far, t, k, lo, hi, own, arrived):
    copies = []
    for band in range(BANDS):
        at = pl.ds(8 * band, 8)
        for n, (far, near) in enumerate(((t_far, t), (k_far, k))):
            copy = pltpu.make_async_copy(far.at[at, :], near.at[at, :], arrived.at[n, band])
            copy.start()
            copies.append(copy)
    for ref in (lo, hi, own):
        ref[...] = jnp.zeros_like(ref)
    for copy in copies:
        copy.wait()
    for n, (ref, column) in enumerate(((t, 0), (k, 0), (t, TILES - 1), (k, TILES - 1))):
        strip = ref[:, 128 * column : 128 * column + 128].T
        at = 127 if column else 0
        edge = strip[at : at + 1, :]
        own[n : n + 1, 0:ROWS] = edge
        (hi if column else lo)[n % 2 : n % 2 + 1, 0:ROWS] = edge


def total(terms):
    sums = [None] * 4
    for n, term in enumerate(terms):
        sums[n % 4] = plus(sums[n % 4], term)
    return (sums[0] + sums[1]) + (sums[2] + sums[3])


def x_matrix_kernel(t, k, e, along, back, gain, sep, lo, hi, ends, t_flat, flat):
    lane = lax.broadcasted_iota(jnp.int32, (8, 128), 1)
    for band in range(BANDS):
        ks = [tile(k, band, c) for c in range(TILES)]
        ts = [tile(t, band, c) for c in range(TILES)]
        k_left = [pltpu.roll(v, 127, 1) for v in ks]
        t_left = [pltpu.roll(v, 127, 1) for v in ts]
        flow = []
        for c in range(TILES):
            at = pl.ds((band * TILES + c) * 8, 8)
            flat[at, :] = ks[c]
            t_flat[at, :] = ts[c]
            n = min(c + 1, TILES - 1)
            k_next = jnp.where(lane == 127, k_left[n], k_left[c])
            t_next = jnp.where(lane == 127, t_left[n], t_left[c])
            f = 8000.0 * (ks[c] + k_next) * (t_next - ts[c])
            if c == TILES - 1:
                f = jnp.where(lane == 127, 0.0, f)
            flow.append(f)
        turned = [pltpu.roll(v, 1, 1) for v in flow]
        for c in range(TILES):
            at = pl.ds((band * TILES + c) * 8, 8)
            first = turned[c - 1] if c else jnp.zeros_like(turned[0])
            f_before = jnp.where(lane == 0, first, turned[c])
            e[at, :] = 2.0 * ts[c] + (flow[c] - f_before)

    def link(l):
        if l == ROWS - 1:
            return jnp.zeros((TILES, 128), F32)
        return 1000.0 * (row(flat, l) + row(flat, l + 1))

    factor(link, ROWS, X_LEVELS, x_shift, along, back, gain, sep)
    one = jnp.ones((TILES, 128), F32)

    def at_start(l):
        return one if l == 0 else None

    def at_end(l):
        return one if l == ROWS - 1 else None

    def to(ref):
        def store(l, value):
            ref[l] = value

        return store

    args = (ROWS, X_LEVELS, x_shift, along, back, gain, sep)
    solve(at_start, *args, lo, to(lo))
    solve(at_end, *args, hi, to(hi))
    ends[0] = total(lo[i] * row(e, i) for i in range(ROWS))
    ends[1] = total(hi[i] * row(e, i) for i in range(ROWS))
    ends[2] = lo[0]
    ends[3] = lo[ROWS - 1]
    ends[4] = hi[ROWS - 1]
    ends[5] = row(flat, 0)
    ends[6] = row(flat, ROWS - 1)


def x_port_kernel(ends, lo, hi, own, below, above, keep, give, edge, port, side):
    at = lax.axis_index("gy")
    side[...] = jnp.zeros_like(side)
    t_lo, k_lo, t_hi, k_hi = (own[n : n + 1, :] for n in range(4))
    before = jnp.where(at == 0, 0.0, below[...])
    after = jnp.where(at == lax.axis_size("gy") - 1, 0.0, above[...])
    side[0:1, :] = -8000.0 * (k_lo + before[1:2, :]) * (t_lo - before[0:1, :])
    side[127:128, :] = 8000.0 * (k_hi + after[1:2, :]) * (after[0:1, :] - t_hi)
    edge[...] = side[...].T[0:ROWS, :]
    lane = lax.broadcasted_iota(jnp.int32, (1, 128), 1)
    for n, response in enumerate((lo, hi)):
        port[n] = ends[n]
        for column, kept in ((0, 0), (TILES - 1, 127)):
            term = edge[...] * response[:, column, :]
            term = jnp.where(lane == kept, jnp.sum(term, axis=0, keepdims=True), 0.0)
            port[n, column : column + 1, :] = port[n, column : column + 1, :] + term
    core = lax.rem(lax.axis_index("gx"), 2)
    for n in range(7):
        ref = port if n < 2 else ends
        keep[n], give[n] = choose(core == 0, halves(ref, n), halves(ref, n)[::-1])


def halves(ref, n):
    return ref[n, : TILES // 2, :], ref[n, TILES // 2 :, :]


def x_solve_kernel(e, along, back, gain, sep, edge, u, flat):
    lane = lax.broadcasted_iota(jnp.int32, (8, 128), 1)
    flat[...] = e[...]
    for band in range(BANDS):
        part = edge[8 * band : 8 * band + 8, :]
        at = pl.ds(band * TILES * 8, 8)
        flat[at, :] = flat[at, :] + jnp.where(lane == 0, part, 0.0)
        at = pl.ds((band * TILES + TILES - 1) * 8, 8)
        flat[at, :] = flat[at, :] + jnp.where(lane == 127, part, 0.0)

    def store(l, value):
        u[l] = value

    def source(l):
        return row(flat, l)

    solve(source, ROWS, X_LEVELS, x_shift, along, back, gain, sep, u, store)


def take(ref):
    return tuple(ref[n] for n in range(7))


def join(one, two, scale):
    a1, b1, al1, be1, ga1, kf1, kl1 = one
    a2, b2, al2, be2, ga2, kf2, kl2 = two
    rho = 1.0 / (1.0 / (scale * (kl1 + kf2)) + al2 + ga1)
    delta = (a2 - b1) * rho
    return (
        a1 + be1 * delta,
        b2 - be2 * delta,
        al1 - be1 * be1 * rho,
        be1 * be2 * rho,
        ga2 - be2 * be2 * rho,
        kf1,
        kl2,
    )


def past_up(state, port, scale):
    p, q, k = state
    a, b, al, be, ga, kf, kl = port
    w = be / (1.0 / (scale * (k + kf)) + al + q)
    return (b - w * (a - p), ga - w * be, kl)


def past_down(state, port, scale):
    p, q, k = state
    a, b, al, be, ga, kf, kl = port
    w = be / (1.0 / (scale * (k + kl)) + ga + q)
    return (a + w * (p - b), al - w * be, kf)


def choose(condition, new, old):
    return tuple(jnp.where(condition, x, y) for x, y in zip(new, old))


def reach(index, ports, lo, hi, scale):
    count = len(ports)
    for n in range(count - 1):
        lo = choose(n < index, past_up(lo, ports[n], scale), lo)
    for n in reversed(range(1, count)):
        hi = choose(n > index, past_down(hi, ports[n], scale), hi)
    return lo, hi


def flows(port, lo, hi, scale):
    a, b, al, be, ga, kf, kl = port
    d_lo = 1.0 / (scale * (lo[2] + kf)) + al + lo[1]
    d_hi = 1.0 / (scale * (hi[2] + kl)) + ga + hi[1]
    c_lo, c_hi = a - lo[0], hi[0] - b
    inverse = 1.0 / (d_lo * d_hi - be * be)
    return (d_hi * c_lo + be * c_hi) * inverse, (d_lo * c_hi + be * c_lo) * inverse


def place(index, own, received, table):
    table[index] = own[...]
    for s, value in zip(RING, received):
        table[lax.rem(index + 4 - s, 4)] = value[...]


def pair_kernel(own, other, out):
    core = lax.rem(lax.axis_index("gx"), 2)
    mine, theirs = take(own), take(other)
    first = choose(core == 0, mine, theirs)
    second = choose(core == 0, theirs, mine)
    for n, value in enumerate(join(first, second, 1000.0)):
        out[n] = value


def four_kernel(own, r1, r2, r3, out, table):
    z = lax.rem(lax.div(lax.axis_index("gx"), 2), 4)
    place(z, own, (r1, r2, r3), table)
    ports = [take(table.at[j]) for j in range(4)]
    joined = join(join(ports[0], ports[1], 1000.0), join(ports[2], ports[3], 1000.0), 1000.0)
    for n, value in enumerate(joined):
        out[n] = value


def to_runs(blocks, out):
    for p in range(TILES // 2):
        stack = [blocks(band, 2 * p + half) for half in range(2) for band in range(BANDS)]
        out[128 * p : 128 * p + 128, :] = jnp.concatenate(stack, axis=0).T


def cell(ref, l):
    return ref[pl.ds(l, 8, stride=128), :]


def from_runs(turned, store):
    for p in range(TILES // 2):
        block = turned[128 * p : 128 * p + 128, :].T
        for half in range(2):
            for band in range(BANDS):
                at = ROWS * half + 8 * band
                store(band, 2 * p + half, block[at : at + 8, :])


def put(ref):
    def store(band, column, value):
        ref[8 * band : 8 * band + 8, 128 * column : 128 * column + 128] = value

    return store


def y_matrix_kernel(k, along, back, gain, sep, lo, hi, ends, turned):
    to_runs(lambda band, column: tile(k, band, column), turned)
    lane = lax.broadcasted_iota(jnp.int32, (8, 128), 1)
    sublane = lax.broadcasted_iota(jnp.int32, (8, 128), 0)
    very_last = (lane >= 64) & (sublane == 7)
    very_first = (lane < 64) & (sublane == 0)

    def link(l):
        if l == Y_STEPS - 1:
            both = 4000.0 * (cell(turned, l) + y_shift(cell(turned, 0), 1))
            return jnp.where(very_last, 0.0, both)
        return 4000.0 * (cell(turned, l) + cell(turned, l + 1))

    factor(link, Y_STEPS, Y_LEVELS, y_shift, along, back, gain, sep)

    def at_start(l):
        return jnp.where(very_first, 1.0, 0.0) if l == 0 else None

    def at_end(l):
        return jnp.where(very_last, 1.0, 0.0) if l == Y_STEPS - 1 else None

    def to(ref):
        def store(l, value):
            ref[l] = value

        return store

    args = (Y_STEPS, Y_LEVELS, y_shift, along, back, gain, sep)
    solve(at_start, *args, lo, to(lo))
    solve(at_end, *args, hi, to(hi))
    last = Y_STEPS - 1
    ends[...] = jnp.zeros_like(ends)
    ends[0:1, :] = lo[0, 0:1, :]
    ends[1:2, :] = pltpu.roll(lo[last], 64, 1)[7:8, :]
    ends[2:3, :] = pltpu.roll(hi[last], 64, 1)[7:8, :]
    ends[3:4, :] = cell(turned, 0)[0:1, :]
    ends[4:5, :] = pltpu.roll(cell(turned, last), 64, 1)[7:8, :]


def upright_kernel(lo, hi, flat_lo, flat_hi, turned):
    for n, (response, flat) in enumerate(((lo, flat_lo), (hi, flat_hi))):
        for l in range(Y_STEPS):
            turned[n, pl.ds(l, 8, stride=128), :] = response[l]
        from_runs(turned.at[n], put(flat))


def blend_kernel(u, x_lo, x_hi, y_lo, y_hi, t, source, lo, hi, mixed, known, flat, side):
    for ref, out in ((u, flat), (x_lo, lo), (x_hi, hi)):
        for i in range(ROWS):
            at = pl.ds((i // 8) * (8 * TILES) + i % 8, TILES, stride=8)
            out[at, :] = ref[i]
    for band in range(BANDS):
        sums = [None, None]
        for column in range(TILES):
            at = pl.ds((band * TILES + column) * 8, 8)
            value = flat[at, :] - 2.0 * t[at, :]
            source[at, :] = value
            for n, response in enumerate((y_lo, y_hi)):
                r = tile(response, band, column)
                sums[n] = plus(sums[n], r * value)
                mixed[2 * n, at, :] = r * lo[at, :]
                mixed[2 * n + 1, at, :] = r * hi[at, :]
        for n in range(2):
            side[64 * n + 8 * band : 64 * n + 8 * band + 8, :] = sums[n]
    known[...] = jnp.broadcast_to(jnp.sum(side[...].T, axis=0, keepdims=True), (8, 128))


def through_kernel(
    own_y, y1, y2, y3, own_z, z1, z2, z3, own, other, keep, give, table_y, table_z
):
    index = lax.axis_index("gx")
    core, z, y = lax.rem(index, 2), lax.rem(lax.div(index, 2), 4), lax.div(index, 8)
    place(y, own_y, (y1, y2, y3), table_y)
    place(z, own_z, (z1, z2, z3), table_z)
    nothing = (jnp.zeros(own.shape[1:], F32),) * 3
    scale = 1000.0
    lo, hi = reach(y, [take(table_y.at[j]) for j in range(4)], nothing, nothing, scale)
    lo, hi = reach(z, [take(table_z.at[j]) for j in range(4)], lo, hi, scale)
    mine, theirs = take(own), take(other)
    first = choose(core == 0, mine, theirs)
    second = choose(core == 0, theirs, mine)
    at_first = flows(first, lo, past_down(hi, second, scale), scale)
    at_second = flows(second, past_up(lo, first, scale), hi, scale)
    keep[0], keep[1] = choose(core == 0, at_first, at_second)
    give[0], give[1] = choose(core == 0, at_second, at_first)


def y_port_kernel(keep, got, mixed, known, ends, port, flow, side):
    core = lax.rem(lax.axis_index("gx"), 2)
    for n in range(2):
        flow[n, : TILES // 2, :] = jnp.where(core == 0, keep[n], got[n])
        flow[n, TILES // 2 :, :] = jnp.where(core == 0, got[n], keep[n])
    sums = [None] * (2 * BANDS)
    for column in range(TILES):
        down, up = across(flow, column)
        for band in range(BANDS):
            at = pl.ds((band * TILES + column) * 8, 8)
            for n in range(2):
                part = up * mixed[2 * n + 1, at, :] - down * mixed[2 * n, at, :]
                sums[BANDS * n + band] = plus(sums[BANDS * n + band], part)
    for n, value in enumerate(sums):
        side[8 * n : 8 * n + 8, :] = value
    both = jnp.sum(side[...].T, axis=0, keepdims=True) + known[0:1, :]
    port[...] = jnp.zeros_like(port)
    port[0:1, :] = both
    port[1:2, :] = pltpu.roll(both, 64, 1)
    port[2:7, :] = ends[0:5, :]


def across(flow, column):
    return tuple(
        jnp.broadcast_to(flow[n, column : column + 1, :], (8, 128)) for n in range(2)
    )


def y_solve_kernel(source, lo, hi, flow, along, back, gain, sep, t, out, d, turned):
    def block(band, column):
        down, up = across(flow, column)
        x = flat_tile(source, band, column)
        return x - down * flat_tile(lo, band, column) + up * flat_tile(hi, band, column)

    to_runs(block, turned)

    def store(l, value):
        d[l] = value

    def cells(l):
        return cell(turned, l)

    solve(cells, Y_STEPS, Y_LEVELS, y_shift, along, back, gain, sep, d, store)
    for l in range(Y_STEPS):
        turned[pl.ds(l, 8, stride=128), :] = d[l]
    keep = put(out)

    def plus_start(band, column, value):
        keep(band, column, value + flat_tile(t, band, column))

    from_runs(turned, plus_start)


def finish_kernel(own, r1, r2, r3, base, y_lo, y_hi, out, table, side, done, sent):
    index = lax.axis_index("gy")
    place(index, own, (r1, r2, r3), table)
    lane = lax.broadcasted_iota(jnp.int32, (1, 128), 1)

    def port_of(ref):
        return tuple(jnp.where(lane < ROWS, ref[n : n + 1, :], 1.0) for n in range(7))

    nothing = (jnp.zeros((1, 128), F32),) * 3
    scale = 4000.0
    lo, hi = reach(index, [port_of(table.at[j]) for j in range(4)], nothing, nothing, scale)
    f_lo, f_hi = flows(port_of(own), lo, hi, scale)
    side[...] = jnp.zeros_like(side)
    side[0:1, :] = f_lo
    side[1:2, :] = f_hi
    upright = side[...].T
    copies = []
    for band in range(BANDS):
        at = slice(8 * band, 8 * band + 8)
        down = jnp.broadcast_to(upright[at, 0:1], (8, 128))
        up = jnp.broadcast_to(upright[at, 1:2], (8, 128))
        keep = put(done)
        for column in range(TILES):
            part = tile(base, band, column)
            part = part - down * tile(y_lo, band, column) + up * tile(y_hi, band, column)
            keep(band, column, part)
        copy = pltpu.make_async_copy(done.at[at, :], out.at[at, :], sent.at[band])
        copy.start()
        copies.append(copy)
    for copy in copies:
        copy.wait()


def around(value, axis, size, stride, step):
    pairs = []
    for i in range(size):
        digit = (i // stride) % 4
        pairs.append((i, i + ((digit + step) % 4 - digit) * stride))
    return lax.ppermute(value, axis, pairs)


def per_device(initial_heat_state, thermal_coefficient):
    t, k = initial_heat_state[0], thermal_coefficient[0]
    natural = struct(ROWS, COLS)
    t, k, own_lo, own_hi, own_edges = call(
        load_kernel,
        [natural, natural] + [struct(8, 128)] * 3,
        [pltpu.SemaphoreType.DMA((2, BANDS))],
        name="load",
        grant=GRANT,
        in_specs=[HBM, HBM],
        out_specs=[VMEM] * 5,
    )(t, k)
    below = around(own_hi, "gy", 4, 1, 1)
    above = around(own_lo, "gy", 4, 1, 3)
    flat = struct(BANDS * TILES * 8, 128)
    runs = struct(TILES // 2 * 128, 128)
    x_field, y_field = struct(ROWS, TILES, 128), struct(Y_STEPS, 8, 128)
    x_port = struct(7, TILES, 128)
    e, *x_coefficients, x_lo, x_hi, x_ends, t_flat, k_flat = call(
        x_matrix_kernel,
        [
            flat,
            x_field,
            x_field,
            x_field,
            struct((2 * X_LEVELS + 1) * SEGMENTS, TILES, 128),
            x_field,
            x_field,
            x_port,
            flat,
            flat,
        ],
        name="x_matrix",
    )(t, k)
    *y_coefficients, y_lo, y_hi, y_ends = call(
        y_matrix_kernel,
        [
            y_field,
            y_field,
            y_field,
            struct((2 * Y_LEVELS + 1) * SEGMENTS, 8, 128),
            y_field,
            y_field,
            struct(8, 128),
        ],
        [scratch(runs)],
        name="y_matrix",
    )(k)
    below, above, y_lo = lax.optimization_barrier((below, above, y_lo))
    half = struct(7, TILES // 2, 128)
    own, give, edge = call(
        x_port_kernel,
        [half, half, struct(ROWS, 128)],
        [scratch(x_port), pltpu.VMEM((128, 128), F32)],
        flops=200_000,
        name="x_port",
    )(x_ends, x_lo, x_hi, own_edges, below, above)
    u = call(x_solve_kernel, x_field, [scratch(flat)], flops=700_000, name="x_solve")(
        e, *x_coefficients, edge
    )
    pairs = [(i, i ^ 1) for i in range(32)]
    other = lax.ppermute(give, "gx", pairs)
    other, u = lax.optimization_barrier((other, u))
    own_z = call(pair_kernel, half, name="pair")(own, other)
    from_z = [around(own_z, "gx", 32, 2, s) for s in RING]
    flat_lo, flat_hi = call(
        upright_kernel,
        [natural, natural],
        [pltpu.VMEM((2, TILES // 2 * 128, 128), F32)],
        name="upright",
    )(y_lo, y_hi)
    *from_z, flat_lo = lax.optimization_barrier((*from_z, flat_lo))
    table = pltpu.VMEM((4, 7, TILES // 2, 128), F32)
    own_y = call(four_kernel, half, [table], name="four")(own_z, *from_z)
    from_y = [around(own_y, "gx", 32, 8, s) for s in RING]
    square = pltpu.VMEM((128, 128), F32)
    source, lo_flat, hi_flat, mixed, known = call(
        blend_kernel,
        [flat, flat, flat, struct(4, BANDS * TILES * 8, 128), struct(8, 128)],
        [scratch(flat), square],
        name="blend",
    )(u, x_lo, x_hi, flat_lo, flat_hi, t_flat)
    some = struct(2, TILES // 2, 128)
    keep, give = call(through_kernel, [some, some], [table, table], name="through")(
        own_y, *from_y, own_z, *from_z, own, other
    )
    got = lax.ppermute(give, "gx", pairs)
    port, flow = call(
        y_port_kernel, [struct(8, 128), struct(2, TILES, 128)], [square], name="y_port"
    )(keep, got, mixed, known, y_ends)
    from_gy = [around(port, "gy", 4, 1, s) for s in RING]
    base = call(
        y_solve_kernel, natural, [scratch(y_field), scratch(runs)], name="y_solve"
    )(source, lo_flat, hi_flat, flow, *y_coefficients, t_flat)
    updated = call(
        finish_kernel,
        natural,
        [
            pltpu.VMEM((4, 8, 128), F32),
            pltpu.VMEM((128, 128), F32),
            scratch(natural),
            pltpu.SemaphoreType.DMA((BANDS,)),
        ],
        name="finish",
        in_specs=[VMEM] * 7,
        out_specs=HBM,
    )(port, *from_gy, base, flat_lo, flat_hi)
    return updated[None]


def solution(mesh):
    placed = (P(None, "gx", "gy"), P(None, "gx", "gy"))
    return jax.shard_map(
        per_device, mesh=mesh, in_specs=placed, out_specs=P(None, "gx", "gy"), check_vma=False
    )
```

```python
import jax
import jax.numpy as jnp
from jax import lax
from jax.experimental import pallas as pl
from jax.experimental.pallas import tpu as pltpu
from jax.sharding import PartitionSpec as P

ROWS, COLS = 64, 2048
BANDS, TILES = ROWS // 8, COLS // 128
SEGMENTS = 4
Y_STEPS = 128
X_LEVELS, Y_LEVELS = 2, 6
GRANT = (527 << 20) // 10
RING = (3, 1, 2)
F32 = jnp.float32
VMEM = pl.BlockSpec(memory_space=pltpu.VMEM)
HBM = pl.BlockSpec(memory_space=pltpu.MemorySpace.HBM)


def struct(*shape):
    return jax.ShapeDtypeStruct(shape, F32)


def scratch(like):
    return pltpu.VMEM(like.shape, like.dtype)


def whole(outs, args):
    return dict(in_specs=[VMEM] * len(args), out_specs=jax.tree.map(lambda _: VMEM, outs))


def call(kernel, outs, buffers=(), flops=2_000_000, name=None, grant=32 << 20, **windows):
    def run(*args):
        return pl.pallas_call(
            kernel,
            out_shape=outs,
            **(windows or whole(outs, args)),
            scratch_shapes=list(buffers),
            compiler_params=pltpu.CompilerParams(vmem_limit_bytes=grant),
            cost_estimate=pl.CostEstimate(flops=flops, bytes_accessed=1 << 20, transcendentals=0),
            name=name,
        )(*args)

    return run


def moved(chain, by, shift):
    out = []
    for s in range(SEGMENTS):
        runs, at = divmod(s + by, SEGMENTS)
        out.append(shift(chain[at], runs) if runs else chain[at])
    return out


def factor(link, n, levels, shift, along, back, gain, sep):
    m = n // SEGMENTS
    near = [link(s * m) for s in range(SEGMENTS)]
    ground = [jnp.ones_like(near[0])] * SEGMENTS
    held = [jnp.ones_like(near[0])] * SEGMENTS
    for step in range(1, m):
        for s in range(SEGMENTS):
            l = s * m + step
            v = link(l)
            r = 1.0 / (near[s] + ground[s] + v)
            t = v * r
            c = near[s] * r
            along[l], back[l], gain[l] = t, c, r
            held[s] = held[s] + ground[s] * c
            near[s] = near[s] * t
            ground[s] = ground[s] * t
            if step < m - 1:
                ground[s] = ground[s] + 1.0
    before = moved(ground, -1, shift)
    own = [held[s] + before[s] for s in range(SEGMENTS)]
    up = near
    down = moved(near, -1, shift)
    for level in range(levels):
        stride = 1 << level
        r = [1.0 / (own[s] + up[s] + down[s]) for s in range(SEGMENTS)]
        r_down, r_up = moved(r, -stride, shift), moved(r, stride, shift)
        own_down, own_up = moved(own, -stride, shift), moved(own, stride, shift)
        down_down, up_up = moved(down, -stride, shift), moved(up, stride, shift)
        for s in range(SEGMENTS):
            a, b = down[s] * r_down[s], up[s] * r_up[s]
            sep[(level * 2) * SEGMENTS + s] = a
            sep[(level * 2 + 1) * SEGMENTS + s] = b
            own[s] = own[s] + a * own_down[s] + b * own_up[s]
            down[s], up[s] = a * down_down[s], b * up_up[s]
    for s in range(SEGMENTS):
        sep[levels * 2 * SEGMENTS + s] = 1.0 / own[s]


def plus(a, b):
    return b if a is None else a if b is None else a + b


def times(a, b):
    return None if a is None else a * b


def solve(source, n, levels, shift, along, back, gain, sep, part, store):
    m = n // SEGMENTS
    total = [source(s * m) for s in range(SEGMENTS)]
    z = [source(s * m + 1) for s in range(SEGMENTS)]
    zero = [[False] * SEGMENTS for _ in range(m)]
    for step in range(1, m):
        for s in range(SEGMENTS):
            l = s * m + step
            zero[step][s] = z[s] is None
            if z[s] is not None:
                part[l] = z[s] * gain[l]
                total[s] = plus(total[s], z[s] * back[l])
                z[s] = z[s] * along[l]
            if step < m - 1:
                z[s] = plus(source(l + 1), z[s])
    shape = jnp.zeros(along.shape[1:], F32)
    z = [shape if v is None else v for v in z]
    before = moved(z, -1, shift)
    total = [plus(total[s], before[s]) for s in range(SEGMENTS)]
    for level in range(levels):
        stride = 1 << level
        lo, hi = moved(total, -stride, shift), moved(total, stride, shift)
        total = [
            total[s]
            + sep[(level * 2) * SEGMENTS + s] * lo[s]
            + sep[(level * 2 + 1) * SEGMENTS + s] * hi[s]
            for s in range(SEGMENTS)
        ]
    value = [total[s] * sep[levels * 2 * SEGMENTS + s] for s in range(SEGMENTS)]
    after = moved(value, 1, shift)
    for s in range(SEGMENTS):
        store(s * m, value[s])
    for step in reversed(range(1, m)):
        for s in range(SEGMENTS):
            l = s * m + step
            known = back[l] * value[s]
            if not zero[step][s]:
                known = known + part[l]
            after[s] = known + along[l] * after[s]
            store(l, after[s])


def x_shift(value, runs):
    return value


def y_shift(value, runs):
    if runs % 2 == 0:
        return pltpu.roll(value, (-(runs // 2)) % 8, 0)
    swapped = pltpu.roll(value, 64, 1)
    late = lax.broadcasted_iota(jnp.int32, value.shape, 1) >= 64
    if runs == 1:
        return jnp.where(late, pltpu.roll(swapped, 7, 0), swapped)
    return jnp.where(late, swapped, pltpu.roll(swapped, 1, 0))


def tile(ref, band, column):
    return ref[8 * band : 8 * band + 8, 128 * column : 128 * column + 128]


def flat_tile(ref, band, column):
    at = (band * TILES + column) * 8
    return ref[at : at + 8, :]


def row(ref, i):
    return ref[pl.ds((i // 8) * (8 * TILES) + i % 8, TILES, stride=8), :]


def load_kernel(t_far, k_far, t, k, lo, hi, own, arrived):
    copies = []
    for band in range(BANDS):
        at = pl.ds(8 * band, 8)
        for n, (far, near) in enumerate(((t_far, t), (k_far, k))):
            copy = pltpu.make_async_copy(far.at[at, :], near.at[at, :], arrived.at[n, band])
            copy.start()
            copies.append(copy)
    for ref in (lo, hi, own):
        ref[...] = jnp.zeros_like(ref)
    for copy in copies:
        copy.wait()
    for n, (ref, column) in enumerate(((t, 0), (k, 0), (t, TILES - 1), (k, TILES - 1))):
        strip = ref[:, 128 * column : 128 * column + 128].T
        at = 127 if column else 0
        edge = strip[at : at + 1, :]
        own[n : n + 1, 0:ROWS] = edge
        (hi if column else lo)[n % 2 : n % 2 + 1, 0:ROWS] = edge


def total(terms):
    sums = [None] * 4
    for n, term in enumerate(terms):
        sums[n % 4] = plus(sums[n % 4], term)
    return (sums[0] + sums[1]) + (sums[2] + sums[3])


def x_matrix_kernel(t, k, e, along, back, gain, sep, lo, hi, ends, t_flat, flat):
    lane = lax.broadcasted_iota(jnp.int32, (8, 128), 1)
    for band in range(BANDS):
        ks = [tile(k, band, c) for c in range(TILES)]
        ts = [tile(t, band, c) for c in range(TILES)]
        k_left = [pltpu.roll(v, 127, 1) for v in ks]
        t_left = [pltpu.roll(v, 127, 1) for v in ts]
        flow = []
        for c in range(TILES):
            at = pl.ds((band * TILES + c) * 8, 8)
            flat[at, :] = ks[c]
            t_flat[at, :] = ts[c]
            n = min(c + 1, TILES - 1)
            k_next = jnp.where(lane == 127, k_left[n], k_left[c])
            t_next = jnp.where(lane == 127, t_left[n], t_left[c])
            f = 8000.0 * (ks[c] + k_next) * (t_next - ts[c])
            if c == TILES - 1:
                f = jnp.where(lane == 127, 0.0, f)
            flow.append(f)
        turned = [pltpu.roll(v, 1, 1) for v in flow]
        for c in range(TILES):
            at = pl.ds((band * TILES + c) * 8, 8)
            first = turned[c - 1] if c else jnp.zeros_like(turned[0])
            f_before = jnp.where(lane == 0, first, turned[c])
            e[at, :] = 2.0 * ts[c] + (flow[c] - f_before)

    def link(l):
        if l == ROWS - 1:
            return jnp.zeros((TILES, 128), F32)
        return 1000.0 * (row(flat, l) + row(flat, l + 1))

    factor(link, ROWS, X_LEVELS, x_shift, along, back, gain, sep)
    one = jnp.ones((TILES, 128), F32)

    def at_start(l):
        return one if l == 0 else None

    def at_end(l):
        return one if l == ROWS - 1 else None

    def to(ref):
        def store(l, value):
            ref[l] = value

        return store

    args = (ROWS, X_LEVELS, x_shift, along, back, gain, sep)
    solve(at_start, *args, lo, to(lo))
    solve(at_end, *args, hi, to(hi))
    ends[0] = total(lo[i] * row(e, i) for i in range(ROWS))
    ends[1] = total(hi[i] * row(e, i) for i in range(ROWS))
    ends[2] = lo[0]
    ends[3] = lo[ROWS - 1]
    ends[4] = hi[ROWS - 1]
    ends[5] = row(flat, 0)
    ends[6] = row(flat, ROWS - 1)


def x_port_kernel(ends, lo, hi, own, below, above, keep, give, edge, port, side):
    at = lax.axis_index("gy")
    side[...] = jnp.zeros_like(side)
    t_lo, k_lo, t_hi, k_hi = (own[n : n + 1, :] for n in range(4))
    before = jnp.where(at == 0, 0.0, below[...])
    after = jnp.where(at == lax.axis_size("gy") - 1, 0.0, above[...])
    side[0:1, :] = -8000.0 * (k_lo + before[1:2, :]) * (t_lo - before[0:1, :])
    side[127:128, :] = 8000.0 * (k_hi + after[1:2, :]) * (after[0:1, :] - t_hi)
    edge[...] = side[...].T[0:ROWS, :]
    lane = lax.broadcasted_iota(jnp.int32, (1, 128), 1)
    for n, response in enumerate((lo, hi)):
        port[n] = ends[n]
        for column, kept in ((0, 0), (TILES - 1, 127)):
            term = edge[...] * response[:, column, :]
            term = jnp.where(lane == kept, jnp.sum(term, axis=0, keepdims=True), 0.0)
            port[n, column : column + 1, :] = port[n, column : column + 1, :] + term
    core = lax.rem(lax.axis_index("gx"), 2)
    for n in range(7):
        ref = port if n < 2 else ends
        keep[n], give[n] = choose(core == 0, halves(ref, n), halves(ref, n)[::-1])


def halves(ref, n):
    return ref[n, : TILES // 2, :], ref[n, TILES // 2 :, :]


def x_solve_kernel(e, along, back, gain, sep, edge, u, flat):
    lane = lax.broadcasted_iota(jnp.int32, (8, 128), 1)
    flat[...] = e[...]
    for band in range(BANDS):
        part = edge[8 * band : 8 * band + 8, :]
        at = pl.ds(band * TILES * 8, 8)
        flat[at, :] = flat[at, :] + jnp.where(lane == 0, part, 0.0)
        at = pl.ds((band * TILES + TILES - 1) * 8, 8)
        flat[at, :] = flat[at, :] + jnp.where(lane == 127, part, 0.0)

    def store(l, value):
        u[l] = value

    def source(l):
        return row(flat, l)

    solve(source, ROWS, X_LEVELS, x_shift, along, back, gain, sep, u, store)


def take(ref):
    return tuple(ref[n] for n in range(7))


def join(one, two, scale):
    a1, b1, al1, be1, ga1, kf1, kl1 = one
    a2, b2, al2, be2, ga2, kf2, kl2 = two
    rho = 1.0 / (1.0 / (scale * (kl1 + kf2)) + al2 + ga1)
    delta = (a2 - b1) * rho
    return (
        a1 + be1 * delta,
        b2 - be2 * delta,
        al1 - be1 * be1 * rho,
        be1 * be2 * rho,
        ga2 - be2 * be2 * rho,
        kf1,
        kl2,
    )


def past_up(state, port, scale):
    p, q, k = state
    a, b, al, be, ga, kf, kl = port
    w = be / (1.0 / (scale * (k + kf)) + al + q)
    return (b - w * (a - p), ga - w * be, kl)


def past_down(state, port, scale):
    p, q, k = state
    a, b, al, be, ga, kf, kl = port
    w = be / (1.0 / (scale * (k + kl)) + ga + q)
    return (a + w * (p - b), al - w * be, kf)


def choose(condition, new, old):
    return tuple(jnp.where(condition, x, y) for x, y in zip(new, old))


def reach(index, ports, lo, hi, scale):
    count = len(ports)
    for n in range(count - 1):
        lo = choose(n < index, past_up(lo, ports[n], scale), lo)
    for n in reversed(range(1, count)):
        hi = choose(n > index, past_down(hi, ports[n], scale), hi)
    return lo, hi


def flows(port, lo, hi, scale):
    a, b, al, be, ga, kf, kl = port
    d_lo = 1.0 / (scale * (lo[2] + kf)) + al + lo[1]
    d_hi = 1.0 / (scale * (hi[2] + kl)) + ga + hi[1]
    c_lo, c_hi = a - lo[0], hi[0] - b
    inverse = 1.0 / (d_lo * d_hi - be * be)
    return (d_hi * c_lo + be * c_hi) * inverse, (d_lo * c_hi + be * c_lo) * inverse


def place(index, own, received, table):
    table[index] = own[...]
    for s, value in zip(RING, received):
        table[lax.rem(index + 4 - s, 4)] = value[...]


def pair_kernel(own, other, out):
    core = lax.rem(lax.axis_index("gx"), 2)
    mine, theirs = take(own), take(other)
    first = choose(core == 0, mine, theirs)
    second = choose(core == 0, theirs, mine)
    for n, value in enumerate(join(first, second, 1000.0)):
        out[n] = value


def four_kernel(own, r1, r2, r3, out, table):
    z = lax.rem(lax.div(lax.axis_index("gx"), 2), 4)
    place(z, own, (r1, r2, r3), table)
    ports = [take(table.at[j]) for j in range(4)]
    joined = join(join(ports[0], ports[1], 1000.0), join(ports[2], ports[3], 1000.0), 1000.0)
    for n, value in enumerate(joined):
        out[n] = value


def to_runs(blocks, out):
    for p in range(TILES // 2):
        stack = [blocks(band, 2 * p + half) for half in range(2) for band in range(BANDS)]
        out[128 * p : 128 * p + 128, :] = jnp.concatenate(stack, axis=0).T


def cell(ref, l):
    return ref[pl.ds(l, 8, stride=128), :]


def from_runs(turned, store):
    for p in range(TILES // 2):
        block = turned[128 * p : 128 * p + 128, :].T
        for half in range(2):
            for band in range(BANDS):
                at = ROWS * half + 8 * band
                store(band, 2 * p + half, block[at : at + 8, :])


def put(ref):
    def store(band, column, value):
        ref[8 * band : 8 * band + 8, 128 * column : 128 * column + 128] = value

    return store


def y_matrix_kernel(k, along, back, gain, sep, lo, hi, ends, turned):
    to_runs(lambda band, column: tile(k, band, column), turned)
    lane = lax.broadcasted_iota(jnp.int32, (8, 128), 1)
    sublane = lax.broadcasted_iota(jnp.int32, (8, 128), 0)
    very_last = (lane >= 64) & (sublane == 7)
    very_first = (lane < 64) & (sublane == 0)

    def link(l):
        if l == Y_STEPS - 1:
            both = 4000.0 * (cell(turned, l) + y_shift(cell(turned, 0), 1))
            return jnp.where(very_last, 0.0, both)
        return 4000.0 * (cell(turned, l) + cell(turned, l + 1))

    factor(link, Y_STEPS, Y_LEVELS, y_shift, along, back, gain, sep)

    def at_start(l):
        return jnp.where(very_first, 1.0, 0.0) if l == 0 else None

    def at_end(l):
        return jnp.where(very_last, 1.0, 0.0) if l == Y_STEPS - 1 else None

    def to(ref):
        def store(l, value):
            ref[l] = value

        return store

    args = (Y_STEPS, Y_LEVELS, y_shift, along, back, gain, sep)
    solve(at_start, *args, lo, to(lo))
    solve(at_end, *args, hi, to(hi))
    last = Y_STEPS - 1
    ends[...] = jnp.zeros_like(ends)
    ends[0:1, :] = lo[0, 0:1, :]
    ends[1:2, :] = pltpu.roll(lo[last], 64, 1)[7:8, :]
    ends[2:3, :] = pltpu.roll(hi[last], 64, 1)[7:8, :]
    ends[3:4, :] = cell(turned, 0)[0:1, :]
    ends[4:5, :] = pltpu.roll(cell(turned, last), 64, 1)[7:8, :]


def upright_kernel(lo, hi, flat_lo, flat_hi, turned):
    for n, (response, flat) in enumerate(((lo, flat_lo), (hi, flat_hi))):
        for l in range(Y_STEPS):
            turned[n, pl.ds(l, 8, stride=128), :] = response[l]
        from_runs(turned.at[n], put(flat))


def blend_kernel(u, x_lo, x_hi, y_lo, y_hi, t, source, lo, hi, mixed, known, flat, side):
    for ref, out in ((u, flat), (x_lo, lo), (x_hi, hi)):
        for i in range(ROWS):
            at = pl.ds((i // 8) * (8 * TILES) + i % 8, TILES, stride=8)
            out[at, :] = ref[i]
    for band in range(BANDS):
        sums = [None, None]
        for column in range(TILES):
            at = pl.ds((band * TILES + column) * 8, 8)
            value = flat[at, :] - 2.0 * t[at, :]
            source[at, :] = value
            for n, response in enumerate((y_lo, y_hi)):
                r = tile(response, band, column)
                sums[n] = plus(sums[n], r * value)
                mixed[2 * n, at, :] = r * lo[at, :]
                mixed[2 * n + 1, at, :] = r * hi[at, :]
        for n in range(2):
            side[64 * n + 8 * band : 64 * n + 8 * band + 8, :] = sums[n]
    known[...] = jnp.broadcast_to(jnp.sum(side[...].T, axis=0, keepdims=True), (8, 128))


def through_kernel(
    own_y, y1, y2, y3, own_z, z1, z2, z3, own, other, keep, give, table_y, table_z
):
    index = lax.axis_index("gx")
    core, z, y = lax.rem(index, 2), lax.rem(lax.div(index, 2), 4), lax.div(index, 8)
    place(y, own_y, (y1, y2, y3), table_y)
    place(z, own_z, (z1, z2, z3), table_z)
    nothing = (jnp.zeros(own.shape[1:], F32),) * 3
    scale = 1000.0
    lo, hi = reach(y, [take(table_y.at[j]) for j in range(4)], nothing, nothing, scale)
    lo, hi = reach(z, [take(table_z.at[j]) for j in range(4)], lo, hi, scale)
    mine, theirs = take(own), take(other)
    first = choose(core == 0, mine, theirs)
    second = choose(core == 0, theirs, mine)
    at_first = flows(first, lo, past_down(hi, second, scale), scale)
    at_second = flows(second, past_up(lo, first, scale), hi, scale)
    keep[0], keep[1] = choose(core == 0, at_first, at_second)
    give[0], give[1] = choose(core == 0, at_second, at_first)


def y_port_kernel(keep, got, mixed, known, ends, port, flow, side):
    core = lax.rem(lax.axis_index("gx"), 2)
    for n in range(2):
        flow[n, : TILES // 2, :] = jnp.where(core == 0, keep[n], got[n])
        flow[n, TILES // 2 :, :] = jnp.where(core == 0, got[n], keep[n])
    sums = [None] * (2 * BANDS)
    for column in range(TILES):
        down, up = across(flow, column)
        for band in range(BANDS):
            at = pl.ds((band * TILES + column) * 8, 8)
            for n in range(2):
                part = up * mixed[2 * n + 1, at, :] - down * mixed[2 * n, at, :]
                sums[BANDS * n + band] = plus(sums[BANDS * n + band], part)
    for n, value in enumerate(sums):
        side[8 * n : 8 * n + 8, :] = value
    both = jnp.sum(side[...].T, axis=0, keepdims=True) + known[0:1, :]
    port[...] = jnp.zeros_like(port)
    port[0:1, :] = both
    port[1:2, :] = pltpu.roll(both, 64, 1)
    port[2:7, :] = ends[0:5, :]


def across(flow, column):
    return tuple(
        jnp.broadcast_to(flow[n, column : column + 1, :], (8, 128)) for n in range(2)
    )


def y_solve_kernel(source, lo, hi, flow, along, back, gain, sep, t, out, d, turned):
    def block(band, column):
        down, up = across(flow, column)
        x = flat_tile(source, band, column)
        return x - down * flat_tile(lo, band, column) + up * flat_tile(hi, band, column)

    to_runs(block, turned)

    def store(l, value):
        d[l] = value

    def cells(l):
        return cell(turned, l)

    solve(cells, Y_STEPS, Y_LEVELS, y_shift, along, back, gain, sep, d, store)
    for l in range(Y_STEPS):
        turned[pl.ds(l, 8, stride=128), :] = d[l]
    keep = put(out)

    def plus_start(band, column, value):
        keep(band, column, value + flat_tile(t, band, column))

    from_runs(turned, plus_start)


def finish_kernel(own, r1, r2, r3, base, y_lo, y_hi, out, table, side, done, sent):
    index = lax.axis_index("gy")
    place(index, own, (r1, r2, r3), table)
    lane = lax.broadcasted_iota(jnp.int32, (1, 128), 1)

    def port_of(ref):
        return tuple(jnp.where(lane < ROWS, ref[n : n + 1, :], 1.0) for n in range(7))

    nothing = (jnp.zeros((1, 128), F32),) * 3
    scale = 4000.0
    lo, hi = reach(index, [port_of(table.at[j]) for j in range(4)], nothing, nothing, scale)
    f_lo, f_hi = flows(port_of(own), lo, hi, scale)
    side[...] = jnp.zeros_like(side)
    side[0:1, :] = f_lo
    side[1:2, :] = f_hi
    upright = side[...].T
    copies = []
    for band in range(BANDS):
        at = slice(8 * band, 8 * band + 8)
        down = jnp.broadcast_to(upright[at, 0:1], (8, 128))
        up = jnp.broadcast_to(upright[at, 1:2], (8, 128))
        keep = put(done)
        for column in range(TILES):
            part = tile(base, band, column)
            part = part - down * tile(y_lo, band, column) + up * tile(y_hi, band, column)
            keep(band, column, part)
        copy = pltpu.make_async_copy(done.at[at, :], out.at[at, :], sent.at[band])
        copy.start()
        copies.append(copy)
    for copy in copies:
        copy.wait()


def around(value, axis, size, stride, step):
    pairs = []
    for i in range(size):
        digit = (i // stride) % 4
        pairs.append((i, i + ((digit + step) % 4 - digit) * stride))
    return lax.ppermute(value, axis, pairs)


def per_device(initial_heat_state, thermal_coefficient):
    t, k = initial_heat_state[0], thermal_coefficient[0]
    natural = struct(ROWS, COLS)
    t, k, own_lo, own_hi, own_edges = call(
        load_kernel,
        [natural, natural] + [struct(8, 128)] * 3,
        [pltpu.SemaphoreType.DMA((2, BANDS))],
        name="load",
        grant=GRANT,
        in_specs=[HBM, HBM],
        out_specs=[VMEM] * 5,
    )(t, k)
    below = around(own_hi, "gy", 4, 1, 1)
    above = around(own_lo, "gy", 4, 1, 3)
    flat = struct(BANDS * TILES * 8, 128)
    runs = struct(TILES // 2 * 128, 128)
    x_field, y_field = struct(ROWS, TILES, 128), struct(Y_STEPS, 8, 128)
    x_port = struct(7, TILES, 128)
    e, *x_coefficients, x_lo, x_hi, x_ends, t_flat, k_flat = call(
        x_matrix_kernel,
        [
            flat,
            x_field,
            x_field,
            x_field,
            struct((2 * X_LEVELS + 1) * SEGMENTS, TILES, 128),
            x_field,
            x_field,
            x_port,
            flat,
            flat,
        ],
        name="x_matrix",
    )(t, k)
    *y_coefficients, y_lo, y_hi, y_ends = call(
        y_matrix_kernel,
        [
            y_field,
            y_field,
            y_field,
            struct((2 * Y_LEVELS + 1) * SEGMENTS, 8, 128),
            y_field,
            y_field,
            struct(8, 128),
        ],
        [scratch(runs)],
        name="y_matrix",
    )(k)
    below, above, y_lo = lax.optimization_barrier((below, above, y_lo))
    half = struct(7, TILES // 2, 128)
    own, give, edge = call(
        x_port_kernel,
        [half, half, struct(ROWS, 128)],
        [scratch(x_port), pltpu.VMEM((128, 128), F32)],
        flops=200_000,
        name="x_port",
    )(x_ends, x_lo, x_hi, own_edges, below, above)
    u = call(x_solve_kernel, x_field, [scratch(flat)], flops=700_000, name="x_solve")(
        e, *x_coefficients, edge
    )
    pairs = [(i, i ^ 1) for i in range(32)]
    other = lax.ppermute(give, "gx", pairs)
    other, u = lax.optimization_barrier((other, u))
    own_z = call(pair_kernel, half, name="pair")(own, other)
    from_z = [around(own_z, "gx", 32, 2, s) for s in RING]
    flat_lo, flat_hi = call(
        upright_kernel,
        [natural, natural],
        [pltpu.VMEM((2, TILES // 2 * 128, 128), F32)],
        name="upright",
    )(y_lo, y_hi)
    *from_z, flat_lo = lax.optimization_barrier((*from_z, flat_lo))
    table = pltpu.VMEM((4, 7, TILES // 2, 128), F32)
    own_y = call(four_kernel, half, [table], name="four")(own_z, *from_z)
    from_y = [around(own_y, "gx", 32, 8, s) for s in RING]
    square = pltpu.VMEM((128, 128), F32)
    source, lo_flat, hi_flat, mixed, known = call(
        blend_kernel,
        [flat, flat, flat, struct(4, BANDS * TILES * 8, 128), struct(8, 128)],
        [scratch(flat), square],
        name="blend",
    )(u, x_lo, x_hi, flat_lo, flat_hi, t_flat)
    some = struct(2, TILES // 2, 128)
    keep, give = call(through_kernel, [some, some], [table, table], name="through")(
        own_y, *from_y, own_z, *from_z, own, other
    )
    got = lax.ppermute(give, "gx", pairs)
    port, flow = call(
        y_port_kernel, [struct(8, 128), struct(2, TILES, 128)], [square], name="y_port"
    )(keep, got, mixed, known, y_ends)
    from_gy = [around(port, "gy", 4, 1, s) for s in RING]
    base = call(
        y_solve_kernel, natural, [scratch(y_field), scratch(runs)], name="y_solve"
    )(source, lo_flat, hi_flat, flow, *y_coefficients, t_flat)
    updated = call(
        finish_kernel,
        natural,
        [
            pltpu.VMEM((4, 8, 128), F32),
            pltpu.VMEM((128, 128), F32),
            scratch(natural),
            pltpu.SemaphoreType.DMA((BANDS,)),
        ],
        name="finish",
        in_specs=[VMEM] * 7,
        out_specs=HBM,
    )(port, *from_gy, base, flat_lo, flat_hi)
    return updated[None]


def solution(mesh):
    placed = (P(None, "gx", "gy"), P(None, "gx", "gy"))
    return jax.shard_map(
        per_device, mesh=mesh, in_specs=placed, out_specs=P(None, "gx", "gy"), check_vma=False
    )
```

```python
import jax
import jax.numpy as jnp
from jax import lax
from jax.experimental import pallas as pl
from jax.experimental.pallas import tpu as pltpu
from jax.sharding import PartitionSpec as P

ROWS, COLS = 64, 2048
BANDS, TILES = ROWS // 8, COLS // 128
SEGMENTS = 4
Y_STEPS = 128
X_LEVELS, Y_LEVELS = 2, 6
GRANT = (527 << 20) // 10
RING = (1, 3, 2)
F32 = jnp.float32
VMEM = pl.BlockSpec(memory_space=pltpu.VMEM)
HBM = pl.BlockSpec(memory_space=pltpu.MemorySpace.HBM)


def struct(*shape):
    return jax.ShapeDtypeStruct(shape, F32)


def scratch(like):
    return pltpu.VMEM(like.shape, like.dtype)


def whole(outs, args):
    return dict(in_specs=[VMEM] * len(args), out_specs=jax.tree.map(lambda _: VMEM, outs))


def call(kernel, outs, buffers=(), flops=2_000_000, name=None, grant=32 << 20, **windows):
    def run(*args):
        return pl.pallas_call(
            kernel,
            out_shape=outs,
            **(windows or whole(outs, args)),
            scratch_shapes=list(buffers),
            compiler_params=pltpu.CompilerParams(vmem_limit_bytes=grant),
            cost_estimate=pl.CostEstimate(flops=flops, bytes_accessed=1 << 20, transcendentals=0),
            name=name,
        )(*args)

    return run


def moved(chain, by, shift):
    out = []
    for s in range(SEGMENTS):
        runs, at = divmod(s + by, SEGMENTS)
        out.append(shift(chain[at], runs) if runs else chain[at])
    return out


def factor(link, n, levels, shift, along, back, gain, sep):
    m = n // SEGMENTS
    near = [link(s * m) for s in range(SEGMENTS)]
    ground = [jnp.ones_like(near[0])] * SEGMENTS
    held = [jnp.ones_like(near[0])] * SEGMENTS
    for step in range(1, m):
        for s in range(SEGMENTS):
            l = s * m + step
            v = link(l)
            r = 1.0 / (near[s] + ground[s] + v)
            t = v * r
            c = near[s] * r
            along[l], back[l], gain[l] = t, c, r
            held[s] = held[s] + ground[s] * c
            near[s] = near[s] * t
            ground[s] = ground[s] * t
            if step < m - 1:
                ground[s] = ground[s] + 1.0
    before = moved(ground, -1, shift)
    own = [held[s] + before[s] for s in range(SEGMENTS)]
    up = near
    down = moved(near, -1, shift)
    for level in range(levels):
        stride = 1 << level
        r = [1.0 / (own[s] + up[s] + down[s]) for s in range(SEGMENTS)]
        r_down, r_up = moved(r, -stride, shift), moved(r, stride, shift)
        own_down, own_up = moved(own, -stride, shift), moved(own, stride, shift)
        down_down, up_up = moved(down, -stride, shift), moved(up, stride, shift)
        for s in range(SEGMENTS):
            a, b = down[s] * r_down[s], up[s] * r_up[s]
            sep[(level * 2) * SEGMENTS + s] = a
            sep[(level * 2 + 1) * SEGMENTS + s] = b
            own[s] = own[s] + a * own_down[s] + b * own_up[s]
            down[s], up[s] = a * down_down[s], b * up_up[s]
    for s in range(SEGMENTS):
        sep[levels * 2 * SEGMENTS + s] = 1.0 / own[s]


def plus(a, b):
    return b if a is None else a if b is None else a + b


def times(a, b):
    return None if a is None else a * b


def solve(source, n, levels, shift, along, back, gain, sep, part, store):
    m = n // SEGMENTS
    total = [source(s * m) for s in range(SEGMENTS)]
    z = [source(s * m + 1) for s in range(SEGMENTS)]
    zero = [[False] * SEGMENTS for _ in range(m)]
    for step in range(1, m):
        for s in range(SEGMENTS):
            l = s * m + step
            zero[step][s] = z[s] is None
            if z[s] is not None:
                part[l] = z[s] * gain[l]
                total[s] = plus(total[s], z[s] * back[l])
                z[s] = z[s] * along[l]
            if step < m - 1:
                z[s] = plus(source(l + 1), z[s])
    shape = jnp.zeros(along.shape[1:], F32)
    z = [shape if v is None else v for v in z]
    before = moved(z, -1, shift)
    total = [plus(total[s], before[s]) for s in range(SEGMENTS)]
    for level in range(levels):
        stride = 1 << level
        lo, hi = moved(total, -stride, shift), moved(total, stride, shift)
        total = [
            total[s]
            + sep[(level * 2) * SEGMENTS + s] * lo[s]
            + sep[(level * 2 + 1) * SEGMENTS + s] * hi[s]
            for s in range(SEGMENTS)
        ]
    value = [total[s] * sep[levels * 2 * SEGMENTS + s] for s in range(SEGMENTS)]
    after = moved(value, 1, shift)
    for s in range(SEGMENTS):
        store(s * m, value[s])
    for step in reversed(range(1, m)):
        for s in range(SEGMENTS):
            l = s * m + step
            known = back[l] * value[s]
            if not zero[step][s]:
                known = known + part[l]
            after[s] = known + along[l] * after[s]
            store(l, after[s])


def x_shift(value, runs):
    return value


def y_shift(value, runs):
    if runs % 2 == 0:
        return pltpu.roll(value, (-(runs // 2)) % 8, 0)
    swapped = pltpu.roll(value, 64, 1)
    late = lax.broadcasted_iota(jnp.int32, value.shape, 1) >= 64
    if runs == 1:
        return jnp.where(late, pltpu.roll(swapped, 7, 0), swapped)
    return jnp.where(late, swapped, pltpu.roll(swapped, 1, 0))


def tile(ref, band, column):
    return ref[8 * band : 8 * band + 8, 128 * column : 128 * column + 128]


def flat_tile(ref, band, column):
    at = (band * TILES + column) * 8
    return ref[at : at + 8, :]


def row(ref, i):
    return ref[pl.ds((i // 8) * (8 * TILES) + i % 8, TILES, stride=8), :]


def load_kernel(t_far, k_far, t, k, lo, hi, own, arrived):
    copies = []
    for band in range(BANDS):
        at = pl.ds(8 * band, 8)
        for n, (far, near) in enumerate(((t_far, t), (k_far, k))):
            copy = pltpu.make_async_copy(far.at[at, :], near.at[at, :], arrived.at[n, band])
            copy.start()
            copies.append(copy)
    for ref in (lo, hi, own):
        ref[...] = jnp.zeros_like(ref)
    for copy in copies:
        copy.wait()
    for n, (ref, column) in enumerate(((t, 0), (k, 0), (t, TILES - 1), (k, TILES - 1))):
        strip = ref[:, 128 * column : 128 * column + 128].T
        at = 127 if column else 0
        edge = strip[at : at + 1, :]
        own[n : n + 1, 0:ROWS] = edge
        (hi if column else lo)[n % 2 : n % 2 + 1, 0:ROWS] = edge


def total(terms):
    sums = [None] * 4
    for n, term in enumerate(terms):
        sums[n % 4] = plus(sums[n % 4], term)
    return (sums[0] + sums[1]) + (sums[2] + sums[3])


def x_matrix_kernel(t, k, e, along, back, gain, sep, lo, hi, ends, t_flat, flat):
    lane = lax.broadcasted_iota(jnp.int32, (8, 128), 1)
    for band in range(BANDS):
        ks = [tile(k, band, c) for c in range(TILES)]
        ts = [tile(t, band, c) for c in range(TILES)]
        k_left = [pltpu.roll(v, 127, 1) for v in ks]
        t_left = [pltpu.roll(v, 127, 1) for v in ts]
        flow = []
        for c in range(TILES):
            at = pl.ds((band * TILES + c) * 8, 8)
            flat[at, :] = ks[c]
            t_flat[at, :] = ts[c]
            n = min(c + 1, TILES - 1)
            k_next = jnp.where(lane == 127, k_left[n], k_left[c])
            t_next = jnp.where(lane == 127, t_left[n], t_left[c])
            f = 8000.0 * (ks[c] + k_next) * (t_next - ts[c])
            if c == TILES - 1:
                f = jnp.where(lane == 127, 0.0, f)
            flow.append(f)
        turned = [pltpu.roll(v, 1, 1) for v in flow]
        for c in range(TILES):
            at = pl.ds((band * TILES + c) * 8, 8)
            first = turned[c - 1] if c else jnp.zeros_like(turned[0])
            f_before = jnp.where(lane == 0, first, turned[c])
            e[at, :] = 2.0 * ts[c] + (flow[c] - f_before)

    def link(l):
        if l == ROWS - 1:
            return jnp.zeros((TILES, 128), F32)
        return 1000.0 * (row(flat, l) + row(flat, l + 1))

    factor(link, ROWS, X_LEVELS, x_shift, along, back, gain, sep)
    one = jnp.ones((TILES, 128), F32)

    def at_start(l):
        return one if l == 0 else None

    def at_end(l):
        return one if l == ROWS - 1 else None

    def to(ref):
        def store(l, value):
            ref[l] = value

        return store

    args = (ROWS, X_LEVELS, x_shift, along, back, gain, sep)
    solve(at_start, *args, lo, to(lo))
    solve(at_end, *args, hi, to(hi))
    ends[0] = total(lo[i] * row(e, i) for i in range(ROWS))
    ends[1] = total(hi[i] * row(e, i) for i in range(ROWS))
    ends[2] = lo[0]
    ends[3] = lo[ROWS - 1]
    ends[4] = hi[ROWS - 1]
    ends[5] = row(flat, 0)
    ends[6] = row(flat, ROWS - 1)


def x_port_kernel(ends, lo, hi, own, below, above, keep, give, edge, port, side):
    at = lax.axis_index("gy")
    side[...] = jnp.zeros_like(side)
    t_lo, k_lo, t_hi, k_hi = (own[n : n + 1, :] for n in range(4))
    before = jnp.where(at == 0, 0.0, below[...])
    after = jnp.where(at == lax.axis_size("gy") - 1, 0.0, above[...])
    side[0:1, :] = -8000.0 * (k_lo + before[1:2, :]) * (t_lo - before[0:1, :])
    side[127:128, :] = 8000.0 * (k_hi + after[1:2, :]) * (after[0:1, :] - t_hi)
    edge[...] = side[...].T[0:ROWS, :]
    lane = lax.broadcasted_iota(jnp.int32, (1, 128), 1)
    for n, response in enumerate((lo, hi)):
        port[n] = ends[n]
        for column, kept in ((0, 0), (TILES - 1, 127)):
            term = edge[...] * response[:, column, :]
            term = jnp.where(lane == kept, jnp.sum(term, axis=0, keepdims=True), 0.0)
            port[n, column : column + 1, :] = port[n, column : column + 1, :] + term
    core = lax.rem(lax.axis_index("gx"), 2)
    for n in range(7):
        ref = port if n < 2 else ends
        keep[n], give[n] = choose(core == 0, halves(ref, n), halves(ref, n)[::-1])


def halves(ref, n):
    return ref[n, : TILES // 2, :], ref[n, TILES // 2 :, :]


def x_solve_kernel(e, along, back, gain, sep, edge, u, flat):
    lane = lax.broadcasted_iota(jnp.int32, (8, 128), 1)
    flat[...] = e[...]
    for band in range(BANDS):
        part = edge[8 * band : 8 * band + 8, :]
        at = pl.ds(band * TILES * 8, 8)
        flat[at, :] = flat[at, :] + jnp.where(lane == 0, part, 0.0)
        at = pl.ds((band * TILES + TILES - 1) * 8, 8)
        flat[at, :] = flat[at, :] + jnp.where(lane == 127, part, 0.0)

    def store(l, value):
        u[l] = value

    def source(l):
        return row(flat, l)

    solve(source, ROWS, X_LEVELS, x_shift, along, back, gain, sep, u, store)


def take(ref):
    return tuple(ref[n] for n in range(7))


def join(one, two, scale):
    a1, b1, al1, be1, ga1, kf1, kl1 = one
    a2, b2, al2, be2, ga2, kf2, kl2 = two
    rho = 1.0 / (1.0 / (scale * (kl1 + kf2)) + al2 + ga1)
    delta = (a2 - b1) * rho
    return (
        a1 + be1 * delta,
        b2 - be2 * delta,
        al1 - be1 * be1 * rho,
        be1 * be2 * rho,
        ga2 - be2 * be2 * rho,
        kf1,
        kl2,
    )


def past_up(state, port, scale):
    p, q, k = state
    a, b, al, be, ga, kf, kl = port
    w = be / (1.0 / (scale * (k + kf)) + al + q)
    return (b - w * (a - p), ga - w * be, kl)


def past_down(state, port, scale):
    p, q, k = state
    a, b, al, be, ga, kf, kl = port
    w = be / (1.0 / (scale * (k + kl)) + ga + q)
    return (a + w * (p - b), al - w * be, kf)


def choose(condition, new, old):
    return tuple(jnp.where(condition, x, y) for x, y in zip(new, old))


def reach(index, ports, lo, hi, scale):
    count = len(ports)
    for n in range(count - 1):
        lo = choose(n < index, past_up(lo, ports[n], scale), lo)
    for n in reversed(range(1, count)):
        hi = choose(n > index, past_down(hi, ports[n], scale), hi)
    return lo, hi


def flows(port, lo, hi, scale):
    a, b, al, be, ga, kf, kl = port
    d_lo = 1.0 / (scale * (lo[2] + kf)) + al + lo[1]
    d_hi = 1.0 / (scale * (hi[2] + kl)) + ga + hi[1]
    c_lo, c_hi = a - lo[0], hi[0] - b
    inverse = 1.0 / (d_lo * d_hi - be * be)
    return (d_hi * c_lo + be * c_hi) * inverse, (d_lo * c_hi + be * c_lo) * inverse


def place(index, own, received, table):
    table[index] = own[...]
    for s, value in zip(RING, received):
        table[lax.bitwise_xor(index, s)] = value[...]


def pair_kernel(own, other, out):
    core = lax.rem(lax.axis_index("gx"), 2)
    mine, theirs = take(own), take(other)
    first = choose(core == 0, mine, theirs)
    second = choose(core == 0, theirs, mine)
    for n, value in enumerate(join(first, second, 1000.0)):
        out[n] = value


def four_kernel(own, r1, r2, r3, out, table):
    z = lax.rem(lax.div(lax.axis_index("gx"), 2), 4)
    place(z, own, (r1, r2, r3), table)
    ports = [take(table.at[j]) for j in range(4)]
    joined = join(join(ports[0], ports[1], 1000.0), join(ports[2], ports[3], 1000.0), 1000.0)
    for n, value in enumerate(joined):
        out[n] = value


def to_runs(blocks, out):
    for p in range(TILES // 2):
        stack = [blocks(band, 2 * p + half) for half in range(2) for band in range(BANDS)]
        out[128 * p : 128 * p + 128, :] = jnp.concatenate(stack, axis=0).T


def cell(ref, l):
    return ref[pl.ds(l, 8, stride=128), :]


def from_runs(turned, store):
    for p in range(TILES // 2):
        block = turned[128 * p : 128 * p + 128, :].T
        for half in range(2):
            for band in range(BANDS):
                at = ROWS * half + 8 * band
                store(band, 2 * p + half, block[at : at + 8, :])


def put(ref):
    def store(band, column, value):
        ref[8 * band : 8 * band + 8, 128 * column : 128 * column + 128] = value

    return store


def y_matrix_kernel(k, along, back, gain, sep, lo, hi, ends, turned):
    to_runs(lambda band, column: tile(k, band, column), turned)
    lane = lax.broadcasted_iota(jnp.int32, (8, 128), 1)
    sublane = lax.broadcasted_iota(jnp.int32, (8, 128), 0)
    very_last = (lane >= 64) & (sublane == 7)
    very_first = (lane < 64) & (sublane == 0)

    def link(l):
        if l == Y_STEPS - 1:
            both = 4000.0 * (cell(turned, l) + y_shift(cell(turned, 0), 1))
            return jnp.where(very_last, 0.0, both)
        return 4000.0 * (cell(turned, l) + cell(turned, l + 1))

    factor(link, Y_STEPS, Y_LEVELS, y_shift, along, back, gain, sep)

    def at_start(l):
        return jnp.where(very_first, 1.0, 0.0) if l == 0 else None

    def at_end(l):
        return jnp.where(very_last, 1.0, 0.0) if l == Y_STEPS - 1 else None

    def to(ref):
        def store(l, value):
            ref[l] = value

        return store

    args = (Y_STEPS, Y_LEVELS, y_shift, along, back, gain, sep)
    solve(at_start, *args, lo, to(lo))
    solve(at_end, *args, hi, to(hi))
    last = Y_STEPS - 1
    ends[...] = jnp.zeros_like(ends)
    ends[0:1, :] = lo[0, 0:1, :]
    ends[1:2, :] = pltpu.roll(lo[last], 64, 1)[7:8, :]
    ends[2:3, :] = pltpu.roll(hi[last], 64, 1)[7:8, :]
    ends[3:4, :] = cell(turned, 0)[0:1, :]
    ends[4:5, :] = pltpu.roll(cell(turned, last), 64, 1)[7:8, :]


def upright_kernel(lo, hi, flat_lo, flat_hi, turned):
    for n, (response, flat) in enumerate(((lo, flat_lo), (hi, flat_hi))):
        for l in range(Y_STEPS):
            turned[n, pl.ds(l, 8, stride=128), :] = response[l]
        from_runs(turned.at[n], put(flat))


def blend_kernel(u, x_lo, x_hi, y_lo, y_hi, t, source, lo, hi, mixed, known, flat, side):
    for ref, out in ((u, flat), (x_lo, lo), (x_hi, hi)):
        for i in range(ROWS):
            at = pl.ds((i // 8) * (8 * TILES) + i % 8, TILES, stride=8)
            out[at, :] = ref[i]
    for band in range(BANDS):
        sums = [None, None]
        for column in range(TILES):
            at = pl.ds((band * TILES + column) * 8, 8)
            value = flat[at, :] - 2.0 * t[at, :]
            source[at, :] = value
            for n, response in enumerate((y_lo, y_hi)):
                r = tile(response, band, column)
                sums[n] = plus(sums[n], r * value)
                mixed[2 * n, at, :] = r * lo[at, :]
                mixed[2 * n + 1, at, :] = r * hi[at, :]
        for n in range(2):
            side[64 * n + 8 * band : 64 * n + 8 * band + 8, :] = sums[n]
    known[...] = jnp.broadcast_to(jnp.sum(side[...].T, axis=0, keepdims=True), (8, 128))


def through_kernel(
    own_y, y1, y2, y3, own_z, z1, z2, z3, own, other, keep, give, table_y, table_z
):
    index = lax.axis_index("gx")
    core, z, y = lax.rem(index, 2), lax.rem(lax.div(index, 2), 4), lax.div(index, 8)
    place(y, own_y, (y1, y2, y3), table_y)
    place(z, own_z, (z1, z2, z3), table_z)
    nothing = (jnp.zeros(own.shape[1:], F32),) * 3
    scale = 1000.0
    lo, hi = reach(y, [take(table_y.at[j]) for j in range(4)], nothing, nothing, scale)
    lo, hi = reach(z, [take(table_z.at[j]) for j in range(4)], lo, hi, scale)
    mine, theirs = take(own), take(other)
    first = choose(core == 0, mine, theirs)
    second = choose(core == 0, theirs, mine)
    at_first = flows(first, lo, past_down(hi, second, scale), scale)
    at_second = flows(second, past_up(lo, first, scale), hi, scale)
    keep[0], keep[1] = choose(core == 0, at_first, at_second)
    give[0], give[1] = choose(core == 0, at_second, at_first)


def y_port_kernel(keep, got, mixed, known, ends, port, flow, side):
    core = lax.rem(lax.axis_index("gx"), 2)
    for n in range(2):
        flow[n, : TILES // 2, :] = jnp.where(core == 0, keep[n], got[n])
        flow[n, TILES // 2 :, :] = jnp.where(core == 0, got[n], keep[n])
    sums = [None] * (2 * BANDS)
    for column in range(TILES):
        down, up = across(flow, column)
        for band in range(BANDS):
            at = pl.ds((band * TILES + column) * 8, 8)
            for n in range(2):
                part = up * mixed[2 * n + 1, at, :] - down * mixed[2 * n, at, :]
                sums[BANDS * n + band] = plus(sums[BANDS * n + band], part)
    for n, value in enumerate(sums):
        side[8 * n : 8 * n + 8, :] = value
    both = jnp.sum(side[...].T, axis=0, keepdims=True) + known[0:1, :]
    port[...] = jnp.zeros_like(port)
    port[0:1, :] = both
    port[1:2, :] = pltpu.roll(both, 64, 1)
    port[2:7, :] = ends[0:5, :]


def across(flow, column):
    return tuple(
        jnp.broadcast_to(flow[n, column : column + 1, :], (8, 128)) for n in range(2)
    )


def y_solve_kernel(source, lo, hi, flow, along, back, gain, sep, t, out, d, turned):
    def block(band, column):
        down, up = across(flow, column)
        x = flat_tile(source, band, column)
        return x - down * flat_tile(lo, band, column) + up * flat_tile(hi, band, column)

    to_runs(block, turned)

    def store(l, value):
        d[l] = value

    def cells(l):
        return cell(turned, l)

    solve(cells, Y_STEPS, Y_LEVELS, y_shift, along, back, gain, sep, d, store)
    for l in range(Y_STEPS):
        turned[pl.ds(l, 8, stride=128), :] = d[l]
    keep = put(out)

    def plus_start(band, column, value):
        keep(band, column, value + flat_tile(t, band, column))

    from_runs(turned, plus_start)


def finish_kernel(own, r1, r2, r3, base, y_lo, y_hi, out, table, side, done, sent):
    index = lax.axis_index("gy")
    place(index, own, (r1, r2, r3), table)
    lane = lax.broadcasted_iota(jnp.int32, (1, 128), 1)

    def port_of(ref):
        return tuple(jnp.where(lane < ROWS, ref[n : n + 1, :], 1.0) for n in range(7))

    nothing = (jnp.zeros((1, 128), F32),) * 3
    scale = 4000.0
    lo, hi = reach(index, [port_of(table.at[j]) for j in range(4)], nothing, nothing, scale)
    f_lo, f_hi = flows(port_of(own), lo, hi, scale)
    side[...] = jnp.zeros_like(side)
    side[0:1, :] = f_lo
    side[1:2, :] = f_hi
    upright = side[...].T
    copies = []
    for band in range(BANDS):
        at = slice(8 * band, 8 * band + 8)
        down = jnp.broadcast_to(upright[at, 0:1], (8, 128))
        up = jnp.broadcast_to(upright[at, 1:2], (8, 128))
        keep = put(done)
        for column in range(TILES):
            part = tile(base, band, column)
            part = part - down * tile(y_lo, band, column) + up * tile(y_hi, band, column)
            keep(band, column, part)
        copy = pltpu.make_async_copy(done.at[at, :], out.at[at, :], sent.at[band])
        copy.start()
        copies.append(copy)
    for copy in copies:
        copy.wait()


def around(value, axis, size, stride, step):
    pairs = []
    for i in range(size):
        digit = (i // stride) % 4
        pairs.append((i, i + ((digit ^ step) - digit) * stride))
    return lax.ppermute(value, axis, pairs)


def per_device(initial_heat_state, thermal_coefficient):
    t, k = initial_heat_state[0], thermal_coefficient[0]
    natural = struct(ROWS, COLS)
    t, k, own_lo, own_hi, own_edges = call(
        load_kernel,
        [natural, natural] + [struct(8, 128)] * 3,
        [pltpu.SemaphoreType.DMA((2, BANDS))],
        name="load",
        grant=GRANT,
        in_specs=[HBM, HBM],
        out_specs=[VMEM] * 5,
    )(t, k)
    below = lax.ppermute(own_hi, "gy", [(i, (i + 1) % 4) for i in range(4)])
    above = lax.ppermute(own_lo, "gy", [((i + 1) % 4, i) for i in range(4)])
    flat = struct(BANDS * TILES * 8, 128)
    runs = struct(TILES // 2 * 128, 128)
    x_field, y_field = struct(ROWS, TILES, 128), struct(Y_STEPS, 8, 128)
    x_port = struct(7, TILES, 128)
    e, *x_coefficients, x_lo, x_hi, x_ends, t_flat, k_flat = call(
        x_matrix_kernel,
        [
            flat,
            x_field,
            x_field,
            x_field,
            struct((2 * X_LEVELS + 1) * SEGMENTS, TILES, 128),
            x_field,
            x_field,
            x_port,
            flat,
            flat,
        ],
        name="x_matrix",
    )(t, k)
    *y_coefficients, y_lo, y_hi, y_ends = call(
        y_matrix_kernel,
        [
            y_field,
            y_field,
            y_field,
            struct((2 * Y_LEVELS + 1) * SEGMENTS, 8, 128),
            y_field,
            y_field,
            struct(8, 128),
        ],
        [scratch(runs)],
        name="y_matrix",
    )(k)
    below, above, y_lo = lax.optimization_barrier((below, above, y_lo))
    half = struct(7, TILES // 2, 128)
    own, give, edge = call(
        x_port_kernel,
        [half, half, struct(ROWS, 128)],
        [scratch(x_port), pltpu.VMEM((128, 128), F32)],
        flops=200_000,
        name="x_port",
    )(x_ends, x_lo, x_hi, own_edges, below, above)
    u = call(x_solve_kernel, x_field, [scratch(flat)], flops=700_000, name="x_solve")(
        e, *x_coefficients, edge
    )
    pairs = [(i, i ^ 1) for i in range(32)]
    other = lax.ppermute(give, "gx", pairs)
    other, u = lax.optimization_barrier((other, u))
    own_z = call(pair_kernel, half, name="pair")(own, other)
    from_z = [around(own_z, "gx", 32, 2, s) for s in RING]
    flat_lo, flat_hi = call(
        upright_kernel,
        [natural, natural],
        [pltpu.VMEM((2, TILES // 2 * 128, 128), F32)],
        name="upright",
    )(y_lo, y_hi)
    *from_z, flat_lo = lax.optimization_barrier((*from_z, flat_lo))
    table = pltpu.VMEM((4, 7, TILES // 2, 128), F32)
    own_y = call(four_kernel, half, [table], name="four")(own_z, *from_z)
    from_y = [around(own_y, "gx", 32, 8, s) for s in RING]
    square = pltpu.VMEM((128, 128), F32)
    source, lo_flat, hi_flat, mixed, known = call(
        blend_kernel,
        [flat, flat, flat, struct(4, BANDS * TILES * 8, 128), struct(8, 128)],
        [scratch(flat), square],
        name="blend",
    )(u, x_lo, x_hi, flat_lo, flat_hi, t_flat)
    some = struct(2, TILES // 2, 128)
    keep, give = call(through_kernel, [some, some], [table, table], name="through")(
        own_y, *from_y, own_z, *from_z, own, other
    )
    got = lax.ppermute(give, "gx", pairs)
    port, flow = call(
        y_port_kernel, [struct(8, 128), struct(2, TILES, 128)], [square], name="y_port"
    )(keep, got, mixed, known, y_ends)
    from_gy = [around(port, "gy", 4, 1, s) for s in RING]
    base = call(
        y_solve_kernel, natural, [scratch(y_field), scratch(runs)], name="y_solve"
    )(source, lo_flat, hi_flat, flow, *y_coefficients, t_flat)
    updated = call(
        finish_kernel,
        natural,
        [
            pltpu.VMEM((4, 8, 128), F32),
            pltpu.VMEM((128, 128), F32),
            scratch(natural),
            pltpu.SemaphoreType.DMA((BANDS,)),
        ],
        name="finish",
        in_specs=[VMEM] * 7,
        out_specs=HBM,
    )(port, *from_gy, base, flat_lo, flat_hi)
    return updated[None]


def solution(mesh):
    placed = (P(None, "gx", "gy"), P(None, "gx", "gy"))
    return jax.shard_map(
        per_device, mesh=mesh, in_specs=placed, out_specs=P(None, "gx", "gy"), check_vma=False
    )
```

```python
import jax
import jax.numpy as jnp
from jax import lax
from jax.experimental import pallas as pl
from jax.experimental.pallas import tpu as pltpu
from jax.sharding import PartitionSpec as P

ROWS, COLS = 64, 2048
BANDS, TILES = ROWS // 8, COLS // 128
SEGMENTS = 4
Y_STEPS = 128
X_LEVELS, Y_LEVELS = 2, 6
GRANT = (527 << 20) // 10
RING = (1, 2, 3)
F32 = jnp.float32
VMEM = pl.BlockSpec(memory_space=pltpu.VMEM)
HBM = pl.BlockSpec(memory_space=pltpu.MemorySpace.HBM)


def struct(*shape):
    return jax.ShapeDtypeStruct(shape, F32)


def scratch(like):
    return pltpu.VMEM(like.shape, like.dtype)


def whole(outs, args):
    return dict(in_specs=[VMEM] * len(args), out_specs=jax.tree.map(lambda _: VMEM, outs))


def call(kernel, outs, buffers=(), flops=2_000_000, name=None, grant=32 << 20, **windows):
    def run(*args):
        return pl.pallas_call(
            kernel,
            out_shape=outs,
            **(windows or whole(outs, args)),
            scratch_shapes=list(buffers),
            compiler_params=pltpu.CompilerParams(vmem_limit_bytes=grant),
            cost_estimate=pl.CostEstimate(flops=flops, bytes_accessed=1 << 20, transcendentals=0),
            name=name,
        )(*args)

    return run


def moved(chain, by, shift):
    out = []
    for s in range(SEGMENTS):
        runs, at = divmod(s + by, SEGMENTS)
        out.append(shift(chain[at], runs) if runs else chain[at])
    return out


def factor(link, n, levels, shift, along, back, gain, sep):
    m = n // SEGMENTS
    near = [link(s * m) for s in range(SEGMENTS)]
    ground = [jnp.ones_like(near[0])] * SEGMENTS
    held = [jnp.ones_like(near[0])] * SEGMENTS
    for step in range(1, m):
        for s in range(SEGMENTS):
            l = s * m + step
            v = link(l)
            r = 1.0 / (near[s] + ground[s] + v)
            t = v * r
            c = near[s] * r
            along[l], back[l], gain[l] = t, c, r
            held[s] = held[s] + ground[s] * c
            near[s] = near[s] * t
            ground[s] = ground[s] * t
            if step < m - 1:
                ground[s] = ground[s] + 1.0
    before = moved(ground, -1, shift)
    own = [held[s] + before[s] for s in range(SEGMENTS)]
    up = near
    down = moved(near, -1, shift)
    for level in range(levels):
        stride = 1 << level
        r = [1.0 / (own[s] + up[s] + down[s]) for s in range(SEGMENTS)]
        r_down, r_up = moved(r, -stride, shift), moved(r, stride, shift)
        own_down, own_up = moved(own, -stride, shift), moved(own, stride, shift)
        down_down, up_up = moved(down, -stride, shift), moved(up, stride, shift)
        for s in range(SEGMENTS):
            a, b = down[s] * r_down[s], up[s] * r_up[s]
            sep[(level * 2) * SEGMENTS + s] = a
            sep[(level * 2 + 1) * SEGMENTS + s] = b
            own[s] = own[s] + a * own_down[s] + b * own_up[s]
            down[s], up[s] = a * down_down[s], b * up_up[s]
    for s in range(SEGMENTS):
        sep[levels * 2 * SEGMENTS + s] = 1.0 / own[s]


def plus(a, b):
    return b if a is None else a if b is None else a + b


def times(a, b):
    return None if a is None else a * b


def solve(source, n, levels, shift, along, back, gain, sep, part, store):
    m = n // SEGMENTS
    total = [source(s * m) for s in range(SEGMENTS)]
    z = [source(s * m + 1) for s in range(SEGMENTS)]
    zero = [[False] * SEGMENTS for _ in range(m)]
    for step in range(1, m):
        for s in range(SEGMENTS):
            l = s * m + step
            zero[step][s] = z[s] is None
            if z[s] is not None:
                part[l] = z[s] * gain[l]
                total[s] = plus(total[s], z[s] * back[l])
                z[s] = z[s] * along[l]
            if step < m - 1:
                z[s] = plus(source(l + 1), z[s])
    shape = jnp.zeros(along.shape[1:], F32)
    z = [shape if v is None else v for v in z]
    before = moved(z, -1, shift)
    total = [plus(total[s], before[s]) for s in range(SEGMENTS)]
    for level in range(levels):
        stride = 1 << level
        lo, hi = moved(total, -stride, shift), moved(total, stride, shift)
        total = [
            total[s]
            + sep[(level * 2) * SEGMENTS + s] * lo[s]
            + sep[(level * 2 + 1) * SEGMENTS + s] * hi[s]
            for s in range(SEGMENTS)
        ]
    value = [total[s] * sep[levels * 2 * SEGMENTS + s] for s in range(SEGMENTS)]
    after = moved(value, 1, shift)
    for s in range(SEGMENTS):
        store(s * m, value[s])
    for step in reversed(range(1, m)):
        for s in range(SEGMENTS):
            l = s * m + step
            known = back[l] * value[s]
            if not zero[step][s]:
                known = known + part[l]
            after[s] = known + along[l] * after[s]
            store(l, after[s])


def x_shift(value, runs):
    return value


def y_shift(value, runs):
    if runs % 2 == 0:
        return pltpu.roll(value, (-(runs // 2)) % 8, 0)
    swapped = pltpu.roll(value, 64, 1)
    late = lax.broadcasted_iota(jnp.int32, value.shape, 1) >= 64
    if runs == 1:
        return jnp.where(late, pltpu.roll(swapped, 7, 0), swapped)
    return jnp.where(late, swapped, pltpu.roll(swapped, 1, 0))


def tile(ref, band, column):
    return ref[8 * band : 8 * band + 8, 128 * column : 128 * column + 128]


def flat_tile(ref, band, column):
    at = (band * TILES + column) * 8
    return ref[at : at + 8, :]


def row(ref, i):
    return ref[pl.ds((i // 8) * (8 * TILES) + i % 8, TILES, stride=8), :]


def load_kernel(t_far, k_far, t, k, lo, hi, own, arrived):
    copies = []
    for band in range(BANDS):
        at = pl.ds(8 * band, 8)
        for n, (far, near) in enumerate(((t_far, t), (k_far, k))):
            copy = pltpu.make_async_copy(far.at[at, :], near.at[at, :], arrived.at[n, band])
            copy.start()
            copies.append(copy)
    for ref in (lo, hi, own):
        ref[...] = jnp.zeros_like(ref)
    for copy in copies:
        copy.wait()
    for n, (ref, column) in enumerate(((t, 0), (k, 0), (t, TILES - 1), (k, TILES - 1))):
        strip = ref[:, 128 * column : 128 * column + 128].T
        at = 127 if column else 0
        edge = strip[at : at + 1, :]
        own[n : n + 1, 0:ROWS] = edge
        (hi if column else lo)[n % 2 : n % 2 + 1, 0:ROWS] = edge


def total(terms):
    sums = [None] * 4
    for n, term in enumerate(terms):
        sums[n % 4] = plus(sums[n % 4], term)
    return (sums[0] + sums[1]) + (sums[2] + sums[3])


def x_matrix_kernel(t, k, e, along, back, gain, sep, lo, hi, ends, t_flat, flat):
    lane = lax.broadcasted_iota(jnp.int32, (8, 128), 1)
    for band in range(BANDS):
        ks = [tile(k, band, c) for c in range(TILES)]
        ts = [tile(t, band, c) for c in range(TILES)]
        k_left = [pltpu.roll(v, 127, 1) for v in ks]
        t_left = [pltpu.roll(v, 127, 1) for v in ts]
        flow = []
        for c in range(TILES):
            at = pl.ds((band * TILES + c) * 8, 8)
            flat[at, :] = ks[c]
            t_flat[at, :] = ts[c]
            n = min(c + 1, TILES - 1)
            k_next = jnp.where(lane == 127, k_left[n], k_left[c])
            t_next = jnp.where(lane == 127, t_left[n], t_left[c])
            f = 8000.0 * (ks[c] + k_next) * (t_next - ts[c])
            if c == TILES - 1:
                f = jnp.where(lane == 127, 0.0, f)
            flow.append(f)
        turned = [pltpu.roll(v, 1, 1) for v in flow]
        for c in range(TILES):
            at = pl.ds((band * TILES + c) * 8, 8)
            first = turned[c - 1] if c else jnp.zeros_like(turned[0])
            f_before = jnp.where(lane == 0, first, turned[c])
            e[at, :] = 2.0 * ts[c] + (flow[c] - f_before)

    def link(l):
        if l == ROWS - 1:
            return jnp.zeros((TILES, 128), F32)
        return 1000.0 * (row(flat, l) + row(flat, l + 1))

    factor(link, ROWS, X_LEVELS, x_shift, along, back, gain, sep)
    one = jnp.ones((TILES, 128), F32)

    def at_start(l):
        return one if l == 0 else None

    def at_end(l):
        return one if l == ROWS - 1 else None

    def to(ref):
        def store(l, value):
            ref[l] = value

        return store

    args = (ROWS, X_LEVELS, x_shift, along, back, gain, sep)
    solve(at_start, *args, lo, to(lo))
    solve(at_end, *args, hi, to(hi))
    ends[0] = total(lo[i] * row(e, i) for i in range(ROWS))
    ends[1] = total(hi[i] * row(e, i) for i in range(ROWS))
    ends[2] = lo[0]
    ends[3] = lo[ROWS - 1]
    ends[4] = hi[ROWS - 1]
    ends[5] = row(flat, 0)
    ends[6] = row(flat, ROWS - 1)


def x_port_kernel(ends, lo, hi, own, below, above, keep, give, edge, port, side):
    at = lax.axis_index("gy")
    side[...] = jnp.zeros_like(side)
    t_lo, k_lo, t_hi, k_hi = (own[n : n + 1, :] for n in range(4))
    before = jnp.where(at == 0, 0.0, below[...])
    after = jnp.where(at == lax.axis_size("gy") - 1, 0.0, above[...])
    side[0:1, :] = -8000.0 * (k_lo + before[1:2, :]) * (t_lo - before[0:1, :])
    side[127:128, :] = 8000.0 * (k_hi + after[1:2, :]) * (after[0:1, :] - t_hi)
    edge[...] = side[...].T[0:ROWS, :]
    lane = lax.broadcasted_iota(jnp.int32, (1, 128), 1)
    for n, response in enumerate((lo, hi)):
        port[n] = ends[n]
        for column, kept in ((0, 0), (TILES - 1, 127)):
            term = edge[...] * response[:, column, :]
            term = jnp.where(lane == kept, jnp.sum(term, axis=0, keepdims=True), 0.0)
            port[n, column : column + 1, :] = port[n, column : column + 1, :] + term
    core = lax.rem(lax.axis_index("gx"), 2)
    for n in range(7):
        ref = port if n < 2 else ends
        keep[n], give[n] = choose(core == 0, halves(ref, n), halves(ref, n)[::-1])


def halves(ref, n):
    return ref[n, : TILES // 2, :], ref[n, TILES // 2 :, :]


def x_solve_kernel(e, along, back, gain, sep, edge, u, flat):
    lane = lax.broadcasted_iota(jnp.int32, (8, 128), 1)
    flat[...] = e[...]
    for band in range(BANDS):
        part = edge[8 * band : 8 * band + 8, :]
        at = pl.ds(band * TILES * 8, 8)
        flat[at, :] = flat[at, :] + jnp.where(lane == 0, part, 0.0)
        at = pl.ds((band * TILES + TILES - 1) * 8, 8)
        flat[at, :] = flat[at, :] + jnp.where(lane == 127, part, 0.0)

    def store(l, value):
        u[l] = value

    def source(l):
        return row(flat, l)

    solve(source, ROWS, X_LEVELS, x_shift, along, back, gain, sep, u, store)


def take(ref):
    return tuple(ref[n] for n in range(7))


def join(one, two, scale):
    a1, b1, al1, be1, ga1, kf1, kl1 = one
    a2, b2, al2, be2, ga2, kf2, kl2 = two
    rho = 1.0 / (1.0 / (scale * (kl1 + kf2)) + al2 + ga1)
    delta = (a2 - b1) * rho
    return (
        a1 + be1 * delta,
        b2 - be2 * delta,
        al1 - be1 * be1 * rho,
        be1 * be2 * rho,
        ga2 - be2 * be2 * rho,
        kf1,
        kl2,
    )


def past_up(state, port, scale):
    p, q, k = state
    a, b, al, be, ga, kf, kl = port
    w = be / (1.0 / (scale * (k + kf)) + al + q)
    return (b - w * (a - p), ga - w * be, kl)


def past_down(state, port, scale):
    p, q, k = state
    a, b, al, be, ga, kf, kl = port
    w = be / (1.0 / (scale * (k + kl)) + ga + q)
    return (a + w * (p - b), al - w * be, kf)


def choose(condition, new, old):
    return tuple(jnp.where(condition, x, y) for x, y in zip(new, old))


def reach(index, ports, lo, hi, scale):
    count = len(ports)
    for n in range(count - 1):
        lo = choose(n < index, past_up(lo, ports[n], scale), lo)
    for n in reversed(range(1, count)):
        hi = choose(n > index, past_down(hi, ports[n], scale), hi)
    return lo, hi


def flows(port, lo, hi, scale):
    a, b, al, be, ga, kf, kl = port
    d_lo = 1.0 / (scale * (lo[2] + kf)) + al + lo[1]
    d_hi = 1.0 / (scale * (hi[2] + kl)) + ga + hi[1]
    c_lo, c_hi = a - lo[0], hi[0] - b
    inverse = 1.0 / (d_lo * d_hi - be * be)
    return (d_hi * c_lo + be * c_hi) * inverse, (d_lo * c_hi + be * c_lo) * inverse


def place(index, own, received, table):
    table[index] = own[...]
    for s, value in zip(RING, received):
        table[lax.bitwise_xor(index, s)] = value[...]


def pair_kernel(own, other, out):
    core = lax.rem(lax.axis_index("gx"), 2)
    mine, theirs = take(own), take(other)
    first = choose(core == 0, mine, theirs)
    second = choose(core == 0, theirs, mine)
    for n, value in enumerate(join(first, second, 1000.0)):
        out[n] = value


def four_kernel(own, r1, r2, r3, out, table):
    z = lax.rem(lax.div(lax.axis_index("gx"), 2), 4)
    place(z, own, (r1, r2, r3), table)
    ports = [take(table.at[j]) for j in range(4)]
    joined = join(join(ports[0], ports[1], 1000.0), join(ports[2], ports[3], 1000.0), 1000.0)
    for n, value in enumerate(joined):
        out[n] = value


def to_runs(blocks, out):
    for p in range(TILES // 2):
        stack = [blocks(band, 2 * p + half) for half in range(2) for band in range(BANDS)]
        out[128 * p : 128 * p + 128, :] = jnp.concatenate(stack, axis=0).T


def cell(ref, l):
    return ref[pl.ds(l, 8, stride=128), :]


def from_runs(turned, store):
    for p in range(TILES // 2):
        block = turned[128 * p : 128 * p + 128, :].T
        for half in range(2):
            for band in range(BANDS):
                at = ROWS * half + 8 * band
                store(band, 2 * p + half, block[at : at + 8, :])


def put(ref):
    def store(band, column, value):
        ref[8 * band : 8 * band + 8, 128 * column : 128 * column + 128] = value

    return store


def y_matrix_kernel(k, along, back, gain, sep, lo, hi, ends, turned):
    to_runs(lambda band, column: tile(k, band, column), turned)
    lane = lax.broadcasted_iota(jnp.int32, (8, 128), 1)
    sublane = lax.broadcasted_iota(jnp.int32, (8, 128), 0)
    very_last = (lane >= 64) & (sublane == 7)
    very_first = (lane < 64) & (sublane == 0)

    def link(l):
        if l == Y_STEPS - 1:
            both = 4000.0 * (cell(turned, l) + y_shift(cell(turned, 0), 1))
            return jnp.where(very_last, 0.0, both)
        return 4000.0 * (cell(turned, l) + cell(turned, l + 1))

    factor(link, Y_STEPS, Y_LEVELS, y_shift, along, back, gain, sep)

    def at_start(l):
        return jnp.where(very_first, 1.0, 0.0) if l == 0 else None

    def at_end(l):
        return jnp.where(very_last, 1.0, 0.0) if l == Y_STEPS - 1 else None

    def to(ref):
        def store(l, value):
            ref[l] = value

        return store

    args = (Y_STEPS, Y_LEVELS, y_shift, along, back, gain, sep)
    solve(at_start, *args, lo, to(lo))
    solve(at_end, *args, hi, to(hi))
    last = Y_STEPS - 1
    ends[...] = jnp.zeros_like(ends)
    ends[0:1, :] = lo[0, 0:1, :]
    ends[1:2, :] = pltpu.roll(lo[last], 64, 1)[7:8, :]
    ends[2:3, :] = pltpu.roll(hi[last], 64, 1)[7:8, :]
    ends[3:4, :] = cell(turned, 0)[0:1, :]
    ends[4:5, :] = pltpu.roll(cell(turned, last), 64, 1)[7:8, :]


def upright_kernel(lo, hi, flat_lo, flat_hi, turned):
    for n, (response, flat) in enumerate(((lo, flat_lo), (hi, flat_hi))):
        for l in range(Y_STEPS):
            turned[n, pl.ds(l, 8, stride=128), :] = response[l]
        from_runs(turned.at[n], put(flat))


def blend_kernel(u, x_lo, x_hi, y_lo, y_hi, t, source, lo, hi, mixed, known, flat, side):
    for ref, out in ((u, flat), (x_lo, lo), (x_hi, hi)):
        for i in range(ROWS):
            at = pl.ds((i // 8) * (8 * TILES) + i % 8, TILES, stride=8)
            out[at, :] = ref[i]
    for band in range(BANDS):
        sums = [None, None]
        for column in range(TILES):
            at = pl.ds((band * TILES + column) * 8, 8)
            value = flat[at, :] - 2.0 * t[at, :]
            source[at, :] = value
            for n, response in enumerate((y_lo, y_hi)):
                r = tile(response, band, column)
                sums[n] = plus(sums[n], r * value)
                mixed[2 * n, at, :] = r * lo[at, :]
                mixed[2 * n + 1, at, :] = r * hi[at, :]
        for n in range(2):
            side[64 * n + 8 * band : 64 * n + 8 * band + 8, :] = sums[n]
    known[...] = jnp.broadcast_to(jnp.sum(side[...].T, axis=0, keepdims=True), (8, 128))


def through_kernel(
    own_y, y1, y2, y3, own_z, z1, z2, z3, own, other, keep, give, table_y, table_z
):
    index = lax.axis_index("gx")
    core, z, y = lax.rem(index, 2), lax.rem(lax.div(index, 2), 4), lax.div(index, 8)
    place(y, own_y, (y1, y2, y3), table_y)
    place(z, own_z, (z1, z2, z3), table_z)
    nothing = (jnp.zeros(own.shape[1:], F32),) * 3
    scale = 1000.0
    lo, hi = reach(y, [take(table_y.at[j]) for j in range(4)], nothing, nothing, scale)
    lo, hi = reach(z, [take(table_z.at[j]) for j in range(4)], lo, hi, scale)
    mine, theirs = take(own), take(other)
    first = choose(core == 0, mine, theirs)
    second = choose(core == 0, theirs, mine)
    at_first = flows(first, lo, past_down(hi, second, scale), scale)
    at_second = flows(second, past_up(lo, first, scale), hi, scale)
    keep[0], keep[1] = choose(core == 0, at_first, at_second)
    give[0], give[1] = choose(core == 0, at_second, at_first)


def y_port_kernel(keep, got, mixed, known, ends, port, flow, side):
    core = lax.rem(lax.axis_index("gx"), 2)
    for n in range(2):
        flow[n, : TILES // 2, :] = jnp.where(core == 0, keep[n], got[n])
        flow[n, TILES // 2 :, :] = jnp.where(core == 0, got[n], keep[n])
    sums = [None] * (2 * BANDS)
    for column in range(TILES):
        down, up = across(flow, column)
        for band in range(BANDS):
            at = pl.ds((band * TILES + column) * 8, 8)
            for n in range(2):
                part = up * mixed[2 * n + 1, at, :] - down * mixed[2 * n, at, :]
                sums[BANDS * n + band] = plus(sums[BANDS * n + band], part)
    for n, value in enumerate(sums):
        side[8 * n : 8 * n + 8, :] = value
    both = jnp.sum(side[...].T, axis=0, keepdims=True) + known[0:1, :]
    port[...] = jnp.zeros_like(port)
    port[0:1, :] = both
    port[1:2, :] = pltpu.roll(both, 64, 1)
    port[2:7, :] = ends[0:5, :]


def across(flow, column):
    return tuple(
        jnp.broadcast_to(flow[n, column : column + 1, :], (8, 128)) for n in range(2)
    )


def y_solve_kernel(source, lo, hi, flow, along, back, gain, sep, t, out, d, turned):
    def block(band, column):
        down, up = across(flow, column)
        x = flat_tile(source, band, column)
        return x - down * flat_tile(lo, band, column) + up * flat_tile(hi, band, column)

    to_runs(block, turned)

    def store(l, value):
        d[l] = value

    def cells(l):
        return cell(turned, l)

    solve(cells, Y_STEPS, Y_LEVELS, y_shift, along, back, gain, sep, d, store)
    for l in range(Y_STEPS):
        turned[pl.ds(l, 8, stride=128), :] = d[l]
    keep = put(out)

    def plus_start(band, column, value):
        keep(band, column, value + flat_tile(t, band, column))

    from_runs(turned, plus_start)


def finish_kernel(own, r1, r2, r3, base, y_lo, y_hi, out, table, side, done, sent):
    index = lax.axis_index("gy")
    place(index, own, (r1, r2, r3), table)
    lane = lax.broadcasted_iota(jnp.int32, (1, 128), 1)

    def port_of(ref):
        return tuple(jnp.where(lane < ROWS, ref[n : n + 1, :], 1.0) for n in range(7))

    nothing = (jnp.zeros((1, 128), F32),) * 3
    scale = 4000.0
    lo, hi = reach(index, [port_of(table.at[j]) for j in range(4)], nothing, nothing, scale)
    f_lo, f_hi = flows(port_of(own), lo, hi, scale)
    side[...] = jnp.zeros_like(side)
    side[0:1, :] = f_lo
    side[1:2, :] = f_hi
    upright = side[...].T
    copies = []
    for band in range(BANDS):
        at = slice(8 * band, 8 * band + 8)
        down = jnp.broadcast_to(upright[at, 0:1], (8, 128))
        up = jnp.broadcast_to(upright[at, 1:2], (8, 128))
        keep = put(done)
        for column in range(TILES):
            part = tile(base, band, column)
            part = part - down * tile(y_lo, band, column) + up * tile(y_hi, band, column)
            keep(band, column, part)
        copy = pltpu.make_async_copy(done.at[at, :], out.at[at, :], sent.at[band])
        copy.start()
        copies.append(copy)
    for copy in copies:
        copy.wait()


def around(value, axis, size, stride, step):
    pairs = []
    for i in range(size):
        digit = (i // stride) % 4
        pairs.append((i, i + ((digit ^ step) - digit) * stride))
    return lax.ppermute(value, axis, pairs)


def per_device(initial_heat_state, thermal_coefficient):
    t, k = initial_heat_state[0], thermal_coefficient[0]
    natural = struct(ROWS, COLS)
    t, k, own_lo, own_hi, own_edges = call(
        load_kernel,
        [natural, natural] + [struct(8, 128)] * 3,
        [pltpu.SemaphoreType.DMA((2, BANDS))],
        name="load",
        grant=GRANT,
        in_specs=[HBM, HBM],
        out_specs=[VMEM] * 5,
    )(t, k)
    below = lax.ppermute(own_hi, "gy", [(i, (i + 1) % 4) for i in range(4)])
    above = lax.ppermute(own_lo, "gy", [((i + 1) % 4, i) for i in range(4)])
    flat = struct(BANDS * TILES * 8, 128)
    runs = struct(TILES // 2 * 128, 128)
    x_field, y_field = struct(ROWS, TILES, 128), struct(Y_STEPS, 8, 128)
    x_port = struct(7, TILES, 128)
    e, *x_coefficients, x_lo, x_hi, x_ends, t_flat, k_flat = call(
        x_matrix_kernel,
        [
            flat,
            x_field,
            x_field,
            x_field,
            struct((2 * X_LEVELS + 1) * SEGMENTS, TILES, 128),
            x_field,
            x_field,
            x_port,
            flat,
            flat,
        ],
        name="x_matrix",
    )(t, k)
    *y_coefficients, y_lo, y_hi, y_ends = call(
        y_matrix_kernel,
        [
            y_field,
            y_field,
            y_field,
            struct((2 * Y_LEVELS + 1) * SEGMENTS, 8, 128),
            y_field,
            y_field,
            struct(8, 128),
        ],
        [scratch(runs)],
        name="y_matrix",
    )(k)
    below, above, y_lo = lax.optimization_barrier((below, above, y_lo))
    half = struct(7, TILES // 2, 128)
    own, give, edge = call(
        x_port_kernel,
        [half, half, struct(ROWS, 128)],
        [scratch(x_port), pltpu.VMEM((128, 128), F32)],
        flops=200_000,
        name="x_port",
    )(x_ends, x_lo, x_hi, own_edges, below, above)
    u = call(x_solve_kernel, x_field, [scratch(flat)], flops=700_000, name="x_solve")(
        e, *x_coefficients, edge
    )
    pairs = [(i, i ^ 1) for i in range(32)]
    other = lax.ppermute(give, "gx", pairs)
    other, u = lax.optimization_barrier((other, u))
    own_z = call(pair_kernel, half, name="pair")(own, other)
    from_z = [around(own_z, "gx", 32, 2, s) for s in RING]
    flat_lo, flat_hi = call(
        upright_kernel,
        [natural, natural],
        [pltpu.VMEM((2, TILES // 2 * 128, 128), F32)],
        name="upright",
    )(y_lo, y_hi)
    *from_z, flat_lo = lax.optimization_barrier((*from_z, flat_lo))
    table = pltpu.VMEM((4, 7, TILES // 2, 128), F32)
    own_y = call(four_kernel, half, [table], name="four")(own_z, *from_z)
    from_y = [around(own_y, "gx", 32, 8, s) for s in RING]
    square = pltpu.VMEM((128, 128), F32)
    source, lo_flat, hi_flat, mixed, known = call(
        blend_kernel,
        [flat, flat, flat, struct(4, BANDS * TILES * 8, 128), struct(8, 128)],
        [scratch(flat), square],
        name="blend",
    )(u, x_lo, x_hi, flat_lo, flat_hi, t_flat)
    some = struct(2, TILES // 2, 128)
    keep, give = call(through_kernel, [some, some], [table, table], name="through")(
        own_y, *from_y, own_z, *from_z, own, other
    )
    got = lax.ppermute(give, "gx", pairs)
    port, flow = call(
        y_port_kernel, [struct(8, 128), struct(2, TILES, 128)], [square], name="y_port"
    )(keep, got, mixed, known, y_ends)
    from_gy = [around(port, "gy", 4, 1, s) for s in RING]
    base = call(
        y_solve_kernel, natural, [scratch(y_field), scratch(runs)], name="y_solve"
    )(source, lo_flat, hi_flat, flow, *y_coefficients, t_flat)
    updated = call(
        finish_kernel,
        natural,
        [
            pltpu.VMEM((4, 8, 128), F32),
            pltpu.VMEM((128, 128), F32),
            scratch(natural),
            pltpu.SemaphoreType.DMA((BANDS,)),
        ],
        name="finish",
        in_specs=[VMEM] * 7,
        out_specs=HBM,
    )(port, *from_gy, base, flat_lo, flat_hi)
    return updated[None]


def solution(mesh):
    placed = (P(None, "gx", "gy"), P(None, "gx", "gy"))
    return jax.shard_map(
        per_device, mesh=mesh, in_specs=placed, out_specs=P(None, "gx", "gy"), check_vma=False
    )
```

```python
import jax
import jax.numpy as jnp
from jax import lax
from jax.experimental import pallas as pl
from jax.experimental.pallas import tpu as pltpu
from jax.sharding import PartitionSpec as P

ROWS, COLS = 64, 2048
BANDS, TILES = ROWS // 8, COLS // 128
SEGMENTS = 4
Y_STEPS = 128
X_LEVELS, Y_LEVELS = 2, 6
GRANT = (527 << 20) // 10
RING, LAST_RING = (2, 3, 1), (1, 2, 3)
F32 = jnp.float32
VMEM = pl.BlockSpec(memory_space=pltpu.VMEM)
HBM = pl.BlockSpec(memory_space=pltpu.MemorySpace.HBM)


def struct(*shape):
    return jax.ShapeDtypeStruct(shape, F32)


def scratch(like):
    return pltpu.VMEM(like.shape, like.dtype)


def whole(outs, args):
    return dict(in_specs=[VMEM] * len(args), out_specs=jax.tree.map(lambda _: VMEM, outs))


def call(kernel, outs, buffers=(), flops=2_000_000, name=None, grant=32 << 20, **windows):
    def run(*args):
        return pl.pallas_call(
            kernel,
            out_shape=outs,
            **(windows or whole(outs, args)),
            scratch_shapes=list(buffers),
            compiler_params=pltpu.CompilerParams(vmem_limit_bytes=grant),
            cost_estimate=pl.CostEstimate(flops=flops, bytes_accessed=1 << 20, transcendentals=0),
            name=name,
        )(*args)

    return run


def moved(chain, by, shift):
    out = []
    for s in range(SEGMENTS):
        runs, at = divmod(s + by, SEGMENTS)
        out.append(shift(chain[at], runs) if runs else chain[at])
    return out


def factor(link, n, levels, shift, along, back, gain, sep):
    m = n // SEGMENTS
    near = [link(s * m) for s in range(SEGMENTS)]
    ground = [jnp.ones_like(near[0])] * SEGMENTS
    held = [jnp.ones_like(near[0])] * SEGMENTS
    for step in range(1, m):
        for s in range(SEGMENTS):
            l = s * m + step
            v = link(l)
            r = 1.0 / (near[s] + ground[s] + v)
            t = v * r
            c = near[s] * r
            along[l], back[l], gain[l] = t, c, r
            held[s] = held[s] + ground[s] * c
            near[s] = near[s] * t
            ground[s] = ground[s] * t
            if step < m - 1:
                ground[s] = ground[s] + 1.0
    before = moved(ground, -1, shift)
    own = [held[s] + before[s] for s in range(SEGMENTS)]
    up = near
    down = moved(near, -1, shift)
    for level in range(levels):
        stride = 1 << level
        r = [1.0 / (own[s] + up[s] + down[s]) for s in range(SEGMENTS)]
        r_down, r_up = moved(r, -stride, shift), moved(r, stride, shift)
        own_down, own_up = moved(own, -stride, shift), moved(own, stride, shift)
        down_down, up_up = moved(down, -stride, shift), moved(up, stride, shift)
        for s in range(SEGMENTS):
            a, b = down[s] * r_down[s], up[s] * r_up[s]
            sep[(level * 2) * SEGMENTS + s] = a
            sep[(level * 2 + 1) * SEGMENTS + s] = b
            own[s] = own[s] + a * own_down[s] + b * own_up[s]
            down[s], up[s] = a * down_down[s], b * up_up[s]
    for s in range(SEGMENTS):
        sep[levels * 2 * SEGMENTS + s] = 1.0 / own[s]


def plus(a, b):
    return b if a is None else a if b is None else a + b


def times(a, b):
    return None if a is None else a * b


def solve(source, n, levels, shift, along, back, gain, sep, part, store):
    m = n // SEGMENTS
    total = [source(s * m) for s in range(SEGMENTS)]
    z = [source(s * m + 1) for s in range(SEGMENTS)]
    zero = [[False] * SEGMENTS for _ in range(m)]
    for step in range(1, m):
        for s in range(SEGMENTS):
            l = s * m + step
            zero[step][s] = z[s] is None
            if z[s] is not None:
                part[l] = z[s] * gain[l]
                total[s] = plus(total[s], z[s] * back[l])
                z[s] = z[s] * along[l]
            if step < m - 1:
                z[s] = plus(source(l + 1), z[s])
    shape = jnp.zeros(along.shape[1:], F32)
    z = [shape if v is None else v for v in z]
    before = moved(z, -1, shift)
    total = [plus(total[s], before[s]) for s in range(SEGMENTS)]
    for level in range(levels):
        stride = 1 << level
        lo, hi = moved(total, -stride, shift), moved(total, stride, shift)
        total = [
            total[s]
            + sep[(level * 2) * SEGMENTS + s] * lo[s]
            + sep[(level * 2 + 1) * SEGMENTS + s] * hi[s]
            for s in range(SEGMENTS)
        ]
    value = [total[s] * sep[levels * 2 * SEGMENTS + s] for s in range(SEGMENTS)]
    after = moved(value, 1, shift)
    for s in range(SEGMENTS):
        store(s * m, value[s])
    for step in reversed(range(1, m)):
        for s in range(SEGMENTS):
            l = s * m + step
            known = back[l] * value[s]
            if not zero[step][s]:
                known = known + part[l]
            after[s] = known + along[l] * after[s]
            store(l, after[s])


def x_shift(value, runs):
    return value


def y_shift(value, runs):
    if runs % 2 == 0:
        return pltpu.roll(value, (-(runs // 2)) % 8, 0)
    swapped = pltpu.roll(value, 64, 1)
    late = lax.broadcasted_iota(jnp.int32, value.shape, 1) >= 64
    if runs == 1:
        return jnp.where(late, pltpu.roll(swapped, 7, 0), swapped)
    return jnp.where(late, swapped, pltpu.roll(swapped, 1, 0))


def tile(ref, band, column):
    return ref[8 * band : 8 * band + 8, 128 * column : 128 * column + 128]


def flat_tile(ref, band, column):
    at = (band * TILES + column) * 8
    return ref[at : at + 8, :]


def row(ref, i):
    return ref[pl.ds((i // 8) * (8 * TILES) + i % 8, TILES, stride=8), :]


def load_kernel(t_far, k_far, t, k, lo, hi, own, arrived):
    copies = []
    for band in range(BANDS):
        at = pl.ds(8 * band, 8)
        for n, (far, near) in enumerate(((t_far, t), (k_far, k))):
            copy = pltpu.make_async_copy(far.at[at, :], near.at[at, :], arrived.at[n, band])
            copy.start()
            copies.append(copy)
    for ref in (lo, hi, own):
        ref[...] = jnp.zeros_like(ref)
    for copy in copies:
        copy.wait()
    for n, (ref, column) in enumerate(((t, 0), (k, 0), (t, TILES - 1), (k, TILES - 1))):
        strip = ref[:, 128 * column : 128 * column + 128].T
        at = 127 if column else 0
        edge = strip[at : at + 1, :]
        own[n : n + 1, 0:ROWS] = edge
        (hi if column else lo)[n % 2 : n % 2 + 1, 0:ROWS] = edge


def total(terms):
    sums = [None] * 4
    for n, term in enumerate(terms):
        sums[n % 4] = plus(sums[n % 4], term)
    return (sums[0] + sums[1]) + (sums[2] + sums[3])


def x_matrix_kernel(t, k, e, along, back, gain, sep, lo, hi, ends, t_flat, flat):
    lane = lax.broadcasted_iota(jnp.int32, (8, 128), 1)
    for band in range(BANDS):
        ks = [tile(k, band, c) for c in range(TILES)]
        ts = [tile(t, band, c) for c in range(TILES)]
        k_left = [pltpu.roll(v, 127, 1) for v in ks]
        t_left = [pltpu.roll(v, 127, 1) for v in ts]
        flow = []
        for c in range(TILES):
            at = pl.ds((band * TILES + c) * 8, 8)
            flat[at, :] = ks[c]
            t_flat[at, :] = ts[c]
            n = min(c + 1, TILES - 1)
            k_next = jnp.where(lane == 127, k_left[n], k_left[c])
            t_next = jnp.where(lane == 127, t_left[n], t_left[c])
            f = 8000.0 * (ks[c] + k_next) * (t_next - ts[c])
            if c == TILES - 1:
                f = jnp.where(lane == 127, 0.0, f)
            flow.append(f)
        turned = [pltpu.roll(v, 1, 1) for v in flow]
        for c in range(TILES):
            at = pl.ds((band * TILES + c) * 8, 8)
            first = turned[c - 1] if c else jnp.zeros_like(turned[0])
            f_before = jnp.where(lane == 0, first, turned[c])
            e[at, :] = 2.0 * ts[c] + (flow[c] - f_before)

    def link(l):
        if l == ROWS - 1:
            return jnp.zeros((TILES, 128), F32)
        return 1000.0 * (row(flat, l) + row(flat, l + 1))

    factor(link, ROWS, X_LEVELS, x_shift, along, back, gain, sep)
    one = jnp.ones((TILES, 128), F32)

    def at_start(l):
        return one if l == 0 else None

    def at_end(l):
        return one if l == ROWS - 1 else None

    def to(ref):
        def store(l, value):
            ref[l] = value

        return store

    args = (ROWS, X_LEVELS, x_shift, along, back, gain, sep)
    solve(at_start, *args, lo, to(lo))
    solve(at_end, *args, hi, to(hi))
    ends[0] = total(lo[i] * row(e, i) for i in range(ROWS))
    ends[1] = total(hi[i] * row(e, i) for i in range(ROWS))
    ends[2] = lo[0]
    ends[3] = lo[ROWS - 1]
    ends[4] = hi[ROWS - 1]
    ends[5] = row(flat, 0)
    ends[6] = row(flat, ROWS - 1)


def x_port_kernel(ends, lo, hi, own, below, above, port, edge, side):
    at = lax.axis_index("gy")
    side[...] = jnp.zeros_like(side)
    t_lo, k_lo, t_hi, k_hi = (own[n : n + 1, :] for n in range(4))
    before = jnp.where(at == 0, 0.0, below[...])
    after = jnp.where(at == lax.axis_size("gy") - 1, 0.0, above[...])
    side[0:1, :] = -8000.0 * (k_lo + before[1:2, :]) * (t_lo - before[0:1, :])
    side[127:128, :] = 8000.0 * (k_hi + after[1:2, :]) * (after[0:1, :] - t_hi)
    edge[...] = side[...].T[0:ROWS, :]
    lane = lax.broadcasted_iota(jnp.int32, (1, 128), 1)
    for n, response in enumerate((lo, hi)):
        port[n] = ends[n]
        for column, kept in ((0, 0), (TILES - 1, 127)):
            term = edge[...] * response[:, column, :]
            term = jnp.where(lane == kept, jnp.sum(term, axis=0, keepdims=True), 0.0)
            port[n, column : column + 1, :] = port[n, column : column + 1, :] + term
    for n in range(2, 7):
        port[n] = ends[n]


def x_solve_kernel(e, along, back, gain, sep, edge, u, flat):
    lane = lax.broadcasted_iota(jnp.int32, (8, 128), 1)
    flat[...] = e[...]
    for band in range(BANDS):
        part = edge[8 * band : 8 * band + 8, :]
        at = pl.ds(band * TILES * 8, 8)
        flat[at, :] = flat[at, :] + jnp.where(lane == 0, part, 0.0)
        at = pl.ds((band * TILES + TILES - 1) * 8, 8)
        flat[at, :] = flat[at, :] + jnp.where(lane == 127, part, 0.0)

    def store(l, value):
        u[l] = value

    def source(l):
        return row(flat, l)

    solve(source, ROWS, X_LEVELS, x_shift, along, back, gain, sep, u, store)


def take(ref):
    return tuple(ref[n] for n in range(7))


def join(one, two, scale):
    a1, b1, al1, be1, ga1, kf1, kl1 = one
    a2, b2, al2, be2, ga2, kf2, kl2 = two
    rho = 1.0 / (1.0 / (scale * (kl1 + kf2)) + al2 + ga1)
    delta = (a2 - b1) * rho
    return (
        a1 + be1 * delta,
        b2 - be2 * delta,
        al1 - be1 * be1 * rho,
        be1 * be2 * rho,
        ga2 - be2 * be2 * rho,
        kf1,
        kl2,
    )


def past_up(state, port, scale):
    p, q, k = state
    a, b, al, be, ga, kf, kl = port
    w = be / (1.0 / (scale * (k + kf)) + al + q)
    return (b - w * (a - p), ga - w * be, kl)


def past_down(state, port, scale):
    p, q, k = state
    a, b, al, be, ga, kf, kl = port
    w = be / (1.0 / (scale * (k + kl)) + ga + q)
    return (a + w * (p - b), al - w * be, kf)


def choose(condition, new, old):
    return tuple(jnp.where(condition, x, y) for x, y in zip(new, old))


def reach(index, ports, lo, hi, scale):
    count = len(ports)
    for n in range(count - 1):
        lo = choose(n < index, past_up(lo, ports[n], scale), lo)
    for n in reversed(range(1, count)):
        hi = choose(n > index, past_down(hi, ports[n], scale), hi)
    return lo, hi


def flows(port, lo, hi, scale):
    a, b, al, be, ga, kf, kl = port
    d_lo = 1.0 / (scale * (lo[2] + kf)) + al + lo[1]
    d_hi = 1.0 / (scale * (hi[2] + kl)) + ga + hi[1]
    c_lo, c_hi = a - lo[0], hi[0] - b
    inverse = 1.0 / (d_lo * d_hi - be * be)
    return (d_hi * c_lo + be * c_hi) * inverse, (d_lo * c_hi + be * c_lo) * inverse


def place(index, own, received, table, ring=RING):
    table[index] = own[...]
    for s, value in zip(ring, received):
        table[lax.bitwise_xor(index, s)] = value[...]


def pair_kernel(own, other, out):
    core = lax.rem(lax.axis_index("gx"), 2)
    mine, theirs = take(own), take(other)
    first = choose(core == 0, mine, theirs)
    second = choose(core == 0, theirs, mine)
    for n, value in enumerate(join(first, second, 1000.0)):
        out[n] = value


def four_kernel(own, r1, r2, r3, out, table):
    z = lax.rem(lax.div(lax.axis_index("gx"), 2), 4)
    place(z, own, (r1, r2, r3), table)
    ports = [take(table.at[j]) for j in range(4)]
    joined = join(join(ports[0], ports[1], 1000.0), join(ports[2], ports[3], 1000.0), 1000.0)
    for n, value in enumerate(joined):
        out[n] = value


def to_runs(blocks, out):
    for p in range(TILES // 2):
        stack = [blocks(band, 2 * p + half) for half in range(2) for band in range(BANDS)]
        out[128 * p : 128 * p + 128, :] = jnp.concatenate(stack, axis=0).T


def cell(ref, l):
    return ref[pl.ds(l, 8, stride=128), :]


def from_runs(turned, store):
    for p in range(TILES // 2):
        block = turned[128 * p : 128 * p + 128, :].T
        for half in range(2):
            for band in range(BANDS):
                at = ROWS * half + 8 * band
                store(band, 2 * p + half, block[at : at + 8, :])


def put(ref):
    def store(band, column, value):
        ref[8 * band : 8 * band + 8, 128 * column : 128 * column + 128] = value

    return store


def y_matrix_kernel(k, along, back, gain, sep, lo, hi, ends, turned):
    to_runs(lambda band, column: tile(k, band, column), turned)
    lane = lax.broadcasted_iota(jnp.int32, (8, 128), 1)
    sublane = lax.broadcasted_iota(jnp.int32, (8, 128), 0)
    very_last = (lane >= 64) & (sublane == 7)
    very_first = (lane < 64) & (sublane == 0)

    def link(l):
        if l == Y_STEPS - 1:
            both = 4000.0 * (cell(turned, l) + y_shift(cell(turned, 0), 1))
            return jnp.where(very_last, 0.0, both)
        return 4000.0 * (cell(turned, l) + cell(turned, l + 1))

    factor(link, Y_STEPS, Y_LEVELS, y_shift, along, back, gain, sep)

    def at_start(l):
        return jnp.where(very_first, 1.0, 0.0) if l == 0 else None

    def at_end(l):
        return jnp.where(very_last, 1.0, 0.0) if l == Y_STEPS - 1 else None

    def to(ref):
        def store(l, value):
            ref[l] = value

        return store

    args = (Y_STEPS, Y_LEVELS, y_shift, along, back, gain, sep)
    solve(at_start, *args, lo, to(lo))
    solve(at_end, *args, hi, to(hi))
    last = Y_STEPS - 1
    ends[...] = jnp.zeros_like(ends)
    ends[0:1, :] = lo[0, 0:1, :]
    ends[1:2, :] = pltpu.roll(lo[last], 64, 1)[7:8, :]
    ends[2:3, :] = pltpu.roll(hi[last], 64, 1)[7:8, :]
    ends[3:4, :] = cell(turned, 0)[0:1, :]
    ends[4:5, :] = pltpu.roll(cell(turned, last), 64, 1)[7:8, :]


def upright_kernel(lo, hi, flat_lo, flat_hi, turned):
    for n, (response, flat) in enumerate(((lo, flat_lo), (hi, flat_hi))):
        for l in range(Y_STEPS):
            turned[n, pl.ds(l, 8, stride=128), :] = response[l]
        from_runs(turned.at[n], put(flat))


def blend_kernel(u, x_lo, x_hi, y_lo, y_hi, t, source, lo, hi, mixed, known, flat, side):
    for ref, out in ((u, flat), (x_lo, lo), (x_hi, hi)):
        for i in range(ROWS):
            at = pl.ds((i // 8) * (8 * TILES) + i % 8, TILES, stride=8)
            out[at, :] = ref[i]
    for band in range(BANDS):
        sums = [None, None]
        for column in range(TILES):
            at = pl.ds((band * TILES + column) * 8, 8)
            value = flat[at, :] - 2.0 * t[at, :]
            source[at, :] = value
            for n, response in enumerate((y_lo, y_hi)):
                r = tile(response, band, column)
                sums[n] = plus(sums[n], r * value)
                mixed[2 * n, at, :] = r * lo[at, :]
                mixed[2 * n + 1, at, :] = r * hi[at, :]
        for n in range(2):
            side[64 * n + 8 * band : 64 * n + 8 * band + 8, :] = sums[n]
    known[...] = jnp.broadcast_to(jnp.sum(side[...].T, axis=0, keepdims=True), (8, 128))


def y_port_kernel(
    own_y, y1, y2, y3, own_z, z1, z2, z3, own, other, mixed, known, ends,
    port, flow, table_y, table_z, side,
):
    index = lax.axis_index("gx")
    core, z, y = lax.rem(index, 2), lax.rem(lax.div(index, 2), 4), lax.div(index, 8)
    place(y, own_y, (y1, y2, y3), table_y)
    place(z, own_z, (z1, z2, z3), table_z)
    nothing = (jnp.zeros((TILES, 128), F32),) * 3
    scale = 1000.0
    lo, hi = reach(y, [take(table_y.at[j]) for j in range(4)], nothing, nothing, scale)
    lo, hi = reach(z, [take(table_z.at[j]) for j in range(4)], lo, hi, scale)
    mine, theirs = take(own), take(other)
    lo = choose(core == 1, past_up(lo, theirs, scale), lo)
    hi = choose(core == 0, past_down(hi, theirs, scale), hi)
    flow[0], flow[1] = flows(mine, lo, hi, scale)
    sums = [None] * (2 * BANDS)
    for column in range(TILES):
        down, up = across(flow, column)
        for band in range(BANDS):
            at = pl.ds((band * TILES + column) * 8, 8)
            for n in range(2):
                part = up * mixed[2 * n + 1, at, :] - down * mixed[2 * n, at, :]
                sums[BANDS * n + band] = plus(sums[BANDS * n + band], part)
    for n, value in enumerate(sums):
        side[8 * n : 8 * n + 8, :] = value
    both = jnp.sum(side[...].T, axis=0, keepdims=True) + known[0:1, :]
    port[...] = jnp.zeros_like(port)
    port[0:1, :] = both
    port[1:2, :] = pltpu.roll(both, 64, 1)
    port[2:7, :] = ends[0:5, :]


def across(flow, column):
    return tuple(
        jnp.broadcast_to(flow[n, column : column + 1, :], (8, 128)) for n in range(2)
    )


def y_solve_kernel(source, lo, hi, flow, along, back, gain, sep, t, out, d, turned):
    def block(band, column):
        down, up = across(flow, column)
        x = flat_tile(source, band, column)
        return x - down * flat_tile(lo, band, column) + up * flat_tile(hi, band, column)

    to_runs(block, turned)

    def store(l, value):
        d[l] = value

    def cells(l):
        return cell(turned, l)

    solve(cells, Y_STEPS, Y_LEVELS, y_shift, along, back, gain, sep, d, store)
    for l in range(Y_STEPS):
        turned[pl.ds(l, 8, stride=128), :] = d[l]
    keep = put(out)

    def plus_start(band, column, value):
        keep(band, column, value + flat_tile(t, band, column))

    from_runs(turned, plus_start)


def finish_kernel(own, r1, r2, r3, base, y_lo, y_hi, out, table, side, done, sent):
    index = lax.axis_index("gy")
    place(index, own, (r1, r2, r3), table, LAST_RING)
    lane = lax.broadcasted_iota(jnp.int32, (1, 128), 1)

    def port_of(ref):
        return tuple(jnp.where(lane < ROWS, ref[n : n + 1, :], 1.0) for n in range(7))

    nothing = (jnp.zeros((1, 128), F32),) * 3
    scale = 4000.0
    lo, hi = reach(index, [port_of(table.at[j]) for j in range(4)], nothing, nothing, scale)
    f_lo, f_hi = flows(port_of(own), lo, hi, scale)
    side[...] = jnp.zeros_like(side)
    side[0:1, :] = f_lo
    side[1:2, :] = f_hi
    upright = side[...].T
    copies = []
    for band in range(BANDS):
        at = slice(8 * band, 8 * band + 8)
        down = jnp.broadcast_to(upright[at, 0:1], (8, 128))
        up = jnp.broadcast_to(upright[at, 1:2], (8, 128))
        keep = put(done)
        for column in range(TILES):
            part = tile(base, band, column)
            part = part - down * tile(y_lo, band, column) + up * tile(y_hi, band, column)
            keep(band, column, part)
        copy = pltpu.make_async_copy(done.at[at, :], out.at[at, :], sent.at[band])
        copy.start()
        copies.append(copy)
    for copy in copies:
        copy.wait()


def around(value, axis, size, stride, step):
    pairs = []
    for i in range(size):
        digit = (i // stride) % 4
        pairs.append((i, i + ((digit ^ step) - digit) * stride))
    return lax.ppermute(value, axis, pairs)


def per_device(initial_heat_state, thermal_coefficient):
    t, k = initial_heat_state[0], thermal_coefficient[0]
    natural = struct(ROWS, COLS)
    t, k, own_lo, own_hi, own_edges = call(
        load_kernel,
        [natural, natural] + [struct(8, 128)] * 3,
        [pltpu.SemaphoreType.DMA((2, BANDS))],
        name="load",
        grant=GRANT,
        in_specs=[HBM, HBM],
        out_specs=[VMEM] * 5,
    )(t, k)
    below = lax.ppermute(own_hi, "gy", [(i, (i + 1) % 4) for i in range(4)])
    above = lax.ppermute(own_lo, "gy", [((i + 1) % 4, i) for i in range(4)])
    flat = struct(BANDS * TILES * 8, 128)
    runs = struct(TILES // 2 * 128, 128)
    x_field, y_field = struct(ROWS, TILES, 128), struct(Y_STEPS, 8, 128)
    x_port = struct(7, TILES, 128)
    e, *x_coefficients, x_lo, x_hi, x_ends, t_flat, k_flat = call(
        x_matrix_kernel,
        [
            flat,
            x_field,
            x_field,
            x_field,
            struct((2 * X_LEVELS + 1) * SEGMENTS, TILES, 128),
            x_field,
            x_field,
            x_port,
            flat,
            flat,
        ],
        name="x_matrix",
    )(t, k)
    *y_coefficients, y_lo, y_hi, y_ends = call(
        y_matrix_kernel,
        [
            y_field,
            y_field,
            y_field,
            struct((2 * Y_LEVELS + 1) * SEGMENTS, 8, 128),
            y_field,
            y_field,
            struct(8, 128),
        ],
        [scratch(runs)],
        name="y_matrix",
    )(k)
    below, above, y_lo = lax.optimization_barrier((below, above, y_lo))
    own, edge = call(
        x_port_kernel,
        [x_port, struct(ROWS, 128)],
        [pltpu.VMEM((128, 128), F32)],
        flops=200_000,
        name="x_port",
    )(x_ends, x_lo, x_hi, own_edges, below, above)
    u = call(x_solve_kernel, x_field, [scratch(flat)], flops=700_000, name="x_solve")(
        e, *x_coefficients, edge
    )
    other = lax.ppermute(own, "gx", [(i, i ^ 1) for i in range(32)])
    other, u = lax.optimization_barrier((other, u))
    own_z = call(pair_kernel, x_port, name="pair")(own, other)
    from_z = [around(own_z, "gx", 32, 2, s) for s in RING]
    flat_lo, flat_hi = call(
        upright_kernel,
        [natural, natural],
        [pltpu.VMEM((2, TILES // 2 * 128, 128), F32)],
        name="upright",
    )(y_lo, y_hi)
    *from_z, flat_lo = lax.optimization_barrier((*from_z, flat_lo))
    table = pltpu.VMEM((4, 7, TILES, 128), F32)
    own_y = call(four_kernel, x_port, [table], name="four")(own_z, *from_z)
    from_y = [around(own_y, "gx", 32, 8, s) for s in RING]
    square = pltpu.VMEM((128, 128), F32)
    source, lo_flat, hi_flat, mixed, known = call(
        blend_kernel,
        [flat, flat, flat, struct(4, BANDS * TILES * 8, 128), struct(8, 128)],
        [scratch(flat), square],
        name="blend",
    )(u, x_lo, x_hi, flat_lo, flat_hi, t_flat)
    port, flow = call(
        y_port_kernel,
        [struct(8, 128), struct(2, TILES, 128)],
        [table, table, square],
        name="y_port",
    )(own_y, *from_y, own_z, *from_z, own, other, mixed, known, y_ends)
    from_gy = [around(port, "gy", 4, 1, s) for s in LAST_RING]
    base = call(
        y_solve_kernel, natural, [scratch(y_field), scratch(runs)], name="y_solve"
    )(source, lo_flat, hi_flat, flow, *y_coefficients, t_flat)
    updated = call(
        finish_kernel,
        natural,
        [
            pltpu.VMEM((4, 8, 128), F32),
            pltpu.VMEM((128, 128), F32),
            scratch(natural),
            pltpu.SemaphoreType.DMA((BANDS,)),
        ],
        name="finish",
        in_specs=[VMEM] * 7,
        out_specs=HBM,
    )(port, *from_gy, base, flat_lo, flat_hi)
    return updated[None]


def solution(mesh):
    placed = (P(None, "gx", "gy"), P(None, "gx", "gy"))
    return jax.shard_map(
        per_device, mesh=mesh, in_specs=placed, out_specs=P(None, "gx", "gy"), check_vma=False
    )
```

```python
import jax
import jax.numpy as jnp
from jax import lax
from jax.experimental import pallas as pl
from jax.experimental.pallas import tpu as pltpu
from jax.sharding import PartitionSpec as P

ROWS, COLS = 64, 2048
BANDS, TILES = ROWS // 8, COLS // 128
SEGMENTS = 4
Y_STEPS = 128
X_LEVELS, Y_LEVELS = 2, 6
GRANT = (527 << 20) // 10
RING, LAST_RING = (2, 3, 1), (1, 2, 3)
F32 = jnp.float32
VMEM = pl.BlockSpec(memory_space=pltpu.VMEM)
HBM = pl.BlockSpec(memory_space=pltpu.MemorySpace.HBM)


def struct(*shape):
    return jax.ShapeDtypeStruct(shape, F32)


def scratch(like):
    return pltpu.VMEM(like.shape, like.dtype)


def whole(outs, args):
    return dict(in_specs=[VMEM] * len(args), out_specs=jax.tree.map(lambda _: VMEM, outs))


def call(kernel, outs, buffers=(), flops=2_000_000, name=None, grant=32 << 20, **windows):
    def run(*args):
        return pl.pallas_call(
            kernel,
            out_shape=outs,
            **(windows or whole(outs, args)),
            scratch_shapes=list(buffers),
            compiler_params=pltpu.CompilerParams(vmem_limit_bytes=grant),
            cost_estimate=pl.CostEstimate(flops=flops, bytes_accessed=1 << 20, transcendentals=0),
            name=name,
        )(*args)

    return run


def moved(chain, by, shift):
    out = []
    for s in range(SEGMENTS):
        runs, at = divmod(s + by, SEGMENTS)
        out.append(shift(chain[at], runs) if runs else chain[at])
    return out


def factor(link, n, levels, shift, along, back, gain, sep):
    m = n // SEGMENTS
    near = [link(s * m) for s in range(SEGMENTS)]
    ground = [jnp.ones_like(near[0])] * SEGMENTS
    held = [jnp.ones_like(near[0])] * SEGMENTS
    for step in range(1, m):
        for s in range(SEGMENTS):
            l = s * m + step
            v = link(l)
            r = 1.0 / (near[s] + ground[s] + v)
            t = v * r
            c = near[s] * r
            along[l], back[l], gain[l] = t, c, r
            held[s] = held[s] + ground[s] * c
            near[s] = near[s] * t
            ground[s] = ground[s] * t
            if step < m - 1:
                ground[s] = ground[s] + 1.0
    before = moved(ground, -1, shift)
    own = [held[s] + before[s] for s in range(SEGMENTS)]
    up = near
    down = moved(near, -1, shift)
    for level in range(levels):
        stride = 1 << level
        r = [1.0 / (own[s] + up[s] + down[s]) for s in range(SEGMENTS)]
        r_down, r_up = moved(r, -stride, shift), moved(r, stride, shift)
        own_down, own_up = moved(own, -stride, shift), moved(own, stride, shift)
        down_down, up_up = moved(down, -stride, shift), moved(up, stride, shift)
        for s in range(SEGMENTS):
            a, b = down[s] * r_down[s], up[s] * r_up[s]
            sep[(level * 2) * SEGMENTS + s] = a
            sep[(level * 2 + 1) * SEGMENTS + s] = b
            own[s] = own[s] + a * own_down[s] + b * own_up[s]
            down[s], up[s] = a * down_down[s], b * up_up[s]
    for s in range(SEGMENTS):
        sep[levels * 2 * SEGMENTS + s] = 1.0 / own[s]


def plus(a, b):
    return b if a is None else a if b is None else a + b


def times(a, b):
    return None if a is None else a * b


def solve(source, n, levels, shift, along, back, gain, sep, part, store):
    m = n // SEGMENTS
    total = [source(s * m) for s in range(SEGMENTS)]
    z = [source(s * m + 1) for s in range(SEGMENTS)]
    zero = [[False] * SEGMENTS for _ in range(m)]
    for step in range(1, m):
        for s in range(SEGMENTS):
            l = s * m + step
            zero[step][s] = z[s] is None
            if z[s] is not None:
                part[l] = z[s] * gain[l]
                total[s] = plus(total[s], z[s] * back[l])
                z[s] = z[s] * along[l]
            if step < m - 1:
                z[s] = plus(source(l + 1), z[s])
    shape = jnp.zeros(along.shape[1:], F32)
    z = [shape if v is None else v for v in z]
    before = moved(z, -1, shift)
    total = [plus(total[s], before[s]) for s in range(SEGMENTS)]
    for level in range(levels):
        stride = 1 << level
        lo, hi = moved(total, -stride, shift), moved(total, stride, shift)
        total = [
            total[s]
            + sep[(level * 2) * SEGMENTS + s] * lo[s]
            + sep[(level * 2 + 1) * SEGMENTS + s] * hi[s]
            for s in range(SEGMENTS)
        ]
    value = [total[s] * sep[levels * 2 * SEGMENTS + s] for s in range(SEGMENTS)]
    after = moved(value, 1, shift)
    for s in range(SEGMENTS):
        store(s * m, value[s])
    for step in reversed(range(1, m)):
        for s in range(SEGMENTS):
            l = s * m + step
            known = back[l] * value[s]
            if not zero[step][s]:
                known = known + part[l]
            after[s] = known + along[l] * after[s]
            store(l, after[s])


def x_shift(value, runs):
    return value


def y_shift(value, runs):
    if runs % 2 == 0:
        return pltpu.roll(value, (-(runs // 2)) % 8, 0)
    swapped = pltpu.roll(value, 64, 1)
    late = lax.broadcasted_iota(jnp.int32, value.shape, 1) >= 64
    if runs == 1:
        return jnp.where(late, pltpu.roll(swapped, 7, 0), swapped)
    return jnp.where(late, swapped, pltpu.roll(swapped, 1, 0))


def tile(ref, band, column):
    return ref[8 * band : 8 * band + 8, 128 * column : 128 * column + 128]


def flat_tile(ref, band, column):
    at = (band * TILES + column) * 8
    return ref[at : at + 8, :]


def row(ref, i):
    return ref[pl.ds((i // 8) * (8 * TILES) + i % 8, TILES, stride=8), :]


def load_kernel(t_far, k_far, t, k, one, three, own, arrived):
    copies = []
    for band in range(BANDS):
        at = pl.ds(8 * band, 8)
        for n, (far, near) in enumerate(((t_far, t), (k_far, k))):
            copy = pltpu.make_async_copy(far.at[at, :], near.at[at, :], arrived.at[n, band])
            copy.start()
            copies.append(copy)
    for ref in (one, three, own):
        ref[...] = jnp.zeros_like(ref)
    for copy in copies:
        copy.wait()
    edges = []
    for n, (ref, column) in enumerate(((t, 0), (k, 0), (t, TILES - 1), (k, TILES - 1))):
        strip = ref[:, 128 * column : 128 * column + 128].T
        at = 127 if column else 0
        edges.append(strip[at : at + 1, :])
        own[n : n + 1, 0:ROWS] = edges[n]
    even = lax.rem(lax.axis_index("gy"), 2) == 0
    for n in range(2):
        lo, hi = edges[n], edges[2 + n]
        one[n : n + 1, 0:ROWS] = jnp.where(even, hi, lo)
        three[n : n + 1, 0:ROWS] = jnp.where(even, lo, hi)


def total(terms):
    sums = [None] * 4
    for n, term in enumerate(terms):
        sums[n % 4] = plus(sums[n % 4], term)
    return (sums[0] + sums[1]) + (sums[2] + sums[3])


def x_matrix_kernel(t, k, e, along, back, gain, sep, lo, hi, ends, t_flat, flat):
    lane = lax.broadcasted_iota(jnp.int32, (8, 128), 1)
    for band in range(BANDS):
        ks = [tile(k, band, c) for c in range(TILES)]
        ts = [tile(t, band, c) for c in range(TILES)]
        k_left = [pltpu.roll(v, 127, 1) for v in ks]
        t_left = [pltpu.roll(v, 127, 1) for v in ts]
        flow = []
        for c in range(TILES):
            at = pl.ds((band * TILES + c) * 8, 8)
            flat[at, :] = ks[c]
            t_flat[at, :] = ts[c]
            n = min(c + 1, TILES - 1)
            k_next = jnp.where(lane == 127, k_left[n], k_left[c])
            t_next = jnp.where(lane == 127, t_left[n], t_left[c])
            f = 8000.0 * (ks[c] + k_next) * (t_next - ts[c])
            if c == TILES - 1:
                f = jnp.where(lane == 127, 0.0, f)
            flow.append(f)
        turned = [pltpu.roll(v, 1, 1) for v in flow]
        for c in range(TILES):
            at = pl.ds((band * TILES + c) * 8, 8)
            first = turned[c - 1] if c else jnp.zeros_like(turned[0])
            f_before = jnp.where(lane == 0, first, turned[c])
            e[at, :] = 2.0 * ts[c] + (flow[c] - f_before)

    def link(l):
        if l == ROWS - 1:
            return jnp.zeros((TILES, 128), F32)
        return 1000.0 * (row(flat, l) + row(flat, l + 1))

    factor(link, ROWS, X_LEVELS, x_shift, along, back, gain, sep)
    one = jnp.ones((TILES, 128), F32)

    def at_start(l):
        return one if l == 0 else None

    def at_end(l):
        return one if l == ROWS - 1 else None

    def to(ref):
        def store(l, value):
            ref[l] = value

        return store

    args = (ROWS, X_LEVELS, x_shift, along, back, gain, sep)
    solve(at_start, *args, lo, to(lo))
    solve(at_end, *args, hi, to(hi))
    ends[0] = total(lo[i] * row(e, i) for i in range(ROWS))
    ends[1] = total(hi[i] * row(e, i) for i in range(ROWS))
    ends[2] = lo[0]
    ends[3] = lo[ROWS - 1]
    ends[4] = hi[ROWS - 1]
    ends[5] = row(flat, 0)
    ends[6] = row(flat, ROWS - 1)


def x_port_kernel(ends, lo, hi, own, from_one, from_three, port, edge, side):
    at = lax.axis_index("gy")
    side[...] = jnp.zeros_like(side)
    t_lo, k_lo, t_hi, k_hi = (own[n : n + 1, :] for n in range(4))
    even = lax.rem(at, 2) == 0
    below = jnp.where(even, from_three[...], from_one[...])
    above = jnp.where(even, from_one[...], from_three[...])
    before = jnp.where(at == 0, 0.0, below)
    after = jnp.where(at == lax.axis_size("gy") - 1, 0.0, above)
    side[0:1, :] = -8000.0 * (k_lo + before[1:2, :]) * (t_lo - before[0:1, :])
    side[127:128, :] = 8000.0 * (k_hi + after[1:2, :]) * (after[0:1, :] - t_hi)
    edge[...] = side[...].T[0:ROWS, :]
    lane = lax.broadcasted_iota(jnp.int32, (1, 128), 1)
    for n, response in enumerate((lo, hi)):
        port[n] = ends[n]
        for column, kept in ((0, 0), (TILES - 1, 127)):
            term = edge[...] * response[:, column, :]
            term = jnp.where(lane == kept, jnp.sum(term, axis=0, keepdims=True), 0.0)
            port[n, column : column + 1, :] = port[n, column : column + 1, :] + term
    for n in range(2, 7):
        port[n] = ends[n]


def x_solve_kernel(e, along, back, gain, sep, edge, u, flat):
    lane = lax.broadcasted_iota(jnp.int32, (8, 128), 1)
    flat[...] = e[...]
    for band in range(BANDS):
        part = edge[8 * band : 8 * band + 8, :]
        at = pl.ds(band * TILES * 8, 8)
        flat[at, :] = flat[at, :] + jnp.where(lane == 0, part, 0.0)
        at = pl.ds((band * TILES + TILES - 1) * 8, 8)
        flat[at, :] = flat[at, :] + jnp.where(lane == 127, part, 0.0)

    def store(l, value):
        u[l] = value

    def source(l):
        return row(flat, l)

    solve(source, ROWS, X_LEVELS, x_shift, along, back, gain, sep, u, store)


def take(ref):
    return tuple(ref[n] for n in range(7))


def join(one, two, scale):
    a1, b1, al1, be1, ga1, kf1, kl1 = one
    a2, b2, al2, be2, ga2, kf2, kl2 = two
    rho = 1.0 / (1.0 / (scale * (kl1 + kf2)) + al2 + ga1)
    delta = (a2 - b1) * rho
    return (
        a1 + be1 * delta,
        b2 - be2 * delta,
        al1 - be1 * be1 * rho,
        be1 * be2 * rho,
        ga2 - be2 * be2 * rho,
        kf1,
        kl2,
    )


def past_up(state, port, scale):
    p, q, k = state
    a, b, al, be, ga, kf, kl = port
    w = be / (1.0 / (scale * (k + kf)) + al + q)
    return (b - w * (a - p), ga - w * be, kl)


def past_down(state, port, scale):
    p, q, k = state
    a, b, al, be, ga, kf, kl = port
    w = be / (1.0 / (scale * (k + kl)) + ga + q)
    return (a + w * (p - b), al - w * be, kf)


def choose(condition, new, old):
    return tuple(jnp.where(condition, x, y) for x, y in zip(new, old))


def reach(index, ports, lo, hi, scale):
    count = len(ports)
    for n in range(count - 1):
        lo = choose(n < index, past_up(lo, ports[n], scale), lo)
    for n in reversed(range(1, count)):
        hi = choose(n > index, past_down(hi, ports[n], scale), hi)
    return lo, hi


def flows(port, lo, hi, scale):
    a, b, al, be, ga, kf, kl = port
    d_lo = 1.0 / (scale * (lo[2] + kf)) + al + lo[1]
    d_hi = 1.0 / (scale * (hi[2] + kl)) + ga + hi[1]
    c_lo, c_hi = a - lo[0], hi[0] - b
    inverse = 1.0 / (d_lo * d_hi - be * be)
    return (d_hi * c_lo + be * c_hi) * inverse, (d_lo * c_hi + be * c_lo) * inverse


def place(index, own, received, table, ring=RING):
    table[index] = own[...]
    for s, value in zip(ring, received):
        table[lax.bitwise_xor(index, s)] = value[...]


def pair_kernel(own, other, out):
    core = lax.rem(lax.axis_index("gx"), 2)
    mine, theirs = take(own), take(other)
    first = choose(core == 0, mine, theirs)
    second = choose(core == 0, theirs, mine)
    for n, value in enumerate(join(first, second, 1000.0)):
        out[n] = value


def four_kernel(own, r1, r2, r3, out, table):
    z = lax.rem(lax.div(lax.axis_index("gx"), 2), 4)
    place(z, own, (r1, r2, r3), table)
    ports = [take(table.at[j]) for j in range(4)]
    joined = join(join(ports[0], ports[1], 1000.0), join(ports[2], ports[3], 1000.0), 1000.0)
    for n, value in enumerate(joined):
        out[n] = value


def to_runs(blocks, out):
    for p in range(TILES // 2):
        stack = [blocks(band, 2 * p + half) for half in range(2) for band in range(BANDS)]
        out[128 * p : 128 * p + 128, :] = jnp.concatenate(stack, axis=0).T


def cell(ref, l):
    return ref[pl.ds(l, 8, stride=128), :]


def from_runs(turned, store):
    for p in range(TILES // 2):
        block = turned[128 * p : 128 * p + 128, :].T
        for half in range(2):
            for band in range(BANDS):
                at = ROWS * half + 8 * band
                store(band, 2 * p + half, block[at : at + 8, :])


def put(ref):
    def store(band, column, value):
        ref[8 * band : 8 * band + 8, 128 * column : 128 * column + 128] = value

    return store


def y_matrix_kernel(k, along, back, gain, sep, lo, hi, ends, turned):
    to_runs(lambda band, column: tile(k, band, column), turned)
    lane = lax.broadcasted_iota(jnp.int32, (8, 128), 1)
    sublane = lax.broadcasted_iota(jnp.int32, (8, 128), 0)
    very_last = (lane >= 64) & (sublane == 7)
    very_first = (lane < 64) & (sublane == 0)

    def link(l):
        if l == Y_STEPS - 1:
            both = 4000.0 * (cell(turned, l) + y_shift(cell(turned, 0), 1))
            return jnp.where(very_last, 0.0, both)
        return 4000.0 * (cell(turned, l) + cell(turned, l + 1))

    factor(link, Y_STEPS, Y_LEVELS, y_shift, along, back, gain, sep)

    def at_start(l):
        return jnp.where(very_first, 1.0, 0.0) if l == 0 else None

    def at_end(l):
        return jnp.where(very_last, 1.0, 0.0) if l == Y_STEPS - 1 else None

    def to(ref):
        def store(l, value):
            ref[l] = value

        return store

    args = (Y_STEPS, Y_LEVELS, y_shift, along, back, gain, sep)
    solve(at_start, *args, lo, to(lo))
    solve(at_end, *args, hi, to(hi))
    last = Y_STEPS - 1
    ends[...] = jnp.zeros_like(ends)
    ends[0:1, :] = lo[0, 0:1, :]
    ends[1:2, :] = pltpu.roll(lo[last], 64, 1)[7:8, :]
    ends[2:3, :] = pltpu.roll(hi[last], 64, 1)[7:8, :]
    ends[3:4, :] = cell(turned, 0)[0:1, :]
    ends[4:5, :] = pltpu.roll(cell(turned, last), 64, 1)[7:8, :]


def upright_kernel(lo, hi, flat_lo, flat_hi, turned):
    for n, (response, flat) in enumerate(((lo, flat_lo), (hi, flat_hi))):
        for l in range(Y_STEPS):
            turned[n, pl.ds(l, 8, stride=128), :] = response[l]
        from_runs(turned.at[n], put(flat))


def blend_kernel(u, x_lo, x_hi, y_lo, y_hi, t, source, lo, hi, mixed, known, flat, side):
    for ref, out in ((u, flat), (x_lo, lo), (x_hi, hi)):
        for i in range(ROWS):
            at = pl.ds((i // 8) * (8 * TILES) + i % 8, TILES, stride=8)
            out[at, :] = ref[i]
    for band in range(BANDS):
        sums = [None, None]
        for column in range(TILES):
            at = pl.ds((band * TILES + column) * 8, 8)
            value = flat[at, :] - 2.0 * t[at, :]
            source[at, :] = value
            for n, response in enumerate((y_lo, y_hi)):
                r = tile(response, band, column)
                sums[n] = plus(sums[n], r * value)
                mixed[2 * n, at, :] = r * lo[at, :]
                mixed[2 * n + 1, at, :] = r * hi[at, :]
        for n in range(2):
            side[64 * n + 8 * band : 64 * n + 8 * band + 8, :] = sums[n]
    known[...] = jnp.broadcast_to(jnp.sum(side[...].T, axis=0, keepdims=True), (8, 128))


def y_port_kernel(
    own_y, y1, y2, y3, own_z, z1, z2, z3, own, other, mixed, known, ends,
    port, flow, table_y, table_z, side,
):
    index = lax.axis_index("gx")
    core, z, y = lax.rem(index, 2), lax.rem(lax.div(index, 2), 4), lax.div(index, 8)
    place(y, own_y, (y1, y2, y3), table_y)
    place(z, own_z, (z1, z2, z3), table_z)
    nothing = (jnp.zeros((TILES, 128), F32),) * 3
    scale = 1000.0
    lo, hi = reach(y, [take(table_y.at[j]) for j in range(4)], nothing, nothing, scale)
    lo, hi = reach(z, [take(table_z.at[j]) for j in range(4)], lo, hi, scale)
    mine, theirs = take(own), take(other)
    lo = choose(core == 1, past_up(lo, theirs, scale), lo)
    hi = choose(core == 0, past_down(hi, theirs, scale), hi)
    flow[0], flow[1] = flows(mine, lo, hi, scale)
    sums = [None] * (2 * BANDS)
    for column in range(TILES):
        down, up = across(flow, column)
        for band in range(BANDS):
            at = pl.ds((band * TILES + column) * 8, 8)
            for n in range(2):
                part = up * mixed[2 * n + 1, at, :] - down * mixed[2 * n, at, :]
                sums[BANDS * n + band] = plus(sums[BANDS * n + band], part)
    for n, value in enumerate(sums):
        side[8 * n : 8 * n + 8, :] = value
    both = jnp.sum(side[...].T, axis=0, keepdims=True) + known[0:1, :]
    port[...] = jnp.zeros_like(port)
    port[0:1, :] = both
    port[1:2, :] = pltpu.roll(both, 64, 1)
    port[2:7, :] = ends[0:5, :]


def across(flow, column):
    return tuple(
        jnp.broadcast_to(flow[n, column : column + 1, :], (8, 128)) for n in range(2)
    )


def y_solve_kernel(source, lo, hi, flow, along, back, gain, sep, t, out, d, turned):
    def block(band, column):
        down, up = across(flow, column)
        x = flat_tile(source, band, column)
        return x - down * flat_tile(lo, band, column) + up * flat_tile(hi, band, column)

    to_runs(block, turned)

    def store(l, value):
        d[l] = value

    def cells(l):
        return cell(turned, l)

    solve(cells, Y_STEPS, Y_LEVELS, y_shift, along, back, gain, sep, d, store)
    for l in range(Y_STEPS):
        turned[pl.ds(l, 8, stride=128), :] = d[l]
    keep = put(out)

    def plus_start(band, column, value):
        keep(band, column, value + flat_tile(t, band, column))

    from_runs(turned, plus_start)


def finish_kernel(own, r1, r2, r3, base, y_lo, y_hi, out, table, side, done, sent):
    index = lax.axis_index("gy")
    place(index, own, (r1, r2, r3), table, LAST_RING)
    lane = lax.broadcasted_iota(jnp.int32, (1, 128), 1)

    def port_of(ref):
        return tuple(jnp.where(lane < ROWS, ref[n : n + 1, :], 1.0) for n in range(7))

    nothing = (jnp.zeros((1, 128), F32),) * 3
    scale = 4000.0
    lo, hi = reach(index, [port_of(table.at[j]) for j in range(4)], nothing, nothing, scale)
    f_lo, f_hi = flows(port_of(own), lo, hi, scale)
    side[...] = jnp.zeros_like(side)
    side[0:1, :] = f_lo
    side[1:2, :] = f_hi
    upright = side[...].T
    copies = []
    for band in range(BANDS):
        at = slice(8 * band, 8 * band + 8)
        down = jnp.broadcast_to(upright[at, 0:1], (8, 128))
        up = jnp.broadcast_to(upright[at, 1:2], (8, 128))
        keep = put(done)
        for column in range(TILES):
            part = tile(base, band, column)
            part = part - down * tile(y_lo, band, column) + up * tile(y_hi, band, column)
            keep(band, column, part)
        copy = pltpu.make_async_copy(done.at[at, :], out.at[at, :], sent.at[band])
        copy.start()
        copies.append(copy)
    for copy in copies:
        copy.wait()


def around(value, axis, size, stride, step):
    pairs = []
    for i in range(size):
        digit = (i // stride) % 4
        pairs.append((i, i + ((digit ^ step) - digit) * stride))
    return lax.ppermute(value, axis, pairs)


def per_device(initial_heat_state, thermal_coefficient):
    t, k = initial_heat_state[0], thermal_coefficient[0]
    natural = struct(ROWS, COLS)
    t, k, to_one, to_three, own_edges = call(
        load_kernel,
        [natural, natural] + [struct(8, 128)] * 3,
        [pltpu.SemaphoreType.DMA((2, BANDS))],
        name="load",
        grant=GRANT,
        in_specs=[HBM, HBM],
        out_specs=[VMEM] * 5,
    )(t, k)
    from_three = around(to_three, "gy", 4, 1, 3)
    from_one = around(to_one, "gy", 4, 1, 1)
    flat = struct(BANDS * TILES * 8, 128)
    runs = struct(TILES // 2 * 128, 128)
    x_field, y_field = struct(ROWS, TILES, 128), struct(Y_STEPS, 8, 128)
    x_port = struct(7, TILES, 128)
    e, *x_coefficients, x_lo, x_hi, x_ends, t_flat, k_flat = call(
        x_matrix_kernel,
        [
            flat,
            x_field,
            x_field,
            x_field,
            struct((2 * X_LEVELS + 1) * SEGMENTS, TILES, 128),
            x_field,
            x_field,
            x_port,
            flat,
            flat,
        ],
        name="x_matrix",
    )(t, k)
    own, edge = call(
        x_port_kernel,
        [x_port, struct(ROWS, 128)],
        [pltpu.VMEM((128, 128), F32)],
        flops=200_000,
        name="x_port",
    )(x_ends, x_lo, x_hi, own_edges, from_one, from_three)
    u = call(x_solve_kernel, x_field, [scratch(flat)], flops=700_000, name="x_solve")(
        e, *x_coefficients, edge
    )
    other = lax.ppermute(own, "gx", [(i, i ^ 1) for i in range(32)])
    other, u = lax.optimization_barrier((other, u))
    own_z = call(pair_kernel, x_port, name="pair")(own, other)
    k_y, own_z = lax.optimization_barrier((k, own_z))
    from_z = [around(own_z, "gx", 32, 2, s) for s in RING]
    *y_coefficients, y_lo, y_hi, y_ends = call(
        y_matrix_kernel,
        [
            y_field,
            y_field,
            y_field,
            struct((2 * Y_LEVELS + 1) * SEGMENTS, 8, 128),
            y_field,
            y_field,
            struct(8, 128),
        ],
        [scratch(runs)],
        name="y_matrix",
    )(k_y)
    flat_lo, flat_hi = call(
        upright_kernel,
        [natural, natural],
        [pltpu.VMEM((2, TILES // 2 * 128, 128), F32)],
        name="upright",
    )(y_lo, y_hi)
    *from_z, flat_lo = lax.optimization_barrier((*from_z, flat_lo))
    table = pltpu.VMEM((4, 7, TILES, 128), F32)
    own_y = call(four_kernel, x_port, [table], name="four")(own_z, *from_z)
    from_y = [around(own_y, "gx", 32, 8, s) for s in RING]
    square = pltpu.VMEM((128, 128), F32)
    source, lo_flat, hi_flat, mixed, known = call(
        blend_kernel,
        [flat, flat, flat, struct(4, BANDS * TILES * 8, 128), struct(8, 128)],
        [scratch(flat), square],
        name="blend",
    )(u, x_lo, x_hi, flat_lo, flat_hi, t_flat)
    port, flow = call(
        y_port_kernel,
        [struct(8, 128), struct(2, TILES, 128)],
        [table, table, square],
        name="y_port",
    )(own_y, *from_y, own_z, *from_z, own, other, mixed, known, y_ends)
    from_gy = [around(port, "gy", 4, 1, s) for s in LAST_RING]
    base = call(
        y_solve_kernel, natural, [scratch(y_field), scratch(runs)], name="y_solve"
    )(source, lo_flat, hi_flat, flow, *y_coefficients, t_flat)
    updated = call(
        finish_kernel,
        natural,
        [
            pltpu.VMEM((4, 8, 128), F32),
            pltpu.VMEM((128, 128), F32),
            scratch(natural),
            pltpu.SemaphoreType.DMA((BANDS,)),
        ],
        name="finish",
        in_specs=[VMEM] * 7,
        out_specs=HBM,
    )(port, *from_gy, base, flat_lo, flat_hi)
    return updated[None]


def solution(mesh):
    placed = (P(None, "gx", "gy"), P(None, "gx", "gy"))
    return jax.shard_map(
        per_device, mesh=mesh, in_specs=placed, out_specs=P(None, "gx", "gy"), check_vma=False
    )
```

```python
import jax
import jax.numpy as jnp
from jax import lax
from jax.experimental import pallas as pl
from jax.experimental.pallas import tpu as pltpu
from jax.sharding import PartitionSpec as P

ROWS, COLS = 64, 2048
BANDS, TILES = ROWS // 8, COLS // 128
SEGMENTS = 4
Y_STEPS = 128
X_LEVELS, Y_LEVELS = 2, 6
GRANT = (527 << 20) // 10
RING, LAST_RING = (2, 3, 1), (1, 2, 3)
F32 = jnp.float32
VMEM = pl.BlockSpec(memory_space=pltpu.VMEM)
HBM = pl.BlockSpec(memory_space=pltpu.MemorySpace.HBM)


def struct(*shape):
    return jax.ShapeDtypeStruct(shape, F32)


def scratch(like):
    return pltpu.VMEM(like.shape, like.dtype)


def whole(outs, args):
    return dict(in_specs=[VMEM] * len(args), out_specs=jax.tree.map(lambda _: VMEM, outs))


def call(kernel, outs, buffers=(), flops=2_000_000, name=None, grant=32 << 20, **windows):
    def run(*args):
        return pl.pallas_call(
            kernel,
            out_shape=outs,
            **(windows or whole(outs, args)),
            scratch_shapes=list(buffers),
            compiler_params=pltpu.CompilerParams(vmem_limit_bytes=grant),
            cost_estimate=pl.CostEstimate(flops=flops, bytes_accessed=1 << 20, transcendentals=0),
            name=name,
        )(*args)

    return run


def moved(chain, by, shift):
    out = []
    for s in range(SEGMENTS):
        runs, at = divmod(s + by, SEGMENTS)
        out.append(shift(chain[at], runs) if runs else chain[at])
    return out


def factor(link, n, levels, shift, along, back, gain, sep):
    m = n // SEGMENTS
    near = [link(s * m) for s in range(SEGMENTS)]
    ground = [jnp.ones_like(near[0])] * SEGMENTS
    held = [jnp.ones_like(near[0])] * SEGMENTS
    for step in range(1, m):
        for s in range(SEGMENTS):
            l = s * m + step
            v = link(l)
            r = 1.0 / (near[s] + ground[s] + v)
            t = v * r
            c = near[s] * r
            along[l], back[l], gain[l] = t, c, r
            held[s] = held[s] + ground[s] * c
            near[s] = near[s] * t
            ground[s] = ground[s] * t
            if step < m - 1:
                ground[s] = ground[s] + 1.0
    before = moved(ground, -1, shift)
    own = [held[s] + before[s] for s in range(SEGMENTS)]
    up = near
    down = moved(near, -1, shift)
    for level in range(levels):
        stride = 1 << level
        r = [1.0 / (own[s] + up[s] + down[s]) for s in range(SEGMENTS)]
        r_down, r_up = moved(r, -stride, shift), moved(r, stride, shift)
        own_down, own_up = moved(own, -stride, shift), moved(own, stride, shift)
        down_down, up_up = moved(down, -stride, shift), moved(up, stride, shift)
        for s in range(SEGMENTS):
            a, b = down[s] * r_down[s], up[s] * r_up[s]
            sep[(level * 2) * SEGMENTS + s] = a
            sep[(level * 2 + 1) * SEGMENTS + s] = b
            own[s] = own[s] + a * own_down[s] + b * own_up[s]
            down[s], up[s] = a * down_down[s], b * up_up[s]
    for s in range(SEGMENTS):
        sep[levels * 2 * SEGMENTS + s] = 1.0 / own[s]


def plus(a, b):
    return b if a is None else a if b is None else a + b


def times(a, b):
    return None if a is None else a * b


def solve(source, n, levels, shift, along, back, gain, sep, part, store):
    m = n // SEGMENTS
    total = [source(s * m) for s in range(SEGMENTS)]
    z = [source(s * m + 1) for s in range(SEGMENTS)]
    zero = [[False] * SEGMENTS for _ in range(m)]
    for step in range(1, m):
        for s in range(SEGMENTS):
            l = s * m + step
            zero[step][s] = z[s] is None
            if z[s] is not None:
                part[l] = z[s] * gain[l]
                total[s] = plus(total[s], z[s] * back[l])
                z[s] = z[s] * along[l]
            if step < m - 1:
                z[s] = plus(source(l + 1), z[s])
    shape = jnp.zeros(along.shape[1:], F32)
    z = [shape if v is None else v for v in z]
    before = moved(z, -1, shift)
    total = [plus(total[s], before[s]) for s in range(SEGMENTS)]
    for level in range(levels):
        stride = 1 << level
        lo, hi = moved(total, -stride, shift), moved(total, stride, shift)
        total = [
            total[s]
            + sep[(level * 2) * SEGMENTS + s] * lo[s]
            + sep[(level * 2 + 1) * SEGMENTS + s] * hi[s]
            for s in range(SEGMENTS)
        ]
    value = [total[s] * sep[levels * 2 * SEGMENTS + s] for s in range(SEGMENTS)]
    after = moved(value, 1, shift)
    for s in range(SEGMENTS):
        store(s * m, value[s])
    for step in reversed(range(1, m)):
        for s in range(SEGMENTS):
            l = s * m + step
            known = back[l] * value[s]
            if not zero[step][s]:
                known = known + part[l]
            after[s] = known + along[l] * after[s]
            store(l, after[s])


def x_shift(value, runs):
    return value


def y_shift(value, runs):
    if runs % 2 == 0:
        return pltpu.roll(value, (-(runs // 2)) % 8, 0)
    swapped = pltpu.roll(value, 64, 1)
    late = lax.broadcasted_iota(jnp.int32, value.shape, 1) >= 64
    if runs == 1:
        return jnp.where(late, pltpu.roll(swapped, 7, 0), swapped)
    return jnp.where(late, swapped, pltpu.roll(swapped, 1, 0))


def tile(ref, band, column):
    return ref[8 * band : 8 * band + 8, 128 * column : 128 * column + 128]


def flat_tile(ref, band, column):
    at = (band * TILES + column) * 8
    return ref[at : at + 8, :]


def row(ref, i):
    return ref[pl.ds((i // 8) * (8 * TILES) + i % 8, TILES, stride=8), :]


def load_kernel(t_far, k_far, t, k, lo, hi, own, strips, early, arrived):
    first = []
    for n, (far, column) in enumerate(
        ((t_far, 0), (k_far, 0), (t_far, TILES - 1), (k_far, TILES - 1))
    ):
        side = pl.ds(128 * column, 128)
        first.append(pltpu.make_async_copy(far.at[:, side], strips.at[n], early.at[n]))
        first[n].start()
    copies = []
    for band in range(BANDS):
        at = pl.ds(8 * band, 8)
        for n, (far, near) in enumerate(((t_far, t), (k_far, k))):
            copy = pltpu.make_async_copy(far.at[at, :], near.at[at, :], arrived.at[n, band])
            copy.start()
            copies.append(copy)
    for ref in (lo, hi, own):
        ref[...] = jnp.zeros_like(ref)
    for n, copy in enumerate(first):
        copy.wait()
        high = n // 2
        at = 127 * high
        edge = strips[n].T[at : at + 1, :]
        own[n : n + 1, 0:ROWS] = edge
        (hi if high else lo)[n % 2 : n % 2 + 1, 0:ROWS] = edge
    for copy in copies:
        copy.wait()


def total(terms):
    sums = [None] * 4
    for n, term in enumerate(terms):
        sums[n % 4] = plus(sums[n % 4], term)
    return (sums[0] + sums[1]) + (sums[2] + sums[3])


def x_matrix_kernel(t, k, e, along, back, gain, sep, lo, hi, ends, t_flat, flat):
    lane = lax.broadcasted_iota(jnp.int32, (8, 128), 1)
    for band in range(BANDS):
        ks = [tile(k, band, c) for c in range(TILES)]
        ts = [tile(t, band, c) for c in range(TILES)]
        k_left = [pltpu.roll(v, 127, 1) for v in ks]
        t_left = [pltpu.roll(v, 127, 1) for v in ts]
        flow = []
        for c in range(TILES):
            at = pl.ds((band * TILES + c) * 8, 8)
            flat[at, :] = ks[c]
            t_flat[at, :] = ts[c]
            n = min(c + 1, TILES - 1)
            k_next = jnp.where(lane == 127, k_left[n], k_left[c])
            t_next = jnp.where(lane == 127, t_left[n], t_left[c])
            f = 8000.0 * (ks[c] + k_next) * (t_next - ts[c])
            if c == TILES - 1:
                f = jnp.where(lane == 127, 0.0, f)
            flow.append(f)
        turned = [pltpu.roll(v, 1, 1) for v in flow]
        for c in range(TILES):
            at = pl.ds((band * TILES + c) * 8, 8)
            first = turned[c - 1] if c else jnp.zeros_like(turned[0])
            f_before = jnp.where(lane == 0, first, turned[c])
            e[at, :] = 2.0 * ts[c] + (flow[c] - f_before)

    def link(l):
        if l == ROWS - 1:
            return jnp.zeros((TILES, 128), F32)
        return 1000.0 * (row(flat, l) + row(flat, l + 1))

    factor(link, ROWS, X_LEVELS, x_shift, along, back, gain, sep)
    one = jnp.ones((TILES, 128), F32)

    def at_start(l):
        return one if l == 0 else None

    def at_end(l):
        return one if l == ROWS - 1 else None

    def to(ref):
        def store(l, value):
            ref[l] = value

        return store

    args = (ROWS, X_LEVELS, x_shift, along, back, gain, sep)
    solve(at_start, *args, lo, to(lo))
    solve(at_end, *args, hi, to(hi))
    ends[0] = total(lo[i] * row(e, i) for i in range(ROWS))
    ends[1] = total(hi[i] * row(e, i) for i in range(ROWS))
    ends[2] = lo[0]
    ends[3] = lo[ROWS - 1]
    ends[4] = hi[ROWS - 1]
    ends[5] = row(flat, 0)
    ends[6] = row(flat, ROWS - 1)


def x_port_kernel(ends, lo, hi, own, below, above, port, edge, side):
    at = lax.axis_index("gy")
    side[...] = jnp.zeros_like(side)
    t_lo, k_lo, t_hi, k_hi = (own[n : n + 1, :] for n in range(4))
    before = jnp.where(at == 0, 0.0, below[...])
    after = jnp.where(at == lax.axis_size("gy") - 1, 0.0, above[...])
    side[0:1, :] = -8000.0 * (k_lo + before[1:2, :]) * (t_lo - before[0:1, :])
    side[127:128, :] = 8000.0 * (k_hi + after[1:2, :]) * (after[0:1, :] - t_hi)
    edge[...] = side[...].T[0:ROWS, :]
    lane = lax.broadcasted_iota(jnp.int32, (1, 128), 1)
    for n, response in enumerate((lo, hi)):
        port[n] = ends[n]
        for column, kept in ((0, 0), (TILES - 1, 127)):
            term = edge[...] * response[:, column, :]
            term = jnp.where(lane == kept, jnp.sum(term, axis=0, keepdims=True), 0.0)
            port[n, column : column + 1, :] = port[n, column : column + 1, :] + term
    for n in range(2, 7):
        port[n] = ends[n]


def x_solve_kernel(e, along, back, gain, sep, edge, u, flat):
    lane = lax.broadcasted_iota(jnp.int32, (8, 128), 1)
    flat[...] = e[...]
    for band in range(BANDS):
        part = edge[8 * band : 8 * band + 8, :]
        at = pl.ds(band * TILES * 8, 8)
        flat[at, :] = flat[at, :] + jnp.where(lane == 0, part, 0.0)
        at = pl.ds((band * TILES + TILES - 1) * 8, 8)
        flat[at, :] = flat[at, :] + jnp.where(lane == 127, part, 0.0)

    def store(l, value):
        u[l] = value

    def source(l):
        return row(flat, l)

    solve(source, ROWS, X_LEVELS, x_shift, along, back, gain, sep, u, store)


def take(ref):
    return tuple(ref[n] for n in range(7))


def join(one, two, scale):
    a1, b1, al1, be1, ga1, kf1, kl1 = one
    a2, b2, al2, be2, ga2, kf2, kl2 = two
    rho = 1.0 / (1.0 / (scale * (kl1 + kf2)) + al2 + ga1)
    delta = (a2 - b1) * rho
    return (
        a1 + be1 * delta,
        b2 - be2 * delta,
        al1 - be1 * be1 * rho,
        be1 * be2 * rho,
        ga2 - be2 * be2 * rho,
        kf1,
        kl2,
    )


def past_up(state, port, scale):
    p, q, k = state
    a, b, al, be, ga, kf, kl = port
    w = be / (1.0 / (scale * (k + kf)) + al + q)
    return (b - w * (a - p), ga - w * be, kl)


def past_down(state, port, scale):
    p, q, k = state
    a, b, al, be, ga, kf, kl = port
    w = be / (1.0 / (scale * (k + kl)) + ga + q)
    return (a + w * (p - b), al - w * be, kf)


def choose(condition, new, old):
    return tuple(jnp.where(condition, x, y) for x, y in zip(new, old))


def reach(index, ports, lo, hi, scale):
    count = len(ports)
    for n in range(count - 1):
        lo = choose(n < index, past_up(lo, ports[n], scale), lo)
    for n in reversed(range(1, count)):
        hi = choose(n > index, past_down(hi, ports[n], scale), hi)
    return lo, hi


def flows(port, lo, hi, scale):
    a, b, al, be, ga, kf, kl = port
    d_lo = 1.0 / (scale * (lo[2] + kf)) + al + lo[1]
    d_hi = 1.0 / (scale * (hi[2] + kl)) + ga + hi[1]
    c_lo, c_hi = a - lo[0], hi[0] - b
    inverse = 1.0 / (d_lo * d_hi - be * be)
    return (d_hi * c_lo + be * c_hi) * inverse, (d_lo * c_hi + be * c_lo) * inverse


def place(index, own, received, table, ring=RING):
    table[index] = own[...]
    for s, value in zip(ring, received):
        table[lax.bitwise_xor(index, s)] = value[...]


def pair_kernel(own, other, out):
    core = lax.rem(lax.axis_index("gx"), 2)
    mine, theirs = take(own), take(other)
    first = choose(core == 0, mine, theirs)
    second = choose(core == 0, theirs, mine)
    for n, value in enumerate(join(first, second, 1000.0)):
        out[n] = value


def four_kernel(own, r1, r2, r3, out, table):
    z = lax.rem(lax.div(lax.axis_index("gx"), 2), 4)
    place(z, own, (r1, r2, r3), table)
    ports = [take(table.at[j]) for j in range(4)]
    joined = join(join(ports[0], ports[1], 1000.0), join(ports[2], ports[3], 1000.0), 1000.0)
    for n, value in enumerate(joined):
        out[n] = value


def to_runs(blocks, out):
    for p in range(TILES // 2):
        stack = [blocks(band, 2 * p + half) for half in range(2) for band in range(BANDS)]
        out[128 * p : 128 * p + 128, :] = jnp.concatenate(stack, axis=0).T


def cell(ref, l):
    return ref[pl.ds(l, 8, stride=128), :]


def from_runs(turned, store):
    for p in range(TILES // 2):
        block = turned[128 * p : 128 * p + 128, :].T
        for half in range(2):
            for band in range(BANDS):
                at = ROWS * half + 8 * band
                store(band, 2 * p + half, block[at : at + 8, :])


def put(ref):
    def store(band, column, value):
        ref[8 * band : 8 * band + 8, 128 * column : 128 * column + 128] = value

    return store


def y_matrix_kernel(k, along, back, gain, sep, lo, hi, ends, turned):
    to_runs(lambda band, column: tile(k, band, column), turned)
    lane = lax.broadcasted_iota(jnp.int32, (8, 128), 1)
    sublane = lax.broadcasted_iota(jnp.int32, (8, 128), 0)
    very_last = (lane >= 64) & (sublane == 7)
    very_first = (lane < 64) & (sublane == 0)

    def link(l):
        if l == Y_STEPS - 1:
            both = 4000.0 * (cell(turned, l) + y_shift(cell(turned, 0), 1))
            return jnp.where(very_last, 0.0, both)
        return 4000.0 * (cell(turned, l) + cell(turned, l + 1))

    factor(link, Y_STEPS, Y_LEVELS, y_shift, along, back, gain, sep)

    def at_start(l):
        return jnp.where(very_first, 1.0, 0.0) if l == 0 else None

    def at_end(l):
        return jnp.where(very_last, 1.0, 0.0) if l == Y_STEPS - 1 else None

    def to(ref):
        def store(l, value):
            ref[l] = value

        return store

    args = (Y_STEPS, Y_LEVELS, y_shift, along, back, gain, sep)
    solve(at_start, *args, lo, to(lo))
    solve(at_end, *args, hi, to(hi))
    last = Y_STEPS - 1
    ends[...] = jnp.zeros_like(ends)
    ends[0:1, :] = lo[0, 0:1, :]
    ends[1:2, :] = pltpu.roll(lo[last], 64, 1)[7:8, :]
    ends[2:3, :] = pltpu.roll(hi[last], 64, 1)[7:8, :]
    ends[3:4, :] = cell(turned, 0)[0:1, :]
    ends[4:5, :] = pltpu.roll(cell(turned, last), 64, 1)[7:8, :]


def upright_kernel(lo, hi, flat_lo, flat_hi, turned):
    for n, (response, flat) in enumerate(((lo, flat_lo), (hi, flat_hi))):
        for l in range(Y_STEPS):
            turned[n, pl.ds(l, 8, stride=128), :] = response[l]
        from_runs(turned.at[n], put(flat))


def blend_kernel(u, x_lo, x_hi, y_lo, y_hi, t, source, lo, hi, mixed, known, flat, side):
    for ref, out in ((u, flat), (x_lo, lo), (x_hi, hi)):
        for i in range(ROWS):
            at = pl.ds((i // 8) * (8 * TILES) + i % 8, TILES, stride=8)
            out[at, :] = ref[i]
    for band in range(BANDS):
        sums = [None, None]
        for column in range(TILES):
            at = pl.ds((band * TILES + column) * 8, 8)
            value = flat[at, :] - 2.0 * t[at, :]
            source[at, :] = value
            for n, response in enumerate((y_lo, y_hi)):
                r = tile(response, band, column)
                sums[n] = plus(sums[n], r * value)
                mixed[2 * n, at, :] = r * lo[at, :]
                mixed[2 * n + 1, at, :] = r * hi[at, :]
        for n in range(2):
            side[64 * n + 8 * band : 64 * n + 8 * band + 8, :] = sums[n]
    known[...] = jnp.broadcast_to(jnp.sum(side[...].T, axis=0, keepdims=True), (8, 128))


def y_port_kernel(
    own_y, y1, y2, y3, own_z, z1, z2, z3, own, other, mixed, known, ends,
    port, flow, table_y, table_z, side,
):
    index = lax.axis_index("gx")
    core, z, y = lax.rem(index, 2), lax.rem(lax.div(index, 2), 4), lax.div(index, 8)
    place(y, own_y, (y1, y2, y3), table_y)
    place(z, own_z, (z1, z2, z3), table_z)
    nothing = (jnp.zeros((TILES, 128), F32),) * 3
    scale = 1000.0
    lo, hi = reach(y, [take(table_y.at[j]) for j in range(4)], nothing, nothing, scale)
    lo, hi = reach(z, [take(table_z.at[j]) for j in range(4)], lo, hi, scale)
    mine, theirs = take(own), take(other)
    lo = choose(core == 1, past_up(lo, theirs, scale), lo)
    hi = choose(core == 0, past_down(hi, theirs, scale), hi)
    flow[0], flow[1] = flows(mine, lo, hi, scale)
    sums = [None] * (2 * BANDS)
    for column in range(TILES):
        down, up = across(flow, column)
        for band in range(BANDS):
            at = pl.ds((band * TILES + column) * 8, 8)
            for n in range(2):
                part = up * mixed[2 * n + 1, at, :] - down * mixed[2 * n, at, :]
                sums[BANDS * n + band] = plus(sums[BANDS * n + band], part)
    for n, value in enumerate(sums):
        side[8 * n : 8 * n + 8, :] = value
    both = jnp.sum(side[...].T, axis=0, keepdims=True) + known[0:1, :]
    port[...] = jnp.zeros_like(port)
    port[0:1, :] = both
    port[1:2, :] = pltpu.roll(both, 64, 1)
    port[2:7, :] = ends[0:5, :]


def across(flow, column):
    return tuple(
        jnp.broadcast_to(flow[n, column : column + 1, :], (8, 128)) for n in range(2)
    )


def y_solve_kernel(source, lo, hi, flow, along, back, gain, sep, t, out, d, turned):
    def block(band, column):
        down, up = across(flow, column)
        x = flat_tile(source, band, column)
        return x - down * flat_tile(lo, band, column) + up * flat_tile(hi, band, column)

    to_runs(block, turned)

    def store(l, value):
        d[l] = value

    def cells(l):
        return cell(turned, l)

    solve(cells, Y_STEPS, Y_LEVELS, y_shift, along, back, gain, sep, d, store)
    for l in range(Y_STEPS):
        turned[pl.ds(l, 8, stride=128), :] = d[l]
    keep = put(out)

    def plus_start(band, column, value):
        keep(band, column, value + flat_tile(t, band, column))

    from_runs(turned, plus_start)


def finish_kernel(own, r1, r2, r3, base, y_lo, y_hi, out, table, side, done, sent):
    index = lax.axis_index("gy")
    place(index, own, (r1, r2, r3), table, LAST_RING)
    lane = lax.broadcasted_iota(jnp.int32, (1, 128), 1)

    def port_of(ref):
        return tuple(jnp.where(lane < ROWS, ref[n : n + 1, :], 1.0) for n in range(7))

    nothing = (jnp.zeros((1, 128), F32),) * 3
    scale = 4000.0
    lo, hi = reach(index, [port_of(table.at[j]) for j in range(4)], nothing, nothing, scale)
    f_lo, f_hi = flows(port_of(own), lo, hi, scale)
    side[...] = jnp.zeros_like(side)
    side[0:1, :] = f_lo
    side[1:2, :] = f_hi
    upright = side[...].T
    copies = []
    for band in range(BANDS):
        at = slice(8 * band, 8 * band + 8)
        down = jnp.broadcast_to(upright[at, 0:1], (8, 128))
        up = jnp.broadcast_to(upright[at, 1:2], (8, 128))
        keep = put(done)
        for column in range(TILES):
            part = tile(base, band, column)
            part = part - down * tile(y_lo, band, column) + up * tile(y_hi, band, column)
            keep(band, column, part)
        copy = pltpu.make_async_copy(done.at[at, :], out.at[at, :], sent.at[band])
        copy.start()
        copies.append(copy)
    for copy in copies:
        copy.wait()


def around(value, axis, size, stride, step):
    pairs = []
    for i in range(size):
        digit = (i // stride) % 4
        pairs.append((i, i + ((digit ^ step) - digit) * stride))
    return lax.ppermute(value, axis, pairs)


def per_device(initial_heat_state, thermal_coefficient):
    t, k = initial_heat_state[0], thermal_coefficient[0]
    natural = struct(ROWS, COLS)
    t, k, own_lo, own_hi, own_edges = call(
        load_kernel,
        [natural, natural] + [struct(8, 128)] * 3,
        [
            pltpu.VMEM((4, ROWS, 128), F32),
            pltpu.SemaphoreType.DMA((4,)),
            pltpu.SemaphoreType.DMA((2, BANDS)),
        ],
        name="load",
        grant=GRANT,
        in_specs=[HBM, HBM],
        out_specs=[VMEM] * 5,
    )(t, k)
    below = lax.ppermute(own_hi, "gy", [(i, (i + 1) % 4) for i in range(4)])
    above = lax.ppermute(own_lo, "gy", [((i + 1) % 4, i) for i in range(4)])
    flat = struct(BANDS * TILES * 8, 128)
    runs = struct(TILES // 2 * 128, 128)
    x_field, y_field = struct(ROWS, TILES, 128), struct(Y_STEPS, 8, 128)
    x_port = struct(7, TILES, 128)
    e, *x_coefficients, x_lo, x_hi, x_ends, t_flat, k_flat = call(
        x_matrix_kernel,
        [
            flat,
            x_field,
            x_field,
            x_field,
            struct((2 * X_LEVELS + 1) * SEGMENTS, TILES, 128),
            x_field,
            x_field,
            x_port,
            flat,
            flat,
        ],
        name="x_matrix",
    )(t, k)
    *y_coefficients, y_lo, y_hi, y_ends = call(
        y_matrix_kernel,
        [
            y_field,
            y_field,
            y_field,
            struct((2 * Y_LEVELS + 1) * SEGMENTS, 8, 128),
            y_field,
            y_field,
            struct(8, 128),
        ],
        [scratch(runs)],
        name="y_matrix",
    )(k)
    below, above, y_lo = lax.optimization_barrier((below, above, y_lo))
    own, edge = call(
        x_port_kernel,
        [x_port, struct(ROWS, 128)],
        [pltpu.VMEM((128, 128), F32)],
        flops=200_000,
        name="x_port",
    )(x_ends, x_lo, x_hi, own_edges, below, above)
    u = call(x_solve_kernel, x_field, [scratch(flat)], flops=700_000, name="x_solve")(
        e, *x_coefficients, edge
    )
    other = lax.ppermute(own, "gx", [(i, i ^ 1) for i in range(32)])
    other, u = lax.optimization_barrier((other, u))
    own_z = call(pair_kernel, x_port, name="pair")(own, other)
    from_z = [around(own_z, "gx", 32, 2, s) for s in RING]
    flat_lo, flat_hi = call(
        upright_kernel,
        [natural, natural],
        [pltpu.VMEM((2, TILES // 2 * 128, 128), F32)],
        name="upright",
    )(y_lo, y_hi)
    *from_z, flat_lo = lax.optimization_barrier((*from_z, flat_lo))
    table = pltpu.VMEM((4, 7, TILES, 128), F32)
    own_y = call(four_kernel, x_port, [table], name="four")(own_z, *from_z)
    from_y = [around(own_y, "gx", 32, 8, s) for s in RING]
    square = pltpu.VMEM((128, 128), F32)
    source, lo_flat, hi_flat, mixed, known = call(
        blend_kernel,
        [flat, flat, flat, struct(4, BANDS * TILES * 8, 128), struct(8, 128)],
        [scratch(flat), square],
        name="blend",
    )(u, x_lo, x_hi, flat_lo, flat_hi, t_flat)
    port, flow = call(
        y_port_kernel,
        [struct(8, 128), struct(2, TILES, 128)],
        [table, table, square],
        name="y_port",
    )(own_y, *from_y, own_z, *from_z, own, other, mixed, known, y_ends)
    from_gy = [around(port, "gy", 4, 1, s) for s in LAST_RING]
    base = call(
        y_solve_kernel, natural, [scratch(y_field), scratch(runs)], name="y_solve"
    )(source, lo_flat, hi_flat, flow, *y_coefficients, t_flat)
    updated = call(
        finish_kernel,
        natural,
        [
            pltpu.VMEM((4, 8, 128), F32),
            pltpu.VMEM((128, 128), F32),
            scratch(natural),
            pltpu.SemaphoreType.DMA((BANDS,)),
        ],
        name="finish",
        in_specs=[VMEM] * 7,
        out_specs=HBM,
    )(port, *from_gy, base, flat_lo, flat_hi)
    return updated[None]


def solution(mesh):
    placed = (P(None, "gx", "gy"), P(None, "gx", "gy"))
    return jax.shard_map(
        per_device, mesh=mesh, in_specs=placed, out_specs=P(None, "gx", "gy"), check_vma=False
    )
```

```python
import jax
import jax.numpy as jnp
from jax import lax
from jax.experimental import pallas as pl
from jax.experimental.pallas import tpu as pltpu
from jax.sharding import PartitionSpec as P

ROWS, COLS = 64, 2048
BANDS, TILES = ROWS // 8, COLS // 128
SEGMENTS = 4
PARTS = 2
Y_STEPS = 128
X_LEVELS, Y_LEVELS = 2, 6
GRANT = (527 << 20) // 10
RING, LAST_RING = (2, 3, 1), (1, 2, 3)
F32 = jnp.float32
VMEM = pl.BlockSpec(memory_space=pltpu.VMEM)
HBM = pl.BlockSpec(memory_space=pltpu.MemorySpace.HBM)


def struct(*shape):
    return jax.ShapeDtypeStruct(shape, F32)


def scratch(like):
    return pltpu.VMEM(like.shape, like.dtype)


def whole(outs, args):
    return dict(in_specs=[VMEM] * len(args), out_specs=jax.tree.map(lambda _: VMEM, outs))


def call(kernel, outs, buffers=(), flops=2_000_000, name=None, grant=32 << 20, **windows):
    def run(*args):
        return pl.pallas_call(
            kernel,
            out_shape=outs,
            **(windows or whole(outs, args)),
            scratch_shapes=list(buffers),
            compiler_params=pltpu.CompilerParams(vmem_limit_bytes=grant),
            cost_estimate=pl.CostEstimate(flops=flops, bytes_accessed=1 << 20, transcendentals=0),
            name=name,
        )(*args)

    return run


def moved(chain, by, shift):
    out = []
    for s in range(SEGMENTS):
        runs, at = divmod(s + by, SEGMENTS)
        out.append(shift(chain[at], runs) if runs else chain[at])
    return out


def factor(link, n, levels, shift, along, back, gain, sep):
    m = n // SEGMENTS
    near = [link(s * m) for s in range(SEGMENTS)]
    ground = [jnp.ones_like(near[0])] * SEGMENTS
    held = [jnp.ones_like(near[0])] * SEGMENTS
    for step in range(1, m):
        for s in range(SEGMENTS):
            l = s * m + step
            v = link(l)
            r = 1.0 / (near[s] + ground[s] + v)
            t = v * r
            c = near[s] * r
            along[l], back[l], gain[l] = t, c, r
            held[s] = held[s] + ground[s] * c
            near[s] = near[s] * t
            ground[s] = ground[s] * t
            if step < m - 1:
                ground[s] = ground[s] + 1.0
    before = moved(ground, -1, shift)
    own = [held[s] + before[s] for s in range(SEGMENTS)]
    up = near
    down = moved(near, -1, shift)
    for level in range(levels):
        stride = 1 << level
        r = [1.0 / (own[s] + up[s] + down[s]) for s in range(SEGMENTS)]
        r_down, r_up = moved(r, -stride, shift), moved(r, stride, shift)
        own_down, own_up = moved(own, -stride, shift), moved(own, stride, shift)
        down_down, up_up = moved(down, -stride, shift), moved(up, stride, shift)
        for s in range(SEGMENTS):
            a, b = down[s] * r_down[s], up[s] * r_up[s]
            sep[(level * 2) * SEGMENTS + s] = a
            sep[(level * 2 + 1) * SEGMENTS + s] = b
            own[s] = own[s] + a * own_down[s] + b * own_up[s]
            down[s], up[s] = a * down_down[s], b * up_up[s]
    for s in range(SEGMENTS):
        sep[levels * 2 * SEGMENTS + s] = 1.0 / own[s]


def plus(a, b):
    return b if a is None else a if b is None else a + b


def times(a, b):
    return None if a is None else a * b


def solve(source, n, levels, shift, along, back, gain, sep, part, store):
    m = n // SEGMENTS
    total = [source(s * m) for s in range(SEGMENTS)]
    z = [source(s * m + 1) for s in range(SEGMENTS)]
    zero = [[False] * SEGMENTS for _ in range(m)]
    for step in range(1, m):
        for s in range(SEGMENTS):
            l = s * m + step
            zero[step][s] = z[s] is None
            if z[s] is not None:
                part[l] = z[s] * gain[l]
                total[s] = plus(total[s], z[s] * back[l])
                z[s] = z[s] * along[l]
            if step < m - 1:
                z[s] = plus(source(l + 1), z[s])
    shape = jnp.zeros(along.shape[1:], F32)
    z = [shape if v is None else v for v in z]
    before = moved(z, -1, shift)
    total = [plus(total[s], before[s]) for s in range(SEGMENTS)]
    for level in range(levels):
        stride = 1 << level
        lo, hi = moved(total, -stride, shift), moved(total, stride, shift)
        total = [
            total[s]
            + sep[(level * 2) * SEGMENTS + s] * lo[s]
            + sep[(level * 2 + 1) * SEGMENTS + s] * hi[s]
            for s in range(SEGMENTS)
        ]
    value = [total[s] * sep[levels * 2 * SEGMENTS + s] for s in range(SEGMENTS)]
    after = moved(value, 1, shift)
    for s in range(SEGMENTS):
        store(s * m, value[s])
    for step in reversed(range(1, m)):
        for s in range(SEGMENTS):
            l = s * m + step
            known = back[l] * value[s]
            if not zero[step][s]:
                known = known + part[l]
            after[s] = known + along[l] * after[s]
            store(l, after[s])


def x_shift(value, runs):
    return value


def y_shift(value, runs):
    if runs % 2 == 0:
        return pltpu.roll(value, (-(runs // 2)) % 8, 0)
    swapped = pltpu.roll(value, 64, 1)
    late = lax.broadcasted_iota(jnp.int32, value.shape, 1) >= 64
    if runs == 1:
        return jnp.where(late, pltpu.roll(swapped, 7, 0), swapped)
    return jnp.where(late, swapped, pltpu.roll(swapped, 1, 0))


def tile(ref, band, column):
    return ref[8 * band : 8 * band + 8, 128 * column : 128 * column + 128]


def flat_tile(ref, band, column):
    at = (band * TILES + column) * 8
    return ref[at : at + 8, :]


def row(ref, i):
    return ref[pl.ds((i // 8) * (8 * TILES) + i % 8, TILES, stride=8), :]


def load_kernel(t_far, k_far, t, k, lo, hi, own, arrived):
    copies = []
    for part in range(PARTS):
        at = pl.ds(ROWS // PARTS * part, ROWS // PARTS)
        for n, (far, near) in enumerate(((t_far, t), (k_far, k))):
            copy = pltpu.make_async_copy(far.at[at, :], near.at[at, :], arrived.at[n, part])
            copy.start()
            copies.append(copy)
    for ref in (lo, hi, own):
        ref[...] = jnp.zeros_like(ref)
    for copy in copies:
        copy.wait()
    for n, (ref, column) in enumerate(((t, 0), (k, 0), (t, TILES - 1), (k, TILES - 1))):
        strip = ref[:, 128 * column : 128 * column + 128].T
        at = 127 if column else 0
        edge = strip[at : at + 1, :]
        own[n : n + 1, 0:ROWS] = edge
        (hi if column else lo)[n % 2 : n % 2 + 1, 0:ROWS] = edge


def total(terms):
    sums = [None] * 4
    for n, term in enumerate(terms):
        sums[n % 4] = plus(sums[n % 4], term)
    return (sums[0] + sums[1]) + (sums[2] + sums[3])


def x_matrix_kernel(t, k, e, along, back, gain, sep, lo, hi, ends, t_flat, flat):
    lane = lax.broadcasted_iota(jnp.int32, (8, 128), 1)
    for band in range(BANDS):
        ks = [tile(k, band, c) for c in range(TILES)]
        ts = [tile(t, band, c) for c in range(TILES)]
        k_left = [pltpu.roll(v, 127, 1) for v in ks]
        t_left = [pltpu.roll(v, 127, 1) for v in ts]
        flow = []
        for c in range(TILES):
            at = pl.ds((band * TILES + c) * 8, 8)
            flat[at, :] = ks[c]
            t_flat[at, :] = ts[c]
            n = min(c + 1, TILES - 1)
            k_next = jnp.where(lane == 127, k_left[n], k_left[c])
            t_next = jnp.where(lane == 127, t_left[n], t_left[c])
            f = 8000.0 * (ks[c] + k_next) * (t_next - ts[c])
            if c == TILES - 1:
                f = jnp.where(lane == 127, 0.0, f)
            flow.append(f)
        turned = [pltpu.roll(v, 1, 1) for v in flow]
        for c in range(TILES):
            at = pl.ds((band * TILES + c) * 8, 8)
            first = turned[c - 1] if c else jnp.zeros_like(turned[0])
            f_before = jnp.where(lane == 0, first, turned[c])
            e[at, :] = 2.0 * ts[c] + (flow[c] - f_before)

    def link(l):
        if l == ROWS - 1:
            return jnp.zeros((TILES, 128), F32)
        return 1000.0 * (row(flat, l) + row(flat, l + 1))

    factor(link, ROWS, X_LEVELS, x_shift, along, back, gain, sep)
    one = jnp.ones((TILES, 128), F32)

    def at_start(l):
        return one if l == 0 else None

    def at_end(l):
        return one if l == ROWS - 1 else None

    def to(ref):
        def store(l, value):
            ref[l] = value

        return store

    args = (ROWS, X_LEVELS, x_shift, along, back, gain, sep)
    solve(at_start, *args, lo, to(lo))
    solve(at_end, *args, hi, to(hi))
    ends[0] = total(lo[i] * row(e, i) for i in range(ROWS))
    ends[1] = total(hi[i] * row(e, i) for i in range(ROWS))
    ends[2] = lo[0]
    ends[3] = lo[ROWS - 1]
    ends[4] = hi[ROWS - 1]
    ends[5] = row(flat, 0)
    ends[6] = row(flat, ROWS - 1)


def x_port_kernel(ends, lo, hi, own, below, above, port, edge, side):
    at = lax.axis_index("gy")
    side[...] = jnp.zeros_like(side)
    t_lo, k_lo, t_hi, k_hi = (own[n : n + 1, :] for n in range(4))
    before = jnp.where(at == 0, 0.0, below[...])
    after = jnp.where(at == lax.axis_size("gy") - 1, 0.0, above[...])
    side[0:1, :] = -8000.0 * (k_lo + before[1:2, :]) * (t_lo - before[0:1, :])
    side[127:128, :] = 8000.0 * (k_hi + after[1:2, :]) * (after[0:1, :] - t_hi)
    edge[...] = side[...].T[0:ROWS, :]
    lane = lax.broadcasted_iota(jnp.int32, (1, 128), 1)
    for n, response in enumerate((lo, hi)):
        port[n] = ends[n]
        for column, kept in ((0, 0), (TILES - 1, 127)):
            term = edge[...] * response[:, column, :]
            term = jnp.where(lane == kept, jnp.sum(term, axis=0, keepdims=True), 0.0)
            port[n, column : column + 1, :] = port[n, column : column + 1, :] + term
    for n in range(2, 7):
        port[n] = ends[n]


def x_solve_kernel(e, along, back, gain, sep, edge, u, flat):
    lane = lax.broadcasted_iota(jnp.int32, (8, 128), 1)
    flat[...] = e[...]
    for band in range(BANDS):
        part = edge[8 * band : 8 * band + 8, :]
        at = pl.ds(band * TILES * 8, 8)
        flat[at, :] = flat[at, :] + jnp.where(lane == 0, part, 0.0)
        at = pl.ds((band * TILES + TILES - 1) * 8, 8)
        flat[at, :] = flat[at, :] + jnp.where(lane == 127, part, 0.0)

    def store(l, value):
        u[l] = value

    def source(l):
        return row(flat, l)

    solve(source, ROWS, X_LEVELS, x_shift, along, back, gain, sep, u, store)


def take(ref):
    return tuple(ref[n] for n in range(7))


def join(one, two, scale):
    a1, b1, al1, be1, ga1, kf1, kl1 = one
    a2, b2, al2, be2, ga2, kf2, kl2 = two
    rho = 1.0 / (1.0 / (scale * (kl1 + kf2)) + al2 + ga1)
    delta = (a2 - b1) * rho
    return (
        a1 + be1 * delta,
        b2 - be2 * delta,
        al1 - be1 * be1 * rho,
        be1 * be2 * rho,
        ga2 - be2 * be2 * rho,
        kf1,
        kl2,
    )


def past_up(state, port, scale):
    p, q, k = state
    a, b, al, be, ga, kf, kl = port
    w = be / (1.0 / (scale * (k + kf)) + al + q)
    return (b - w * (a - p), ga - w * be, kl)


def past_down(state, port, scale):
    p, q, k = state
    a, b, al, be, ga, kf, kl = port
    w = be / (1.0 / (scale * (k + kl)) + ga + q)
    return (a + w * (p - b), al - w * be, kf)


def choose(condition, new, old):
    return tuple(jnp.where(condition, x, y) for x, y in zip(new, old))


def reach(index, ports, lo, hi, scale):
    count = len(ports)
    for n in range(count - 1):
        lo = choose(n < index, past_up(lo, ports[n], scale), lo)
    for n in reversed(range(1, count)):
        hi = choose(n > index, past_down(hi, ports[n], scale), hi)
    return lo, hi


def flows(port, lo, hi, scale):
    a, b, al, be, ga, kf, kl = port
    d_lo = 1.0 / (scale * (lo[2] + kf)) + al + lo[1]
    d_hi = 1.0 / (scale * (hi[2] + kl)) + ga + hi[1]
    c_lo, c_hi = a - lo[0], hi[0] - b
    inverse = 1.0 / (d_lo * d_hi - be * be)
    return (d_hi * c_lo + be * c_hi) * inverse, (d_lo * c_hi + be * c_lo) * inverse


def place(index, own, received, table, ring=RING):
    table[index] = own[...]
    for s, value in zip(ring, received):
        table[lax.bitwise_xor(index, s)] = value[...]


def pair_kernel(own, other, out):
    core = lax.rem(lax.axis_index("gx"), 2)
    mine, theirs = take(own), take(other)
    first = choose(core == 0, mine, theirs)
    second = choose(core == 0, theirs, mine)
    for n, value in enumerate(join(first, second, 1000.0)):
        out[n] = value


def four_kernel(own, r1, r2, r3, out, table):
    z = lax.rem(lax.div(lax.axis_index("gx"), 2), 4)
    place(z, own, (r1, r2, r3), table)
    ports = [take(table.at[j]) for j in range(4)]
    joined = join(join(ports[0], ports[1], 1000.0), join(ports[2], ports[3], 1000.0), 1000.0)
    for n, value in enumerate(joined):
        out[n] = value


def to_runs(blocks, out):
    for p in range(TILES // 2):
        stack = [blocks(band, 2 * p + half) for half in range(2) for band in range(BANDS)]
        out[128 * p : 128 * p + 128, :] = jnp.concatenate(stack, axis=0).T


def cell(ref, l):
    return ref[pl.ds(l, 8, stride=128), :]


def from_runs(turned, store):
    for p in range(TILES // 2):
        block = turned[128 * p : 128 * p + 128, :].T
        for half in range(2):
            for band in range(BANDS):
                at = ROWS * half + 8 * band
                store(band, 2 * p + half, block[at : at + 8, :])


def put(ref):
    def store(band, column, value):
        ref[8 * band : 8 * band + 8, 128 * column : 128 * column + 128] = value

    return store


def y_matrix_kernel(k, along, back, gain, sep, lo, hi, ends, turned):
    to_runs(lambda band, column: tile(k, band, column), turned)
    lane = lax.broadcasted_iota(jnp.int32, (8, 128), 1)
    sublane = lax.broadcasted_iota(jnp.int32, (8, 128), 0)
    very_last = (lane >= 64) & (sublane == 7)
    very_first = (lane < 64) & (sublane == 0)

    def link(l):
        if l == Y_STEPS - 1:
            both = 4000.0 * (cell(turned, l) + y_shift(cell(turned, 0), 1))
            return jnp.where(very_last, 0.0, both)
        return 4000.0 * (cell(turned, l) + cell(turned, l + 1))

    factor(link, Y_STEPS, Y_LEVELS, y_shift, along, back, gain, sep)

    def at_start(l):
        return jnp.where(very_first, 1.0, 0.0) if l == 0 else None

    def at_end(l):
        return jnp.where(very_last, 1.0, 0.0) if l == Y_STEPS - 1 else None

    def to(ref):
        def store(l, value):
            ref[l] = value

        return store

    args = (Y_STEPS, Y_LEVELS, y_shift, along, back, gain, sep)
    solve(at_start, *args, lo, to(lo))
    solve(at_end, *args, hi, to(hi))
    last = Y_STEPS - 1
    ends[...] = jnp.zeros_like(ends)
    ends[0:1, :] = lo[0, 0:1, :]
    ends[1:2, :] = pltpu.roll(lo[last], 64, 1)[7:8, :]
    ends[2:3, :] = pltpu.roll(hi[last], 64, 1)[7:8, :]
    ends[3:4, :] = cell(turned, 0)[0:1, :]
    ends[4:5, :] = pltpu.roll(cell(turned, last), 64, 1)[7:8, :]


def upright_kernel(lo, hi, flat_lo, flat_hi, turned):
    for n, (response, flat) in enumerate(((lo, flat_lo), (hi, flat_hi))):
        for l in range(Y_STEPS):
            turned[n, pl.ds(l, 8, stride=128), :] = response[l]
        from_runs(turned.at[n], put(flat))


def blend_kernel(u, x_lo, x_hi, y_lo, y_hi, t, source, lo, hi, mixed, known, flat, side):
    for ref, out in ((u, flat), (x_lo, lo), (x_hi, hi)):
        for i in range(ROWS):
            at = pl.ds((i // 8) * (8 * TILES) + i % 8, TILES, stride=8)
            out[at, :] = ref[i]
    for band in range(BANDS):
        sums = [None, None]
        for column in range(TILES):
            at = pl.ds((band * TILES + column) * 8, 8)
            value = flat[at, :] - 2.0 * t[at, :]
            source[at, :] = value
            for n, response in enumerate((y_lo, y_hi)):
                r = tile(response, band, column)
                sums[n] = plus(sums[n], r * value)
                mixed[2 * n, at, :] = r * lo[at, :]
                mixed[2 * n + 1, at, :] = r * hi[at, :]
        for n in range(2):
            side[64 * n + 8 * band : 64 * n + 8 * band + 8, :] = sums[n]
    known[...] = jnp.broadcast_to(jnp.sum(side[...].T, axis=0, keepdims=True), (8, 128))


def y_port_kernel(
    own_y, y1, y2, y3, own_z, z1, z2, z3, own, other, mixed, known, ends,
    port, flow, table_y, table_z, side,
):
    index = lax.axis_index("gx")
    core, z, y = lax.rem(index, 2), lax.rem(lax.div(index, 2), 4), lax.div(index, 8)
    place(y, own_y, (y1, y2, y3), table_y)
    place(z, own_z, (z1, z2, z3), table_z)
    nothing = (jnp.zeros((TILES, 128), F32),) * 3
    scale = 1000.0
    lo, hi = reach(y, [take(table_y.at[j]) for j in range(4)], nothing, nothing, scale)
    lo, hi = reach(z, [take(table_z.at[j]) for j in range(4)], lo, hi, scale)
    mine, theirs = take(own), take(other)
    lo = choose(core == 1, past_up(lo, theirs, scale), lo)
    hi = choose(core == 0, past_down(hi, theirs, scale), hi)
    flow[0], flow[1] = flows(mine, lo, hi, scale)
    sums = [None] * (2 * BANDS)
    for column in range(TILES):
        down, up = across(flow, column)
        for band in range(BANDS):
            at = pl.ds((band * TILES + column) * 8, 8)
            for n in range(2):
                part = up * mixed[2 * n + 1, at, :] - down * mixed[2 * n, at, :]
                sums[BANDS * n + band] = plus(sums[BANDS * n + band], part)
    for n, value in enumerate(sums):
        side[8 * n : 8 * n + 8, :] = value
    both = jnp.sum(side[...].T, axis=0, keepdims=True) + known[0:1, :]
    port[...] = jnp.zeros_like(port)
    port[0:1, :] = both
    port[1:2, :] = pltpu.roll(both, 64, 1)
    port[2:7, :] = ends[0:5, :]


def across(flow, column):
    return tuple(
        jnp.broadcast_to(flow[n, column : column + 1, :], (8, 128)) for n in range(2)
    )


def y_solve_kernel(source, lo, hi, flow, along, back, gain, sep, t, out, d, turned):
    def block(band, column):
        down, up = across(flow, column)
        x = flat_tile(source, band, column)
        return x - down * flat_tile(lo, band, column) + up * flat_tile(hi, band, column)

    to_runs(block, turned)

    def store(l, value):
        d[l] = value

    def cells(l):
        return cell(turned, l)

    solve(cells, Y_STEPS, Y_LEVELS, y_shift, along, back, gain, sep, d, store)
    for l in range(Y_STEPS):
        turned[pl.ds(l, 8, stride=128), :] = d[l]
    keep = put(out)

    def plus_start(band, column, value):
        keep(band, column, value + flat_tile(t, band, column))

    from_runs(turned, plus_start)


def finish_kernel(own, r1, r2, r3, base, y_lo, y_hi, out, table, side, done, sent):
    index = lax.axis_index("gy")
    place(index, own, (r1, r2, r3), table, LAST_RING)
    lane = lax.broadcasted_iota(jnp.int32, (1, 128), 1)

    def port_of(ref):
        return tuple(jnp.where(lane < ROWS, ref[n : n + 1, :], 1.0) for n in range(7))

    nothing = (jnp.zeros((1, 128), F32),) * 3
    scale = 4000.0
    lo, hi = reach(index, [port_of(table.at[j]) for j in range(4)], nothing, nothing, scale)
    f_lo, f_hi = flows(port_of(own), lo, hi, scale)
    side[...] = jnp.zeros_like(side)
    side[0:1, :] = f_lo
    side[1:2, :] = f_hi
    upright = side[...].T
    copies = []
    for band in range(BANDS):
        at = slice(8 * band, 8 * band + 8)
        down = jnp.broadcast_to(upright[at, 0:1], (8, 128))
        up = jnp.broadcast_to(upright[at, 1:2], (8, 128))
        keep = put(done)
        for column in range(TILES):
            part = tile(base, band, column)
            part = part - down * tile(y_lo, band, column) + up * tile(y_hi, band, column)
            keep(band, column, part)
        if band % 2:
            pair = pl.ds(8 * band - 8, 16)
            copy = pltpu.make_async_copy(done.at[pair, :], out.at[pair, :], sent.at[band // 2])
            copy.start()
            copies.append(copy)
    for copy in copies:
        copy.wait()


def around(value, axis, size, stride, step):
    pairs = []
    for i in range(size):
        digit = (i // stride) % 4
        pairs.append((i, i + ((digit ^ step) - digit) * stride))
    return lax.ppermute(value, axis, pairs)


def per_device(initial_heat_state, thermal_coefficient):
    t, k = initial_heat_state[0], thermal_coefficient[0]
    natural = struct(ROWS, COLS)
    t, k, own_lo, own_hi, own_edges = call(
        load_kernel,
        [natural, natural] + [struct(8, 128)] * 3,
        [pltpu.SemaphoreType.DMA((2, PARTS))],
        name="load",
        grant=GRANT,
        in_specs=[HBM, HBM],
        out_specs=[VMEM] * 5,
    )(t, k)
    below = lax.ppermute(own_hi, "gy", [(i, (i + 1) % 4) for i in range(4)])
    above = lax.ppermute(own_lo, "gy", [((i + 1) % 4, i) for i in range(4)])
    flat = struct(BANDS * TILES * 8, 128)
    runs = struct(TILES // 2 * 128, 128)
    x_field, y_field = struct(ROWS, TILES, 128), struct(Y_STEPS, 8, 128)
    x_port = struct(7, TILES, 128)
    e, *x_coefficients, x_lo, x_hi, x_ends, t_flat, k_flat = call(
        x_matrix_kernel,
        [
            flat,
            x_field,
            x_field,
            x_field,
            struct((2 * X_LEVELS + 1) * SEGMENTS, TILES, 128),
            x_field,
            x_field,
            x_port,
            flat,
            flat,
        ],
        name="x_matrix",
    )(t, k)
    *y_coefficients, y_lo, y_hi, y_ends = call(
        y_matrix_kernel,
        [
            y_field,
            y_field,
            y_field,
            struct((2 * Y_LEVELS + 1) * SEGMENTS, 8, 128),
            y_field,
            y_field,
            struct(8, 128),
        ],
        [scratch(runs)],
        name="y_matrix",
    )(k)
    below, above, y_lo = lax.optimization_barrier((below, above, y_lo))
    own, edge = call(
        x_port_kernel,
        [x_port, struct(ROWS, 128)],
        [pltpu.VMEM((128, 128), F32)],
        flops=200_000,
        name="x_port",
    )(x_ends, x_lo, x_hi, own_edges, below, above)
    u = call(x_solve_kernel, x_field, [scratch(flat)], flops=700_000, name="x_solve")(
        e, *x_coefficients, edge
    )
    other = lax.ppermute(own, "gx", [(i, i ^ 1) for i in range(32)])
    other, u = lax.optimization_barrier((other, u))
    own_z = call(pair_kernel, x_port, name="pair")(own, other)
    from_z = [around(own_z, "gx", 32, 2, s) for s in RING]
    flat_lo, flat_hi = call(
        upright_kernel,
        [natural, natural],
        [pltpu.VMEM((2, TILES // 2 * 128, 128), F32)],
        name="upright",
    )(y_lo, y_hi)
    *from_z, flat_lo = lax.optimization_barrier((*from_z, flat_lo))
    table = pltpu.VMEM((4, 7, TILES, 128), F32)
    own_y = call(four_kernel, x_port, [table], name="four")(own_z, *from_z)
    from_y = [around(own_y, "gx", 32, 8, s) for s in RING]
    square = pltpu.VMEM((128, 128), F32)
    source, lo_flat, hi_flat, mixed, known = call(
        blend_kernel,
        [flat, flat, flat, struct(4, BANDS * TILES * 8, 128), struct(8, 128)],
        [scratch(flat), square],
        name="blend",
    )(u, x_lo, x_hi, flat_lo, flat_hi, t_flat)
    port, flow = call(
        y_port_kernel,
        [struct(8, 128), struct(2, TILES, 128)],
        [table, table, square],
        name="y_port",
    )(own_y, *from_y, own_z, *from_z, own, other, mixed, known, y_ends)
    from_gy = [around(port, "gy", 4, 1, s) for s in LAST_RING]
    base = call(
        y_solve_kernel, natural, [scratch(y_field), scratch(runs)], name="y_solve"
    )(source, lo_flat, hi_flat, flow, *y_coefficients, t_flat)
    updated = call(
        finish_kernel,
        natural,
        [
            pltpu.VMEM((4, 8, 128), F32),
            pltpu.VMEM((128, 128), F32),
            scratch(natural),
            pltpu.SemaphoreType.DMA((BANDS // 2,)),
        ],
        name="finish",
        in_specs=[VMEM] * 7,
        out_specs=HBM,
    )(port, *from_gy, base, flat_lo, flat_hi)
    return updated[None]


def solution(mesh):
    placed = (P(None, "gx", "gy"), P(None, "gx", "gy"))
    return jax.shard_map(
        per_device, mesh=mesh, in_specs=placed, out_specs=P(None, "gx", "gy"), check_vma=False
    )
```
